32 devices in a mesh: dp: 8 (over y, x, core), mp: 4 (over z).
Axes of the slice: x: 2, y: 2, z: 4, core: 2. Of those that a mesh axis runs over, the one named last changes fastest.
Arguments:
- tokens: bfloat16 [16, 512, 768], P('dp'), may hold values from -6 to 6
- lengths: int32 [16], P('dp'), may hold values from 40 to 512, as said below
- coords: int32 [16, 2, 512], P('dp'), may hold values from 0 to 999
- w_qkv: bfloat16 [3, 768, 768], P(None, None, 'mp'), may hold values from -0.375 to 0.375
- w_pos: bfloat16 [2, 768, 768], P(None, None, 'mp'), may hold values from -0.375 to 0.375
- w_out: bfloat16 [768, 768], P('mp'), may hold values from -0.875 to 0.875
- b_out: float32 [768], replicated, may hold values from -3 to 3
- gain_one: float32 [768], replicated, may hold values from 0.5 to 1.5
- shift_one: float32 [768], replicated, may hold values from -3 to 3
- w_in: bfloat16 [768, 3072], P(None, 'mp'), may hold values from -0.21875 to 0.21875
- b_in: float32 [3072], P('mp'), may hold values from -3 to 3
- w_back: bfloat16 [3072, 768], P('mp'), may hold values from -0.109375 to 0.109375
- b_back: float32 [768], replicated, may hold values from -3 to 3
- gain_two: float32 [768], replicated, may hold values from 0.5 to 1.5
- shift_two: float32 [768], replicated, may hold values from -3 to 3
- cotangent: bfloat16 [16, 512, 768], P('dp'), may hold values from -6 to 6
Outputs:
- layer_out: bfloat16 [16, 512, 768], P('dp')
- grad_tokens: float32 [16, 512, 768], P('dp')
- grad_w_qkv: float32 [3, 768, 768], P(None, None, 'mp')
- grad_w_pos: float32 [2, 768, 768], P(None, None, 'mp')
- grad_w_out: float32 [768, 768], P('mp')
- grad_b_out: float32 [768], replicated
- grad_gain_one: float32 [768], replicated
- grad_shift_one: float32 [768], replicated
- grad_w_in: float32 [768, 3072], P(None, 'mp')
- grad_b_in: float32 [3072], P('mp')
- grad_w_back: float32 [3072, 768], P('mp')
- grad_b_back: float32 [768], replicated
- grad_gain_two: float32 [768], replicated
- grad_shift_two: float32 [768], replicated
The draws below stay inside these ranges and needn't reach their ends.
Inputs may be any that keep to these rules, and one draw needn't show every extreme that they name: `lengths`: in every draw some page has all 512 tokens real.
All inputs are finite; a program needn't handle non-finite values.
Results may differ from the reference program's by a relative error of at most 0.015.
Values sent between devices are 32-bit elements; how exact they have to be, the bound alone decides.
No kernel may reach another device: no remote copies, remote signals or barrier semaphores. Data moves between devices by JAX's collectives and lax.ppermute only.
A program may use at most 128 MiB of HBM per device.

```python
import math
import jax
import jax.numpy as jnp
from jax import lax

D = 768
HEADS = 12
HEAD_DIM = 64
FF = 3072
LEN = 512
MIN_LEN = 40
QGRID = 1000
PAGES = 16


def draw_lengths(key, part):
    first_key, second_key = jax.random.split(jax.random.fold_in(key, 7))
    drawn = jax.random.randint(first_key, (PAGES,), MIN_LEN, LEN + 1)
    chosen = jax.random.randint(second_key, (), 0, PAGES)
    return jnp.where(jnp.arange(PAGES) == chosen, LEN, drawn).astype(jnp.int32)


def with_ends(array, rng, smallest, largest):
    spot = [jax.random.randint(jax.random.fold_in(rng, axis), (), 0, length) for axis, length in enumerate(array.shape)]
    main_axis = array.shape.index(max(array.shape))
    neighbour = spot[:main_axis] + [(spot[main_axis] + 1) % array.shape[main_axis]] + spot[main_axis + 1:]
    return array.at[tuple(spot)].set(smallest).at[tuple(neighbour)].set(largest)


def steps_of(key, dims, pieces, smallest, top_value):
    gain = 1.0
    for dim, blocks in pieces:
        draws = jax.random.uniform(jax.random.fold_in(jax.random.fold_in(key, 6), dim), (blocks,), jnp.float32, smallest / len(pieces), top_value / len(pieces))
        gain = gain * jnp.repeat(jnp.exp(draws), dims[dim] // blocks).reshape((-1,) + (1,) * (len(dims) - 1 - dim))
    return gain


def centred(key, dims, width, reach, shards=(), kind=jnp.bfloat16):
    values = width * jax.random.normal(key, dims, jnp.float32)
    if shards:
        values = values * steps_of(key, dims, shards, -0.22, 0.18)
    return jnp.clip(values, -reach, reach).astype(kind)


def setup_inputs(seed: int = 0) -> dict:
    streams_of = jax.random.split(jax.random.key(seed), 17)
    return {
        "tokens": centred(streams_of[0], (PAGES, LEN, D), 1.0, 6.0, ((0, 8),)),
        "lengths": draw_lengths(jax.random.fold_in(streams_of[16], 71), 0),
        "coords": with_ends(jax.random.randint(streams_of[2], (PAGES, 2, LEN), 0, QGRID), jax.random.fold_in(streams_of[2], 1), 0, QGRID - 1).astype(jnp.int32),
        "w_qkv": centred(streams_of[3], (3, D, D), (D // 3) ** -0.5, 0.375, ((2, 4),)),
        "w_pos": centred(streams_of[4], (2, D, D), (D // 3) ** -0.5, 0.375, ((2, 4),)),
        "w_out": centred(streams_of[5], (D, D), (D // 16) ** -0.5, 0.875, ((0, 4),)),
        "b_out": centred(streams_of[6], (D,), 0.5, 3.0, (), jnp.float32),
        "gain_one": jnp.clip(1.0 + 0.1 * jax.random.normal(streams_of[7], (D,), jnp.float32), 0.5, 1.5),
        "shift_one": centred(streams_of[8], (D,), 0.5, 3.0, (), jnp.float32),
        "w_in": centred(streams_of[9], (D, FF), D ** -0.5, 0.21875, ((1, 4),)),
        "b_in": centred(streams_of[10], (FF,), 0.5, 3.0, ((0, 4),), jnp.float32),
        "w_back": centred(streams_of[11], (FF, D), FF ** -0.5, 0.109375, ((0, 4),)),
        "b_back": centred(streams_of[12], (D,), 0.5, 3.0, (), jnp.float32),
        "gain_two": jnp.clip(1.0 + 0.1 * jax.random.normal(streams_of[13], (D,), jnp.float32), 0.5, 1.5),
        "shift_two": centred(streams_of[14], (D,), 0.5, 3.0, (), jnp.float32),
        "cotangent": centred(streams_of[15], (PAGES, LEN, D), 1.0, 6.0, ((0, 8),)),
    }


@jax.custom_vjp
def low(v):
    return lax.optimization_barrier(v.astype(jnp.bfloat16)).astype(jnp.float32)

@jax.custom_vjp
def low_back(v):
    return v

def low_keep(v):
    return (low(v), None)

def low_pass(kept, grad):
    return (grad,)

def back_keep(v):
    return (v, None)

def back_low(kept, grad):
    return (low(grad),)
low.defvjp(low_keep, low_pass)
low_back.defvjp(back_keep, back_low)

def round_both(values):
    return low(low_back(values))

def matmul_high(left, right):
    return jnp.dot(left, right, precision=lax.Precision.HIGHEST)

def sinusoid(coords):
    quarter = D // 4
    frequency = jnp.exp(jnp.arange(quarter, dtype=jnp.float32) * (-math.log(10000.0) / quarter))
    position = coords.astype(jnp.float32)
    phases = position[:, :, None] * frequency
    sin_cos = jnp.concatenate([jnp.sin(phases), jnp.cos(phases)], axis=2)
    return jnp.concatenate([sin_cos[0], sin_cos[1]], axis=1)

def layer_norm(values, norm_gain, norm_shift):
    center = values - lax.optimization_barrier(jnp.mean(values, axis=-1, keepdims=True))
    spread = lax.optimization_barrier(jnp.mean(center * center, axis=-1, keepdims=True))
    return center * lax.rsqrt(spread + 1e-05) * norm_gain + norm_shift

def attend(inputs):
    queries, key_rows, value_rows, pos_query, pos_key, page_length = inputs
    factor = 1.0 / math.sqrt(3.0 * HEAD_DIM)
    highest = lax.Precision.HIGHEST
    scores = jnp.einsum('ihd,jhd->hij', queries, key_rows, precision=highest)
    scores = scores + jnp.einsum('ihd,jhd->hij', queries, pos_key, precision=highest)
    scores = scores + jnp.einsum('ihd,jhd->hij', pos_query, key_rows, precision=highest)
    scores = scores * factor
    visible = jnp.arange(LEN) < page_length
    scores = low_back(jnp.where(visible[None, None, :], scores, -1e+30))
    weights = low(jax.nn.softmax(scores, axis=2))
    return jnp.einsum('hij,jhd->ihd', weights, value_rows, precision=highest)

def forward(token_rows, w_qkv, w_pos, w_out, b_out, gain_one, shift_one, w_in, b_in, w_back, b_back, gain_two, shift_two, position, lengths):
    shaped = (PAGES, LEN, HEADS, HEAD_DIM)
    queries = round_both(matmul_high(token_rows, w_qkv[0])).reshape(shaped)
    key_rows = round_both(matmul_high(token_rows, w_qkv[1])).reshape(shaped)
    value_rows = round_both(matmul_high(token_rows, w_qkv[2])).reshape(shaped)
    pos_query = round_both(matmul_high(position, w_pos[0])).reshape(shaped)
    pos_key = round_both(matmul_high(position, w_pos[1])).reshape(shaped)
    mixed = lax.map(jax.checkpoint(attend), (queries, key_rows, value_rows, pos_query, pos_key, lengths))
    mixed = round_both(mixed.reshape(PAGES * LEN, D))
    branch = low_back(matmul_high(mixed, w_out) + b_out)
    first = token_rows + branch
    normed = layer_norm(first, gain_one, shift_one)
    hidden_pre = low_back(matmul_high(low(normed), w_in) + b_in)
    hidden = low(jax.nn.gelu(hidden_pre, approximate=False))
    feed = low_back(matmul_high(hidden, w_back) + b_back)
    second = normed + feed
    return low(layer_norm(second, gain_two, shift_two))

def reference(tokens, lengths, coords, w_qkv, w_pos, w_out, b_out, gain_one, shift_one, w_in, b_in, w_back, b_back, gain_two, shift_two, cotangent):
    position = low(jax.vmap(sinusoid)(coords).reshape(PAGES * LEN, D))
    token_rows = tokens.astype(jnp.float32).reshape(PAGES * LEN, D)
    primals = (token_rows, w_qkv.astype(jnp.float32), w_pos.astype(jnp.float32), w_out.astype(jnp.float32), b_out, gain_one, shift_one, w_in.astype(jnp.float32), b_in, w_back.astype(jnp.float32), b_back, gain_two, shift_two)

    def layer(*params):
        return forward(*params, position, lengths)
    output, pull = jax.vjp(layer, *primals)
    grads = pull(cotangent.astype(jnp.float32).reshape(PAGES * LEN, D))
    return (output.astype(jnp.bfloat16).reshape(PAGES, LEN, D), grads[0].reshape(PAGES, LEN, D), grads[1], grads[2], grads[3], grads[4], grads[5], grads[6], grads[7], grads[8], grads[9], grads[10], grads[11], grads[12])
```

```python
from functools import partial
import math

import jax
import jax.numpy as jnp
from jax import lax
from jax.sharding import PartitionSpec as P

HEAD_DIM = 64


def sinusoid(coords, model_width):
    quarter = model_width // 4
    frequency = jnp.exp(jnp.arange(quarter, dtype=jnp.float32) * (-math.log(10000.0) / quarter))
    position = coords.astype(jnp.float32)
    phases = position[:, :, None] * frequency
    sin_cos = jnp.concatenate([jnp.sin(phases), jnp.cos(phases)], axis=2)
    return jnp.concatenate([sin_cos[0], sin_cos[1]], axis=1)


def layer_norm(values, norm_gain, norm_shift):
    center = values - jnp.mean(values, axis=-1, keepdims=True)
    spread = jnp.mean(center * center, axis=-1, keepdims=True)
    return center * lax.rsqrt(spread + 1e-05) * norm_gain + norm_shift


def exact_gelu(values):
    return jax.nn.gelu(values, approximate=False)


def page_scores(queries, key_rows, pos_query, pos_key, page_length):
    factor = 1.0 / math.sqrt(3.0 * queries.shape[2])
    scores = jnp.einsum("ihd,jhd->hij", queries, key_rows, preferred_element_type=jnp.float32)
    scores = scores + jnp.einsum(
        "ihd,jhd->hij", queries, pos_key, preferred_element_type=jnp.float32
    )
    scores = scores + jnp.einsum(
        "ihd,jhd->hij", pos_query, key_rows, preferred_element_type=jnp.float32
    )
    scores = scores * factor
    visible = jnp.arange(queries.shape[0]) < page_length
    return jnp.where(visible[None, None, :], scores, -1e30)


def attend_page(inputs):
    queries, key_rows, value_rows, pos_query, pos_key, page_length = inputs
    scores = page_scores(queries, key_rows, pos_query, pos_key, page_length)
    highest = jnp.max(scores, axis=2, keepdims=True)
    totals = jnp.sum(jnp.exp(scores - highest), axis=2, keepdims=True)
    log_total = highest + jnp.log(totals)
    weights = jnp.exp(scores - log_total).astype(jnp.bfloat16)
    mixed = jnp.einsum("hij,jhd->ihd", weights, value_rows, preferred_element_type=jnp.float32)
    return (mixed.astype(jnp.bfloat16), log_total)


def page_backward(inputs):
    queries, key_rows, value_rows, pos_query, pos_key, page_length, log_total, d_mixed = inputs
    factor = 1.0 / math.sqrt(3.0 * queries.shape[2])
    scores = page_scores(queries, key_rows, pos_query, pos_key, page_length)
    probs = jnp.exp(scores - log_total)
    weights = probs.astype(jnp.bfloat16)
    d_values = jnp.einsum("hij,ihd->jhd", weights, d_mixed, preferred_element_type=jnp.float32)
    d_probs = jnp.einsum("ihd,jhd->hij", d_mixed, value_rows, preferred_element_type=jnp.float32)
    d_scores = (probs * (d_probs - jnp.sum(d_probs * probs, axis=2, keepdims=True))).astype(
        jnp.bfloat16
    )
    by_key = jnp.einsum("hij,jhd->ihd", d_scores, key_rows, preferred_element_type=jnp.float32)
    by_pos_key = jnp.einsum("hij,jhd->ihd", d_scores, pos_key, preferred_element_type=jnp.float32)
    by_query = jnp.einsum("hij,ihd->jhd", d_scores, queries, preferred_element_type=jnp.float32)
    by_pos_query = jnp.einsum(
        "hij,ihd->jhd", d_scores, pos_query, preferred_element_type=jnp.float32
    )
    d_queries = ((by_key + by_pos_key) * factor).astype(jnp.bfloat16)
    d_pos_query = (by_key * factor).astype(jnp.bfloat16)
    d_keys = ((by_query + by_pos_query) * factor).astype(jnp.bfloat16)
    d_pos_key = (by_query * factor).astype(jnp.bfloat16)
    return (d_queries, d_keys, d_values.astype(jnp.bfloat16), d_pos_query, d_pos_key)


def forward(
    token_rows,
    position,
    lengths,
    w_qkv,
    w_pos,
    w_out,
    b_out,
    gain_one,
    shift_one,
    w_in,
    b_in,
    w_back,
    b_back,
    gain_two,
    shift_two,
):
    page_count = lengths.shape[0]
    page_len = token_rows.shape[0] // page_count
    heads_here = w_qkv.shape[2] // HEAD_DIM

    def split_heads(values):
        return values.astype(jnp.bfloat16).reshape(page_count, page_len, heads_here, HEAD_DIM)

    queries = split_heads(jnp.dot(token_rows, w_qkv[0], preferred_element_type=jnp.float32))
    key_rows = split_heads(jnp.dot(token_rows, w_qkv[1], preferred_element_type=jnp.float32))
    value_rows = split_heads(jnp.dot(token_rows, w_qkv[2], preferred_element_type=jnp.float32))
    pos_query = split_heads(jnp.dot(position, w_pos[0], preferred_element_type=jnp.float32))
    pos_key = split_heads(jnp.dot(position, w_pos[1], preferred_element_type=jnp.float32))
    mixed, log_total = lax.map(
        attend_page, (queries, key_rows, value_rows, pos_query, pos_key, lengths)
    )
    mixed = mixed.reshape(page_count * page_len, heads_here * HEAD_DIM)
    branch = lax.psum(jnp.dot(mixed, w_out, preferred_element_type=jnp.float32), "mp") + b_out
    first = token_rows.astype(jnp.float32) + branch
    normed = layer_norm(first, gain_one, shift_one)
    normed_low = normed.astype(jnp.bfloat16)
    hidden_pre = jnp.dot(normed_low, w_in, preferred_element_type=jnp.float32) + b_in
    hidden = exact_gelu(hidden_pre).astype(jnp.bfloat16)
    feed = lax.psum(jnp.dot(hidden, w_back, preferred_element_type=jnp.float32), "mp") + b_back
    second = normed + feed
    output = layer_norm(second, gain_two, shift_two)
    saved = (
        queries,
        key_rows,
        value_rows,
        pos_query,
        pos_key,
        mixed,
        log_total,
        first,
        normed,
        normed_low,
        hidden_pre,
        hidden,
        second,
    )
    return (output, saved)


def body(
    tokens,
    lengths,
    coords,
    w_qkv,
    w_pos,
    w_out,
    b_out,
    gain_one,
    shift_one,
    w_in,
    b_in,
    w_back,
    b_back,
    gain_two,
    shift_two,
    cotangent,
):
    page_count, page_len, model_width = tokens.shape
    token_rows = tokens.reshape(page_count * page_len, model_width)
    position = jax.vmap(partial(sinusoid, model_width=model_width))(coords)
    position = position.astype(jnp.bfloat16).reshape(page_count * page_len, model_width)
    weights_all = (
        w_qkv,
        w_pos,
        w_out,
        b_out,
        gain_one,
        shift_one,
        w_in,
        b_in,
        w_back,
        b_back,
        gain_two,
        shift_two,
    )
    output, saved = forward(token_rows, position, lengths, *weights_all)
    (
        queries,
        key_rows,
        value_rows,
        pos_query,
        pos_key,
        mixed,
        log_total,
        first,
        normed,
        normed_low,
        hidden_pre,
        hidden,
        second,
    ) = saved
    heads_here = w_qkv.shape[2] // HEAD_DIM
    d_output = cotangent.reshape(page_count * page_len, model_width).astype(jnp.float32)
    unused_two, pull_two = jax.vjp(layer_norm, second, gain_two, shift_two)
    d_second, d_gain_two, d_shift_two = pull_two(d_output)
    d_feed = d_second.astype(jnp.bfloat16)
    d_b_back = jnp.sum(d_feed.astype(jnp.float32), axis=0)
    d_w_back = jnp.dot(hidden.T, d_feed, preferred_element_type=jnp.float32)
    d_hidden = jnp.dot(d_feed, w_back.T, preferred_element_type=jnp.float32)
    unused_gelu, pull_gelu = jax.vjp(exact_gelu, hidden_pre)
    d_pre = pull_gelu(d_hidden)[0].astype(jnp.bfloat16)
    d_b_in = jnp.sum(d_pre.astype(jnp.float32), axis=0)
    d_w_in = jnp.dot(normed_low.T, d_pre, preferred_element_type=jnp.float32)
    ffn_terms = (d_w_in, d_b_in, d_w_back, d_b_back, d_gain_two, d_shift_two)
    d_normed = d_second + lax.psum(jnp.dot(d_pre, w_in.T, preferred_element_type=jnp.float32), "mp")
    unused_one, pull_one = jax.vjp(layer_norm, first, gain_one, shift_one)
    d_first, d_gain_one, d_shift_one = pull_one(d_normed)
    d_branch = d_first.astype(jnp.bfloat16)
    d_b_out = jnp.sum(d_branch.astype(jnp.float32), axis=0)
    d_w_out = jnp.dot(mixed.T, d_branch, preferred_element_type=jnp.float32)
    d_mixed = jnp.dot(d_branch, w_out.T, preferred_element_type=jnp.float32).astype(jnp.bfloat16)
    d_mixed = d_mixed.reshape(page_count, page_len, heads_here, HEAD_DIM)
    head_grads = lax.map(
        page_backward,
        (queries, key_rows, value_rows, pos_query, pos_key, lengths, log_total, d_mixed),
    )
    flat_grads = [
        piece.reshape(page_count * page_len, heads_here * HEAD_DIM) for piece in head_grads
    ]
    d_queries, d_keys, d_values, d_pos_query, d_pos_key = flat_grads
    d_w_qkv = jnp.stack(
        [
            jnp.dot(token_rows.T, d_queries, preferred_element_type=jnp.float32),
            jnp.dot(token_rows.T, d_keys, preferred_element_type=jnp.float32),
            jnp.dot(token_rows.T, d_values, preferred_element_type=jnp.float32),
        ]
    )
    d_w_pos = jnp.stack(
        [
            jnp.dot(position.T, d_pos_query, preferred_element_type=jnp.float32),
            jnp.dot(position.T, d_pos_key, preferred_element_type=jnp.float32),
        ]
    )
    input_part = jnp.dot(d_queries, w_qkv[0].T, preferred_element_type=jnp.float32)
    input_part = input_part + jnp.dot(d_keys, w_qkv[1].T, preferred_element_type=jnp.float32)
    input_part = input_part + jnp.dot(d_values, w_qkv[2].T, preferred_element_type=jnp.float32)
    d_tokens = d_first + lax.psum(input_part, "mp")
    summed = lax.psum(
        (
            d_w_qkv,
            d_w_pos,
            d_w_out,
            d_b_out,
            d_gain_one,
            d_shift_one,
            d_w_in,
            d_b_in,
            d_w_back,
            d_b_back,
            d_gain_two,
            d_shift_two,
        ),
        "dp",
    )
    attn_terms = summed[:6]
    ffn_terms = summed[6:]
    sum_w_qkv, sum_w_pos, sum_w_out, sum_b_out, sum_gain_one, sum_shift_one = attn_terms
    sum_w_in, sum_b_in, sum_w_back, sum_b_back, sum_gain_two, sum_shift_two = ffn_terms
    layer_out = output.astype(jnp.bfloat16).reshape(page_count, page_len, model_width)
    grad_tokens = d_tokens.reshape(page_count, page_len, model_width)
    return (
        layer_out,
        grad_tokens,
        sum_w_qkv,
        sum_w_pos,
        sum_w_out,
        sum_b_out,
        sum_gain_one,
        sum_shift_one,
        sum_w_in,
        sum_b_in,
        sum_w_back,
        sum_b_back,
        sum_gain_two,
        sum_shift_two,
    )


def solution(mesh):
    placed = (
        P("dp", None, None),
        P("dp"),
        P("dp", None, None),
        P(None, None, "mp"),
        P(None, None, "mp"),
        P("mp", None),
        P(),
        P(),
        P(),
        P(None, "mp"),
        P("mp"),
        P("mp", None),
        P(),
        P(),
        P(),
        P("dp", None, None),
    )
    return jax.shard_map(
        body,
        mesh=mesh,
        in_specs=placed,
        out_specs=(
            P("dp", None, None),
            P("dp", None, None),
            P(None, None, "mp"),
            P(None, None, "mp"),
            P("mp", None),
            P(),
            P(),
            P(),
            P(None, "mp"),
            P("mp"),
            P("mp", None),
            P(),
            P(),
            P(),
        ),
        check_vma=False,
    )
```

```python
from functools import partial
import math

import jax
import jax.numpy as jnp
import numpy as np
from jax import lax
from jax.experimental import pallas as pl
from jax.experimental.pallas import tpu as pltpu
from jax.sharding import PartitionSpec as P

HEAD_DIM = 64
STEP = 32
NEAR = 1
FAR = 2
MASKED = -1e30


def mm(left, right):
    return jnp.dot(left, right, preferred_element_type=jnp.float32)


def mm_nt(left, right):
    return lax.dot_general(
        left, right, (((1,), (1,)), ((), ())), preferred_element_type=jnp.float32
    )


def mm_tn(left, right):
    return lax.dot_general(
        left, right, (((0,), (0,)), ((), ())), preferred_element_type=jnp.float32
    )


def angle_tables(model_width):
    quarter = model_width // 4
    rate = np.exp(np.arange(quarter) * (-math.log(10000.0) / quarter))
    fine = np.arange(STEP)[:, None] * rate
    coarse = fine * STEP
    zero = np.zeros((STEP, 2 * quarter))
    table = np.concatenate(
        [
            np.concatenate([np.sin(coarse), np.cos(coarse), zero], axis=1),
            np.concatenate([zero, np.sin(fine), np.cos(fine)], axis=1),
        ],
        axis=0,
    )
    parts = []
    rest = table
    for _ in range(3):
        part = rest.astype(jnp.bfloat16)
        parts.append(part)
        rest = rest - part.astype(np.float64)
    return np.concatenate(parts, axis=0)


def sinusoid(coords, model_width):
    quarter = model_width // 4
    table = jnp.asarray(angle_tables(model_width))
    slot = lax.broadcasted_iota(jnp.int32, (coords.shape[0], 2 * STEP), 1)
    hit = (slot == (coords // STEP)[:, None]) | (slot == (coords % STEP)[:, None] + STEP)
    hit = hit.astype(jnp.bfloat16)
    looked = mm(jnp.concatenate([hit, hit, hit], axis=1), table)
    sin_a, cos_a, sin_b, cos_b = [looked[:, k * quarter : (k + 1) * quarter] for k in range(4)]
    return jnp.concatenate([sin_a * cos_b + cos_a * sin_b, cos_a * cos_b - sin_a * sin_b], axis=1)


def head_of(ref, index, head):
    return ref[index, :, head * HEAD_DIM : (head + 1) * HEAD_DIM]


def probs_t(q, k, pq, pk, length, factor):
    left = jnp.concatenate([k, pk, k], axis=1)
    right = jnp.concatenate([q, q, pq], axis=1)
    scores = mm_nt(left, right) * factor
    visible = lax.broadcasted_iota(jnp.int32, scores.shape, 0) < length
    scores = jnp.where(visible, scores, MASKED)
    raised = jnp.exp(scores - jnp.max(scores, axis=0, keepdims=True))
    return raised * (1.0 / jnp.sum(raised, axis=0, keepdims=True))


def attend_kernel(heads, lengths_ref, x_ref, pos_ref, wqkv_ref, wpos_ref, mixed_ref, proj_ref):
    length = lengths_ref[pl.program_id(0)]
    factor = 1.0 / math.sqrt(3.0 * HEAD_DIM)
    rows = x_ref[0]
    for part in range(3):
        proj_ref[0, part] = mm(rows, wqkv_ref[part]).astype(jnp.bfloat16)
    position = pos_ref[0]
    for part in range(2):
        proj_ref[0, 3 + part] = mm(position, wpos_ref[part]).astype(jnp.bfloat16)
    here = proj_ref.at[0]
    for head in range(heads):
        q, k, v, pq, pk = [head_of(here, part, head) for part in range(5)]
        weights = probs_t(q, k, pq, pk, length, factor).astype(jnp.bfloat16)
        mixed = mm_tn(v, weights)
        mixed = mixed.astype(jnp.bfloat16).astype(jnp.float32)
        mixed_ref[0, :, head * HEAD_DIM : (head + 1) * HEAD_DIM] = mixed.T


def attend(lengths, tokens, position, w_qkv, w_pos):
    pages, length, width = tokens.shape
    columns = w_qkv.shape[2]
    page = lambda i, lens: (i, 0, 0)
    whole = lambda i, lens: (0, 0, 0)
    return pl.pallas_call(
        partial(attend_kernel, columns // HEAD_DIM),
        out_shape=(
            jax.ShapeDtypeStruct((pages, length, columns), jnp.float32),
            jax.ShapeDtypeStruct((pages, 5, length, columns), jnp.bfloat16),
        ),
        grid_spec=pltpu.PrefetchScalarGridSpec(
            num_scalar_prefetch=1,
            grid=(pages,),
            in_specs=[
                pl.BlockSpec((1, length, width), page),
                pl.BlockSpec((1, length, width), page),
                pl.BlockSpec(w_qkv.shape, whole),
                pl.BlockSpec(w_pos.shape, whole),
            ],
            out_specs=[
                pl.BlockSpec((1, length, columns), page),
                pl.BlockSpec((1, 5, length, columns), lambda i, lens: (i, 0, 0, 0)),
            ],
        ),
        compiler_params=pltpu.CompilerParams(vmem_limit_bytes=40 << 20),
        cost_estimate=pl.CostEstimate(
            flops=2 * pages * length * columns * (5 * width + 4 * length),
            transcendentals=pages * length * length * columns // HEAD_DIM,
            bytes_accessed=pages * length * (4 * width + 14 * columns),
        ),
        name="attend",
    )(lengths, tokens, position, w_qkv, w_pos)


def attend_back_kernel(heads, scalars_ref, own_ref, far_ref, dm_ref, d_ref, dp_ref):
    length = scalars_ref[1]
    factor = 1.0 / math.sqrt(3.0 * HEAD_DIM)
    columns = heads * HEAD_DIM
    for side, here in enumerate((own_ref.at[0], far_ref)):
        for head in range(heads):
            q, k, v, pq, pk = [head_of(here, part, head) for part in range(5)]
            at = side * columns + head * HEAD_DIM
            dm = dm_ref[:, at : at + HEAD_DIM]
            probs = probs_t(q, k, pq, pk, length, factor)
            weights = probs.astype(jnp.bfloat16)
            d_values = mm(weights, dm)
            d_probs = mm_nt(v, dm)
            inner = jnp.sum(d_probs * probs, axis=0, keepdims=True)
            d_scores = (probs * (d_probs - inner)).astype(jnp.bfloat16)
            by_queries = mm(d_scores, jnp.concatenate([q, pq], axis=1))
            by_query, by_pos_query = by_queries[:, :HEAD_DIM], by_queries[:, HEAD_DIM:]
            by_keys = mm_tn(jnp.concatenate([k, pk], axis=1), d_scores).T
            by_key, by_pos_key = by_keys[:, :HEAD_DIM], by_keys[:, HEAD_DIM:]
            grads = (
                ((by_key + by_pos_key) * factor, 0, d_ref, 3),
                ((by_query + by_pos_query) * factor, 1, d_ref, 3),
                (d_values, 2, d_ref, 3),
                (by_key * factor, 0, dp_ref, 2),
                (by_query * factor, 1, dp_ref, 2),
            )
            for value, part, ref, parts in grads:
                to = (side * parts + part) * columns + head * HEAD_DIM
                ref[:, to : to + HEAD_DIM] = value.astype(jnp.bfloat16)


def attend_back(scalars, proj, far_proj, d_mixed):
    pages, parts, length, columns = proj.shape
    heads = columns // HEAD_DIM
    return pl.pallas_call(
        partial(attend_back_kernel, heads),
        out_shape=(
            jax.ShapeDtypeStruct((length, 6 * columns), jnp.bfloat16),
            jax.ShapeDtypeStruct((length, 4 * columns), jnp.bfloat16),
        ),
        grid_spec=pltpu.PrefetchScalarGridSpec(
            num_scalar_prefetch=1,
            grid=(1,),
            in_specs=[
                pl.BlockSpec((1, parts, length, columns), lambda i, s: (s[0], 0, 0, 0)),
                pl.BlockSpec((parts, length, columns), lambda i, s: (0, 0, 0)),
                pl.BlockSpec((length, 2 * columns), lambda i, s: (0, 0)),
            ],
            out_specs=[
                pl.BlockSpec((length, 6 * columns), lambda i, s: (0, 0)),
                pl.BlockSpec((length, 4 * columns), lambda i, s: (0, 0)),
            ],
        ),
        compiler_params=pltpu.CompilerParams(vmem_limit_bytes=40 << 20),
        cost_estimate=pl.CostEstimate(
            flops=2 * 2 * heads * length * length * HEAD_DIM * 9,
            transcendentals=2 * heads * length * length,
            bytes_accessed=length * columns * 44,
        ),
        name="attend_back",
    )(scalars, proj, far_proj, d_mixed)


def norm_parts(values):
    center = values - jnp.mean(values, axis=-1, keepdims=True)
    spread = jnp.mean(center * center, axis=-1, keepdims=True)
    scale = lax.rsqrt(spread + 1e-05)
    return center * scale, scale


def norm_back(grad, gain, xhat, scale):
    up = grad * gain
    mean = jnp.mean(up, axis=-1, keepdims=True)
    along = jnp.mean(up * xhat, axis=-1, keepdims=True)
    return scale * (up - mean - xhat * along)


def column_sum(values):
    return jnp.sum(values.astype(jnp.float32), axis=0)


def body(
    dp_size,
    mp_size,
    tokens,
    lengths,
    coords,
    w_qkv,
    w_pos,
    w_out,
    b_out,
    gain_one,
    shift_one,
    w_in,
    b_in,
    w_back,
    b_back,
    gain_two,
    shift_two,
    cotangent,
):
    pages, length, width = tokens.shape
    columns = w_qkv.shape[2]
    units = w_in.shape[1]
    here = lax.axis_index("mp")
    low = here & 1
    page = here >> 1
    group = lax.axis_index("dp")
    f32, bf16 = jnp.float32, jnp.bfloat16

    one = jnp.where(lengths[0] > 0, 1.0, 0.0).astype(f32)

    def arrived(value):
        return value * one

    def swap(value, bit):
        pairs = [(i, i ^ bit) for i in range(mp_size)]
        return lax.ppermute(value, "mp", pairs)

    def my_rows(value):
        rows = value.shape[0] // dp_size
        return lax.dynamic_slice_in_dim(value, group * rows, rows, 0)

    def gather(value):
        return arrived(lax.all_gather(value, "dp", axis=0, tiled=True))

    def take(value, index):
        return lax.dynamic_index_in_dim(value, index, 0, keepdims=False)

    out_rows = swap(my_rows(w_out).astype(f32), FAR)
    w_out_far = gather(out_rows).astype(bf16)
    unit_rows = jnp.concatenate([my_rows(w_in), my_rows(w_back)], axis=0).astype(f32)
    far_rows = swap(jnp.concatenate([unit_rows, b_in[None], jnp.zeros((7, units), f32)], axis=0), FAR)
    b_in_far = far_rows[unit_rows.shape[0]]
    blocks = gather(far_rows[: unit_rows.shape[0]]).reshape(dp_size, unit_rows.shape[0], -1)
    in_rows = width // dp_size
    w_in_far = blocks[:, :in_rows].reshape(width, units).astype(bf16)
    w_back_far = blocks[:, in_rows:].reshape(units, width).astype(bf16)
    head_rows = jnp.concatenate(
        [my_rows(w_qkv.reshape(-1, columns)), my_rows(w_pos.reshape(-1, columns))], axis=0
    ).astype(f32)
    blocks = gather(swap(head_rows, FAR)).reshape(dp_size, head_rows.shape[0], columns)
    qkv_rows = 3 * width // dp_size
    w_qkv_far = blocks[:, :qkv_rows].reshape(3, width, columns).astype(bf16)
    w_pos_far = blocks[:, qkv_rows:].reshape(2, width, columns).astype(bf16)

    position = [
        sinusoid(coords[:, axis].reshape(-1), width).astype(bf16) for axis in range(2)
    ]
    position = jnp.concatenate(position, axis=1).reshape(pages, length, width)
    mixed_all, proj = attend(lengths, tokens, position, w_qkv, w_pos)

    mixed_far = arrived(swap(take(mixed_all, 1 - page), FAR))
    mixed = jnp.concatenate([take(mixed_all, page), mixed_far], axis=1).astype(bf16)
    w_out_two = jnp.concatenate([w_out, w_out_far], axis=0)
    w_in_two = jnp.concatenate([w_in, w_in_far], axis=1)
    w_back_two = jnp.concatenate([w_back, w_back_far], axis=0)
    b_in_two = jnp.concatenate([b_in, b_in_far], axis=0)
    rows = take(tokens, page)
    pos_rows = take(position, page)
    grad_out = take(cotangent, page).astype(f32)

    part = mm(mixed, w_out_two)
    first = rows.astype(f32) + (part + swap(part, NEAR) + b_out)
    xhat_one, scale_one = norm_parts(first)
    normed = xhat_one * gain_one + shift_one
    normed_low = normed.astype(bf16)
    hidden_pre = mm(normed_low, w_in_two) + b_in_two
    cdf = 0.5 * (1.0 + lax.erf(hidden_pre * math.sqrt(0.5)))
    hidden = (hidden_pre * cdf).astype(bf16)
    part = mm(hidden, w_back_two)
    slope = cdf + hidden_pre * (
        jnp.exp(-0.5 * hidden_pre * hidden_pre) * (1.0 / math.sqrt(2.0 * math.pi))
    )
    second = normed + (part + swap(part, NEAR) + b_back)
    xhat_two, scale_two = norm_parts(second)
    d_second = norm_back(grad_out, gain_two, xhat_two, scale_two)
    d_feed = d_second.astype(bf16)
    d_hidden = mm_nt(d_feed, w_back_two)
    d_pre = (d_hidden * slope).astype(bf16)
    part = mm_nt(d_pre, w_in_two)
    d_normed = d_second + (part + swap(part, NEAR))

    half = length // 2

    def half_of(value, index):
        return lax.dynamic_slice_in_dim(value, index * half, half, 0)

    def spread(mine, other):
        both = jnp.stack([mine, other])
        rest = swap(both, NEAR)
        out = jnp.stack([jnp.where(low == 0, both, rest), jnp.where(low == 0, rest, both)], axis=1)
        out = out.reshape(pages, length, width)
        return jnp.where(page == 0, out, out[::-1])

    output = xhat_two * gain_two + shift_two
    mine = half_of(output, low)
    layer_out = arrived(spread(mine, swap(mine, FAR))).astype(bf16)

    def to_blocks(value):
        return value.reshape(dp_size, -1, value.shape[1])

    def in_first(rows_of):
        value = jnp.stack(rows_of + [jnp.zeros_like(rows_of[0])] * (8 - len(rows_of)))
        return jnp.concatenate(
            [value[None], jnp.zeros((dp_size - 1,) + value.shape, f32)], axis=0
        )

    def reduce_two(own, far):
        both = jnp.concatenate(own + far, axis=1)
        total = lax.psum_scatter(
            both.reshape(-1, both.shape[2]), "dp", scatter_dimension=0, tiled=True
        )
        cut = total.shape[0] // 2
        total = total[:cut] + swap(total[cut:], FAR)
        return lax.all_gather(total, "dp", axis=0, tiled=True).reshape(dp_size, cut, -1)

    d_w_back = mm_tn(hidden, d_feed)
    d_w_in = [mm_tn(normed_low, d_pre[:, :units]), mm_tn(normed_low, d_pre[:, units:])]
    d_b_in = column_sum(d_pre)
    vectors = [
        column_sum(d_feed),
        jnp.sum(grad_out * xhat_two, axis=0),
        jnp.sum(grad_out, axis=0),
    ]
    ffn = reduce_two(
        [to_blocks(d_w_in[0]), to_blocks(d_w_back[:units]), in_first([d_b_in[:units]] + vectors)],
        [to_blocks(d_w_in[1]), to_blocks(d_w_back[units:]), in_first([d_b_in[units:]] + vectors)],
    )
    grad_w_in = ffn[:, :in_rows].reshape(width, units)
    grad_w_back = ffn[:, in_rows : in_rows + units // dp_size].reshape(units, width)
    vectors = ffn[0, in_rows + units // dp_size :]
    grad_b_in, grad_b_back, grad_gain_two, grad_shift_two = vectors[0], vectors[1], vectors[2], vectors[3]

    d_first = norm_back(d_normed, gain_one, xhat_one, scale_one)
    d_branch = d_first.astype(bf16)
    d_mixed = mm_nt(d_branch, w_out_two).astype(bf16)
    far_proj = [mm(rows, w_qkv_far[k]).astype(bf16) for k in range(3)]
    far_proj += [mm(pos_rows, w_pos_far[k]).astype(bf16) for k in range(2)]
    scalars = jnp.stack([page, take(lengths, page)])
    d_heads, d_pos = attend_back(scalars, proj, jnp.stack(far_proj), d_mixed)
    part = mm_nt(d_heads[:, : 3 * columns], jnp.concatenate(list(w_qkv), axis=1))
    part = part + mm_nt(d_heads[:, 3 * columns :], jnp.concatenate(list(w_qkv_far), axis=1))
    mine = half_of(part, low) + swap(half_of(part, 1 - low), NEAR) + half_of(d_first, low)
    grad_tokens = spread(mine, swap(mine, FAR))

    d_w_out = mm_tn(mixed, d_branch)
    vectors = [
        column_sum(d_branch),
        jnp.sum(d_normed * xhat_one, axis=0),
        jnp.sum(d_normed, axis=0),
    ]
    vectors = in_first(vectors)
    grads_x = mm_tn(rows, d_heads)
    grads_p = mm_tn(pos_rows, d_pos)
    attn = reduce_two(
        [to_blocks(d_w_out[:columns]), vectors],
        [to_blocks(d_w_out[columns:]), vectors],
    )
    out_block = columns // dp_size
    grad_w_out = attn[:, :out_block].reshape(columns, width)
    grad_b_out, grad_gain_one, grad_shift_one = [attn[0, out_block + k] for k in range(3)]

    def reduce_columns(value):
        total = lax.psum_scatter(value, "dp", scatter_dimension=0, tiled=True)
        cut = total.shape[1] // 2
        total = total[:, :cut] + swap(total[:, cut:], FAR)
        return lax.all_gather(total, "dp", axis=0, tiled=True)

    grads_x = reduce_columns(grads_x)
    grads_p = reduce_columns(grads_p)
    grad_w_qkv = jnp.stack([grads_x[:, k * columns : (k + 1) * columns] for k in range(3)])
    grad_w_pos = jnp.stack([grads_p[:, k * columns : (k + 1) * columns] for k in range(2)])
    return (
        layer_out,
        grad_tokens,
        grad_w_qkv,
        grad_w_pos,
        grad_w_out,
        grad_b_out,
        grad_gain_one,
        grad_shift_one,
        grad_w_in,
        grad_b_in,
        grad_w_back,
        grad_b_back,
        grad_gain_two,
        grad_shift_two,
    )


def solution(mesh):
    placed = (
        P("dp", None, None),
        P("dp"),
        P("dp", None, None),
        P(None, None, "mp"),
        P(None, None, "mp"),
        P("mp", None),
        P(),
        P(),
        P(),
        P(None, "mp"),
        P("mp"),
        P("mp", None),
        P(),
        P(),
        P(),
        P("dp", None, None),
    )
    return jax.shard_map(
        partial(body, mesh.shape["dp"], mesh.shape["mp"]),
        mesh=mesh,
        in_specs=placed,
        out_specs=(
            P("dp", None, None),
            P("dp", None, None),
            P(None, None, "mp"),
            P(None, None, "mp"),
            P("mp", None),
            P(),
            P(),
            P(),
            P(None, "mp"),
            P("mp"),
            P("mp", None),
            P(),
            P(),
            P(),
        ),
        check_vma=False,
    )
```

```python
from functools import partial
import math

import jax
import jax.numpy as jnp
import numpy as np
from jax import lax
from jax.experimental import pallas as pl
from jax.experimental.pallas import tpu as pltpu
from jax.sharding import PartitionSpec as P

HEAD_DIM = 64
STEP_BITS = 5
STEP = 1 << STEP_BITS
NEAR = 1
FAR = 2
MASKED = -1e30


def mm(left, right):
    return jnp.dot(left, right, preferred_element_type=jnp.float32)


def mm_nt(left, right):
    return lax.dot_general(
        left, right, (((1,), (1,)), ((), ())), preferred_element_type=jnp.float32
    )


def mm_tn(left, right):
    return lax.dot_general(
        left, right, (((0,), (0,)), ((), ())), preferred_element_type=jnp.float32
    )


def angle_tables(model_width):
    quarter = model_width // 4
    rate = np.exp(np.arange(quarter) * (-math.log(10000.0) / quarter))
    fine = np.arange(STEP)[:, None] * rate
    coarse = fine * STEP
    zero = np.zeros((STEP, 2 * quarter))
    table = np.concatenate(
        [
            np.concatenate([np.sin(coarse), np.cos(coarse), zero], axis=1),
            np.concatenate([zero, np.sin(fine), np.cos(fine)], axis=1),
        ],
        axis=0,
    )
    parts = []
    rest = table
    for _ in range(3):
        part = rest.astype(jnp.bfloat16)
        parts.append(part)
        rest = rest - part.astype(np.float64)
    return np.concatenate(parts, axis=0)


def sinusoid(coord, table_ref):
    quarter = table_ref.shape[1] // 4
    slot = lax.broadcasted_iota(jnp.int32, (2 * STEP, coord.shape[1]), 0)
    coarse = coord >> STEP_BITS
    fine = (coord & (STEP - 1)) + STEP
    hit = ((slot == coarse) | (slot == fine)).astype(jnp.float32).astype(jnp.bfloat16)
    looked = mm_tn(jnp.concatenate([hit, hit, hit], axis=0), table_ref[...])
    sin_a, cos_a, sin_b, cos_b = [looked[:, k * quarter : (k + 1) * quarter] for k in range(4)]
    return jnp.concatenate([sin_a * cos_b + cos_a * sin_b, cos_a * cos_b - sin_a * sin_b], axis=1)


def head_of(ref, index, head):
    return ref[index, :, head * HEAD_DIM : (head + 1) * HEAD_DIM]


def probs_t(q, k, pq, pk, length, factor):
    left = jnp.concatenate([k, pk, k], axis=1)
    right = jnp.concatenate([q, q, pq], axis=1)
    scores = mm_nt(left, right) * factor
    visible = lax.broadcasted_iota(jnp.int32, scores.shape, 0) < length
    scores = jnp.where(visible, scores, MASKED)
    raised = jnp.exp(scores - jnp.max(scores, axis=0, keepdims=True))
    return raised * (1.0 / jnp.sum(raised, axis=0, keepdims=True))


def attend_kernel(
    heads, lengths_ref, x_ref, coords_ref, table_ref, wqkv_ref, wpos_ref, mixed_ref, proj_ref, pos_ref
):
    length = lengths_ref[pl.program_id(0)]
    factor = 1.0 / math.sqrt(3.0 * HEAD_DIM)
    rows = x_ref[0]
    for part in range(3):
        proj_ref[0, part] = mm(rows, wqkv_ref[part]).astype(jnp.bfloat16)
    sides = [sinusoid(coords_ref[0, axis : axis + 1], table_ref) for axis in range(2)]
    position = jnp.concatenate(sides, axis=1).astype(jnp.bfloat16)
    pos_ref[0] = position
    for part in range(2):
        proj_ref[0, 3 + part] = mm(position, wpos_ref[part]).astype(jnp.bfloat16)
    here = proj_ref.at[0]
    for head in range(heads):
        q, k, v, pq, pk = [head_of(here, part, head) for part in range(5)]
        weights = probs_t(q, k, pq, pk, length, factor).astype(jnp.bfloat16)
        mixed = mm_tn(v, weights)
        mixed = mixed.astype(jnp.bfloat16).astype(jnp.float32)
        mixed_ref[0, :, head * HEAD_DIM : (head + 1) * HEAD_DIM] = mixed.T


def attend(lengths, tokens, coords, table, w_qkv, w_pos):
    pages, length, width = tokens.shape
    columns = w_qkv.shape[2]
    page = lambda i, lens: (i, 0, 0)
    whole = lambda i, lens: (0, 0, 0)
    return pl.pallas_call(
        partial(attend_kernel, columns // HEAD_DIM),
        out_shape=(
            jax.ShapeDtypeStruct((pages, length, columns), jnp.float32),
            jax.ShapeDtypeStruct((pages, 5, length, columns), jnp.bfloat16),
            jax.ShapeDtypeStruct((pages, length, width), jnp.bfloat16),
        ),
        grid_spec=pltpu.PrefetchScalarGridSpec(
            num_scalar_prefetch=1,
            grid=(pages,),
            in_specs=[
                pl.BlockSpec((1, length, width), page),
                pl.BlockSpec((1,) + coords.shape[1:], page),
                pl.BlockSpec(table.shape, lambda i, lens: (0, 0)),
                pl.BlockSpec(w_qkv.shape, whole),
                pl.BlockSpec(w_pos.shape, whole),
            ],
            out_specs=[
                pl.BlockSpec((1, length, columns), page),
                pl.BlockSpec((1, 5, length, columns), lambda i, lens: (i, 0, 0, 0)),
                pl.BlockSpec((1, length, width), page),
            ],
        ),
        compiler_params=pltpu.CompilerParams(vmem_limit_bytes=48 << 20),
        cost_estimate=pl.CostEstimate(
            flops=2 * pages * length * columns * (5 * width + 4 * length),
            transcendentals=pages * length * length * columns // HEAD_DIM,
            bytes_accessed=pages * length * (4 * width + 14 * columns),
        ),
        name="attend",
    )(lengths, tokens, coords, table, w_qkv, w_pos)


def attend_back_kernel(heads, scalars_ref, own_ref, far_ref, dm_ref, d_ref):
    length = scalars_ref[1]
    factor = 1.0 / math.sqrt(3.0 * HEAD_DIM)
    columns = heads * HEAD_DIM
    for side, here in enumerate((own_ref.at[0], far_ref)):
        for head in range(heads):
            q, k, v, pq, pk = [head_of(here, part, head) for part in range(5)]
            at = side * columns + head * HEAD_DIM
            dm = dm_ref[:, at : at + HEAD_DIM]
            probs = probs_t(q, k, pq, pk, length, factor)
            weights = probs.astype(jnp.bfloat16)
            d_values = mm(weights, dm)
            d_probs = mm_nt(v, dm)
            inner = jnp.sum(d_probs * probs, axis=0, keepdims=True)
            d_scores = (probs * (d_probs - inner)).astype(jnp.bfloat16)
            by_queries = mm(d_scores, jnp.concatenate([q, pq], axis=1))
            by_query, by_pos_query = by_queries[:, :HEAD_DIM], by_queries[:, HEAD_DIM:]
            by_keys = mm_tn(jnp.concatenate([k, pk], axis=1), d_scores).T
            by_key, by_pos_key = by_keys[:, :HEAD_DIM], by_keys[:, HEAD_DIM:]
            grads = (
                (by_key + by_pos_key) * factor,
                (by_query + by_pos_query) * factor,
                d_values,
                by_key * factor,
                by_query * factor,
            )
            for part, value in enumerate(grads):
                d_ref[part, :, at : at + HEAD_DIM] = value.astype(jnp.bfloat16)


def attend_back(scalars, proj, far_proj, d_mixed):
    pages, parts, length, columns = proj.shape
    heads = columns // HEAD_DIM
    return pl.pallas_call(
        partial(attend_back_kernel, heads),
        out_shape=jax.ShapeDtypeStruct((parts, length, 2 * columns), jnp.bfloat16),
        grid_spec=pltpu.PrefetchScalarGridSpec(
            num_scalar_prefetch=1,
            grid=(1,),
            in_specs=[
                pl.BlockSpec((1, parts, length, columns), lambda i, s: (s[0], 0, 0, 0)),
                pl.BlockSpec((parts, length, columns), lambda i, s: (0, 0, 0)),
                pl.BlockSpec((length, 2 * columns), lambda i, s: (0, 0)),
            ],
            out_specs=pl.BlockSpec((parts, length, 2 * columns), lambda i, s: (0, 0, 0)),
        ),
        compiler_params=pltpu.CompilerParams(vmem_limit_bytes=40 << 20),
        cost_estimate=pl.CostEstimate(
            flops=2 * 2 * heads * length * length * HEAD_DIM * 9,
            transcendentals=2 * heads * length * length,
            bytes_accessed=length * columns * 44,
        ),
        name="attend_back",
    )(scalars, proj, far_proj, d_mixed)


def weight_grads_kernel(count, scalars_ref, x_ref, pos_ref, d_ref, db_ref, mixed_ref, vec_ref, out_ref):
    group = scalars_ref[0]
    rows = x_ref.shape[1] // count
    pairs = [(x_ref, d_ref.at[k]) for k in range(3)]
    pairs += [(pos_ref, d_ref.at[k]) for k in range(3, 5)]
    pairs += [(db_ref, mixed_ref)]
    for part, (left, right) in enumerate(pairs):
        product = mm_tn(left[...], right[...])
        for block in range(count):
            out_ref[block ^ group, part * rows : (part + 1) * rows] = product[
                block * rows : (block + 1) * rows
            ]
    for block in range(count):
        out_ref[block ^ group, len(pairs) * rows :] = (
            vec_ref[...] if block == 0 else jnp.zeros_like(vec_ref)
        )


def weight_grads(count, scalars, rows, pos_rows, d_heads, d_branch, mixed, vectors):
    length, width = rows.shape
    wide = d_heads.shape[2]
    block = 6 * (width // count) + vectors.shape[0]
    return pl.pallas_call(
        partial(weight_grads_kernel, count),
        out_shape=jax.ShapeDtypeStruct((count, block, wide), jnp.float32),
        in_specs=[pl.BlockSpec(memory_space=pltpu.SMEM)] + [pl.BlockSpec(memory_space=pltpu.VMEM)] * 6,
        out_specs=pl.BlockSpec(memory_space=pltpu.VMEM),
        compiler_params=pltpu.CompilerParams(vmem_limit_bytes=48 << 20),
        cost_estimate=pl.CostEstimate(
            flops=12 * length * width * wide,
            transcendentals=0,
            bytes_accessed=4 * count * block * wide + 10 * length * wide + 6 * length * width,
        ),
        name="weight_grads",
    )(scalars, rows, pos_rows, d_heads, d_branch, mixed, vectors)


def place_grads_kernel(scalars_ref, low_ref, high_ref, qkv_ref, pos_ref, out_ref, vec_ref, turned):
    group = scalars_ref[0]
    half = low_ref.shape[0]
    count = 2 * half
    rows = qkv_ref.shape[1] // count
    for block in range(count):
        place = block ^ group
        index = place >> 1
        upper = (place & 1) == 1
        at = slice(block * rows, (block + 1) * rows)
        for part in range(6):
            cut = slice(part * rows, (part + 1) * rows)
            value = jnp.where(upper, high_ref[index, cut], low_ref[index, cut])
            if part < 3:
                qkv_ref[part, at] = value
            elif part < 5:
                pos_ref[part - 3, at] = value
            else:
                turned[at] = value
        if block == 0:
            vec_ref[...] = jnp.where(upper, high_ref[index, 6 * rows :], low_ref[index, 6 * rows :])
    out_ref[...] = turned[...].T


def place_grads(scalars, low, high, width):
    columns = low.shape[2]
    vec_rows = low.shape[1] - 6 * (width // (2 * low.shape[0]))
    return pl.pallas_call(
        place_grads_kernel,
        out_shape=(
            jax.ShapeDtypeStruct((3, width, columns), jnp.float32),
            jax.ShapeDtypeStruct((2, width, columns), jnp.float32),
            jax.ShapeDtypeStruct((columns, width), jnp.float32),
            jax.ShapeDtypeStruct((vec_rows, columns), jnp.float32),
        ),
        in_specs=[pl.BlockSpec(memory_space=pltpu.SMEM)] + [pl.BlockSpec(memory_space=pltpu.VMEM)] * 2,
        out_specs=[pl.BlockSpec(memory_space=pltpu.VMEM)] * 4,
        scratch_shapes=[pltpu.VMEM((width, columns), jnp.float32)],
        compiler_params=pltpu.CompilerParams(vmem_limit_bytes=40 << 20),
        cost_estimate=pl.CostEstimate(
            flops=0, transcendentals=0, bytes_accessed=16 * low.size
        ),
        name="place_grads",
    )(scalars, low, high)


def norm_parts(values):
    center = values - jnp.mean(values, axis=-1, keepdims=True)
    spread = jnp.mean(center * center, axis=-1, keepdims=True)
    scale = lax.rsqrt(spread + 1e-05)
    return center * scale, scale


def norm_back(grad, gain, xhat, scale):
    up = grad * gain
    mean = jnp.mean(up, axis=-1, keepdims=True)
    along = jnp.mean(up * xhat, axis=-1, keepdims=True)
    return scale * (up - mean - xhat * along)


def column_sum(values):
    return jnp.sum(values.astype(jnp.float32), axis=0)


def body(
    dp_size,
    mp_size,
    tokens,
    lengths,
    coords,
    w_qkv,
    w_pos,
    w_out,
    b_out,
    gain_one,
    shift_one,
    w_in,
    b_in,
    w_back,
    b_back,
    gain_two,
    shift_two,
    cotangent,
):
    pages, length, width = tokens.shape
    columns = w_qkv.shape[2]
    units = w_in.shape[1]
    here = lax.axis_index("mp")
    low = here & 1
    page = here >> 1
    group = lax.axis_index("dp")
    f32, bf16 = jnp.float32, jnp.bfloat16

    one = jnp.where(lengths[0] > 0, 1.0, 0.0).astype(f32)

    def arrived(value):
        return value * one

    def swap(value, bit):
        pairs = [(i, i ^ bit) for i in range(mp_size)]
        return lax.ppermute(value, "mp", pairs)

    def my_rows(value):
        rows = value.shape[0] // dp_size
        return lax.dynamic_slice_in_dim(value, group * rows, rows, 0)

    def gather(value):
        return arrived(lax.all_gather(value, "dp", axis=0, tiled=True))

    def take(value, index):
        return lax.dynamic_index_in_dim(value, index, 0, keepdims=False)

    def group_swap(value, bit):
        pairs = [(i, i ^ bit) for i in range(dp_size)]
        return lax.ppermute(value, "dp", pairs)

    def after(value, *others):
        return lax.optimization_barrier((value,) + others)[0]

    out_rows = swap(my_rows(w_out).astype(f32), FAR)
    w_out_far = gather(out_rows).astype(bf16)
    unit_rows = jnp.concatenate([my_rows(w_in), my_rows(w_back)], axis=0).astype(f32)
    far_rows = swap(jnp.concatenate([unit_rows, b_in[None], jnp.zeros((7, units), f32)], axis=0), FAR)

    table = jnp.asarray(angle_tables(width))
    mixed_all, proj, position = attend(lengths, tokens, coords, table, w_qkv, w_pos)
    far_rows = after(far_rows, mixed_all)
    b_in_far = far_rows[unit_rows.shape[0]]
    blocks = gather(far_rows[: unit_rows.shape[0]]).reshape(dp_size, unit_rows.shape[0], -1)
    in_rows = width // dp_size
    w_in_far = blocks[:, :in_rows].reshape(width, units).astype(bf16)
    w_back_far = blocks[:, in_rows:].reshape(units, width).astype(bf16)

    mixed_far = swap(take(mixed_all, 1 - page), FAR)
    mixed = jnp.concatenate([take(mixed_all, page), arrived(mixed_far)], axis=1).astype(bf16)
    w_out_two = jnp.concatenate([w_out, w_out_far], axis=0)
    w_in_two = jnp.concatenate([w_in, w_in_far], axis=1)
    w_back_two = jnp.concatenate([w_back, w_back_far], axis=0)
    b_in_two = jnp.concatenate([b_in, b_in_far], axis=0)
    rows = take(tokens, page)
    pos_rows = take(position, page)
    grad_out = take(cotangent, page).astype(f32)

    part = mm(mixed, w_out_two)
    other = swap(part, NEAR)
    head_rows = jnp.concatenate(
        [my_rows(w_qkv.reshape(-1, columns)), my_rows(w_pos.reshape(-1, columns))], axis=0
    )
    head_rows = swap(after(head_rows, part).astype(f32), FAR)
    head_rows = after(head_rows, other)
    blocks = gather(head_rows).reshape(dp_size, head_rows.shape[0], columns)
    qkv_rows = 3 * width // dp_size
    w_qkv_far = blocks[:, :qkv_rows].reshape(3, width, columns).astype(bf16)
    w_pos_far = blocks[:, qkv_rows:].reshape(2, width, columns).astype(bf16)

    first = rows.astype(f32) + (part + other + b_out)
    xhat_one, scale_one = norm_parts(first)
    normed = xhat_one * gain_one + shift_one
    normed_low = normed.astype(bf16)
    hidden_pre = mm(normed_low, w_in_two) + b_in_two
    cdf = 0.5 * (1.0 + lax.erf(hidden_pre * math.sqrt(0.5)))
    hidden = (hidden_pre * cdf).astype(bf16)
    part = mm(hidden, w_back_two)
    slope = cdf + hidden_pre * (
        jnp.exp(-0.5 * hidden_pre * hidden_pre) * (1.0 / math.sqrt(2.0 * math.pi))
    )
    second = normed + (part + swap(part, NEAR) + b_back)
    xhat_two, scale_two = norm_parts(second)
    d_second = norm_back(grad_out, gain_two, xhat_two, scale_two)
    d_feed = d_second.astype(bf16)
    d_hidden = mm_nt(d_feed, w_back_two)
    d_pre = (d_hidden * slope).astype(bf16)
    part = mm_nt(d_pre, w_in_two)
    other = swap(part, NEAR)
    d_normed = d_second + (part + other)

    half = length // 2

    def half_of(value, index):
        return lax.dynamic_slice_in_dim(value, index * half, half, 0)

    def spread(mine, far, rest):
        both = jnp.stack([mine, far])
        out = jnp.stack([jnp.where(low == 0, both, rest), jnp.where(low == 0, rest, both)], axis=1)
        out = out.reshape(pages, length, width)
        return jnp.where(page == 0, out, out[::-1])

    def to_blocks(value):
        return value.reshape(dp_size, -1, value.shape[1])

    def in_first(rows_of):
        value = jnp.stack(rows_of + [jnp.zeros_like(rows_of[0])] * (8 - len(rows_of)))
        return jnp.concatenate([value[None], jnp.zeros((dp_size - 1,) + value.shape, f32)], axis=0)

    d_w_back = mm_tn(hidden, d_feed)
    d_w_in = [mm_tn(normed_low, d_pre[:, :units]), mm_tn(normed_low, d_pre[:, units:])]
    d_b_in = column_sum(d_pre)
    vectors = [
        column_sum(d_feed),
        jnp.sum(grad_out * xhat_two, axis=0),
        jnp.sum(grad_out, axis=0),
    ]
    own = [to_blocks(d_w_in[0]), to_blocks(d_w_back[:units]), in_first([d_b_in[:units]] + vectors)]
    far = [to_blocks(d_w_in[1]), to_blocks(d_w_back[units:]), in_first([d_b_in[units:]] + vectors)]
    ffn = jnp.concatenate(own + far, axis=1)
    ffn = lax.psum_scatter(ffn.reshape(-1, width), "dp", scatter_dimension=0, tiled=True)

    d_first = norm_back(d_normed, gain_one, xhat_one, scale_one)
    d_branch = d_first.astype(bf16)
    d_mixed = mm_nt(d_branch, w_out_two).astype(bf16)
    far_proj = [mm(rows, w_qkv_far[k]).astype(bf16) for k in range(3)]
    far_proj += [mm(pos_rows, w_pos_far[k]).astype(bf16) for k in range(2)]
    scalars = jnp.stack([page, take(lengths, page)])
    d_heads = attend_back(scalars, proj, jnp.stack(far_proj), d_mixed)
    part = mm_nt(d_heads[0], jnp.concatenate([w_qkv[0], w_qkv_far[0]], axis=1))
    for k in (1, 2):
        part = part + mm_nt(d_heads[k], jnp.concatenate([w_qkv[k], w_qkv_far[k]], axis=1))

    chunks = 2
    piece = half // chunks

    def pieces(value):
        return [value[k * piece : (k + 1) * piece] for k in range(chunks)]

    sent = [swap(value, NEAR) for value in pieces(half_of(part, 1 - low))]
    base = pieces(half_of(part, low) + half_of(d_first, low))
    mine = [value + other_value for value, other_value in zip(base, sent)]
    far_mine = [swap(value, FAR) for value in mine]
    rest = [swap(jnp.stack(pair), NEAR) for pair in zip(mine, far_mine)]
    grad_tokens = spread(
        jnp.concatenate(mine, axis=0), jnp.concatenate(far_mine, axis=0), jnp.concatenate(rest, axis=1)
    )

    output = xhat_two * gain_two + shift_two
    out_mine = after(half_of(output, low), other)
    out_far = after(swap(out_mine, FAR), d_heads)
    out_rest = swap(after(jnp.stack([out_mine, out_far]), mine[-1]), NEAR)
    out_rest = after(out_rest, far_mine[-1])
    layer_out = arrived(spread(out_mine, out_far, out_rest)).astype(bf16)

    vectors = jnp.stack(
        [column_sum(d_branch), jnp.sum(d_normed * xhat_one, axis=0), jnp.sum(d_normed, axis=0)]
    ).reshape(-1, columns)
    vectors = jnp.pad(vectors, ((0, -vectors.shape[0] % 8), (0, 0)))
    vectors = jnp.concatenate([vectors, vectors], axis=1)
    scalars = jnp.reshape(group, (1,))
    total = weight_grads(dp_size, scalars, rows, pos_rows, d_heads, d_branch, mixed, vectors)

    bits = [1 << k for k in range(dp_size.bit_length() - 1)]

    def fold(value, bit_list, axis):
        shape = value.shape[1:]
        for bit in bit_list:
            value = value.reshape(((-1, 2) if axis else (2, -1)) + shape)
            kept, given = (value[:, 0], value[:, 1]) if axis else (value[0], value[1])
            value = kept + group_swap(given, bit)
        return value.reshape(shape)

    def unfold(value, bit_list, axis):
        shape = value.shape
        value = value[None]
        for bit in bit_list:
            value = jnp.stack([value, group_swap(value, bit)], axis=axis).reshape((-1,) + shape)
        return value

    cut = total.shape[1] // 16 * 8
    total = total.reshape(dp_size // 2, 2, total.shape[1], -1)
    total = total[:, 0] + group_swap(total[:, 1], bits[0])
    more = bits[1:]
    upper = fold(total[:, :cut], more, 1)
    lower = fold(total[:, cut:], more[::-1], 0)
    total = jnp.concatenate([upper, lower], axis=0)
    total = total[:, :columns] + swap(total[:, columns:], FAR)
    upper = unfold(total[:cut], more, 0)
    lower = unfold(total[cut:], more[::-1], 1)
    total = jnp.concatenate([upper, lower], axis=1)
    grad_w_qkv, grad_w_pos, grad_w_out, vectors = place_grads(
        scalars, total, group_swap(total, bits[0]), width
    )
    vectors = vectors.reshape(-1)
    grad_b_out, grad_gain_one, grad_shift_one = [
        vectors[k * width : (k + 1) * width] for k in range(3)
    ]

    ffn = after(ffn, mine[-1])
    count = ffn.shape[0] // 2
    ffn = ffn[:count] + swap(ffn[count:], FAR)
    ffn = lax.all_gather(ffn, "dp", axis=0, tiled=True).reshape(dp_size, count, -1)
    grad_w_in = ffn[:, :in_rows].reshape(width, units)
    grad_w_back = ffn[:, in_rows : in_rows + units // dp_size].reshape(units, width)
    vectors = ffn[0, in_rows + units // dp_size :]
    grad_b_in, grad_b_back, grad_gain_two, grad_shift_two = vectors[0], vectors[1], vectors[2], vectors[3]
    return (
        layer_out,
        grad_tokens,
        grad_w_qkv,
        grad_w_pos,
        grad_w_out,
        grad_b_out,
        grad_gain_one,
        grad_shift_one,
        grad_w_in,
        grad_b_in,
        grad_w_back,
        grad_b_back,
        grad_gain_two,
        grad_shift_two,
    )


def solution(mesh):
    placed = (
        P("dp", None, None),
        P("dp"),
        P("dp", None, None),
        P(None, None, "mp"),
        P(None, None, "mp"),
        P("mp", None),
        P(),
        P(),
        P(),
        P(None, "mp"),
        P("mp"),
        P("mp", None),
        P(),
        P(),
        P(),
        P("dp", None, None),
    )
    return jax.shard_map(
        partial(body, mesh.shape["dp"], mesh.shape["mp"]),
        mesh=mesh,
        in_specs=placed,
        out_specs=(
            P("dp", None, None),
            P("dp", None, None),
            P(None, None, "mp"),
            P(None, None, "mp"),
            P("mp", None),
            P(),
            P(),
            P(),
            P(None, "mp"),
            P("mp"),
            P("mp", None),
            P(),
            P(),
            P(),
        ),
        check_vma=False,
    )
```

```python
from functools import partial
import math

import jax
import jax.numpy as jnp
import numpy as np
from jax import lax
from jax.experimental import pallas as pl
from jax.experimental.pallas import tpu as pltpu
from jax.sharding import PartitionSpec as P

HEAD_DIM = 64
STEP_BITS = 5
STEP = 1 << STEP_BITS
NEAR = 1
FAR = 2
MASKED = -1e30


def mm(left, right):
    return jnp.dot(left, right, preferred_element_type=jnp.float32)


def mm_nt(left, right):
    return lax.dot_general(
        left, right, (((1,), (1,)), ((), ())), preferred_element_type=jnp.float32
    )


def mm_tn(left, right):
    return lax.dot_general(
        left, right, (((0,), (0,)), ((), ())), preferred_element_type=jnp.float32
    )


def angle_tables(model_width):
    quarter = model_width // 4
    rate = np.exp(np.arange(quarter) * (-math.log(10000.0) / quarter))
    fine = np.arange(STEP)[:, None] * rate
    coarse = fine * STEP
    zero = np.zeros((STEP, 2 * quarter))
    table = np.concatenate(
        [
            np.concatenate([np.sin(coarse), np.cos(coarse), zero], axis=1),
            np.concatenate([zero, np.sin(fine), np.cos(fine)], axis=1),
        ],
        axis=0,
    )
    parts = []
    rest = table
    for _ in range(3):
        part = rest.astype(jnp.bfloat16)
        parts.append(part)
        rest = rest - part.astype(np.float64)
    return np.concatenate(parts, axis=0)


def sinusoid(coord, table_ref):
    quarter = table_ref.shape[1] // 4
    slot = lax.broadcasted_iota(jnp.int32, (2 * STEP, coord.shape[1]), 0)
    coarse = coord >> STEP_BITS
    fine = (coord & (STEP - 1)) + STEP
    hit = ((slot == coarse) | (slot == fine)).astype(jnp.float32).astype(jnp.bfloat16)
    looked = mm_tn(jnp.concatenate([hit, hit, hit], axis=0), table_ref[...])
    sin_a, cos_a, sin_b, cos_b = [looked[:, k * quarter : (k + 1) * quarter] for k in range(4)]
    return jnp.concatenate([sin_a * cos_b + cos_a * sin_b, cos_a * cos_b - sin_a * sin_b], axis=1)


def head_of(ref, index, head):
    return ref[index, :, head * HEAD_DIM : (head + 1) * HEAD_DIM]


def probs_t(q, k, pq, pk, length, factor):
    left = jnp.concatenate([k, pk, k], axis=1)
    right = jnp.concatenate([q, q, pq], axis=1)
    scores = mm_nt(left, right) * factor
    visible = lax.broadcasted_iota(jnp.int32, scores.shape, 0) < length
    scores = jnp.where(visible, scores, MASKED)
    raised = jnp.exp(scores - jnp.max(scores, axis=0, keepdims=True))
    return raised * (1.0 / jnp.sum(raised, axis=0, keepdims=True))


def attend_kernel(
    heads, keep, scalars_ref, x_ref, coords_ref, table_ref, wqkv_ref, wpos_ref, mixed_ref, *kept
):
    length = scalars_ref[1]
    factor = 1.0 / math.sqrt(3.0 * HEAD_DIM)
    proj_ref, pos_ref = kept
    rows = x_ref[0]
    for part in range(3):
        proj_ref[part] = mm(rows, wqkv_ref[part]).astype(jnp.bfloat16)
    sides = [sinusoid(coords_ref[0, axis : axis + 1], table_ref) for axis in range(2)]
    position = jnp.concatenate(sides, axis=1).astype(jnp.bfloat16)
    if keep:
        pos_ref[...] = position
    for part in range(2):
        proj_ref[3 + part] = mm(position, wpos_ref[part]).astype(jnp.bfloat16)
    for head in range(heads):
        q, k, v, pq, pk = [head_of(proj_ref, part, head) for part in range(5)]
        weights = probs_t(q, k, pq, pk, length, factor).astype(jnp.bfloat16)
        mixed = mm_tn(v, weights).T
        mixed = mixed.astype(jnp.bfloat16).astype(mixed_ref.dtype)
        mixed_ref[:, head * HEAD_DIM : (head + 1) * HEAD_DIM] = mixed


def attend(keep, scalars, tokens, coords, table, w_qkv, w_pos):
    pages, length, width = tokens.shape
    columns = w_qkv.shape[2]
    whole = lambda *shape: pl.BlockSpec(shape, lambda i, s: (0,) * len(shape))
    proj = jax.ShapeDtypeStruct((5, length, columns), jnp.bfloat16)
    pos = jax.ShapeDtypeStruct((length, width), jnp.bfloat16)
    mixed = jax.ShapeDtypeStruct((length, columns), jnp.bfloat16 if keep else jnp.float32)
    shapes = (mixed, proj, pos) if keep else (mixed,)
    return pl.pallas_call(
        partial(attend_kernel, columns // HEAD_DIM, keep),
        out_shape=shapes,
        grid_spec=pltpu.PrefetchScalarGridSpec(
            num_scalar_prefetch=1,
            grid=(1,),
            in_specs=[
                pl.BlockSpec((1, length, width), lambda i, s: (s[0], 0, 0)),
                pl.BlockSpec((1,) + coords.shape[1:], lambda i, s: (s[0], 0, 0)),
                whole(*table.shape),
                whole(*w_qkv.shape),
                whole(*w_pos.shape),
            ],
            out_specs=[whole(*shape.shape) for shape in shapes],
            scratch_shapes=[]
            if keep
            else [pltpu.VMEM(proj.shape, proj.dtype), pltpu.VMEM((8, 128), jnp.bfloat16)],
        ),
        compiler_params=pltpu.CompilerParams(vmem_limit_bytes=40 << 20),
        cost_estimate=pl.CostEstimate(
            flops=2 * length * columns * (5 * width + 4 * length),
            transcendentals=length * length * columns // HEAD_DIM,
            bytes_accessed=length * (4 * width + 14 * columns),
        ),
        name="attend",
    )(scalars, tokens, coords, table, w_qkv, w_pos)


def norm_parts(values):
    center = values - jnp.mean(values, axis=-1, keepdims=True)
    spread = jnp.mean(center * center, axis=-1, keepdims=True)
    scale = lax.rsqrt(spread + 1e-05)
    return center * scale, scale


def norm_back(grad, gain, xhat, scale):
    up = grad * gain
    mean = jnp.mean(up, axis=-1, keepdims=True)
    along = jnp.mean(up * xhat, axis=-1, keepdims=True)
    return scale * (up - mean - xhat * along)


def column_sum(values):
    return jnp.sum(values.astype(jnp.float32), axis=0, keepdims=True)


def feed_kernel(
    scalars_ref, x_ref, part_ref, other_ref, b_out_ref, gain_ref, shift_ref, w_in_ref, w_in_far_ref, b_in_ref,
    w_back_ref, w_back_far_ref, next_ref, xhat_ref, scale_ref, low_ref, hidden_ref, slope_ref,
):
    first = x_ref[0].astype(jnp.float32) + (part_ref[...] + other_ref[...] + b_out_ref[...])
    xhat, scale = norm_parts(first)
    low = (xhat * gain_ref[...] + shift_ref[...]).astype(jnp.bfloat16)
    xhat_ref[...] = xhat
    scale_ref[...] = scale
    low_ref[...] = low
    units = w_in_ref.shape[1]
    total = None
    for side, (into, back) in enumerate(((w_in_ref, w_back_ref), (w_in_far_ref, w_back_far_ref))):
        at = slice(side * units, (side + 1) * units)
        pre = mm(low, into[...]) + b_in_ref[side : side + 1]
        cdf = 0.5 * (1.0 + lax.erf(pre * math.sqrt(0.5)))
        hidden = (pre * cdf).astype(jnp.bfloat16)
        hidden_ref[:, at] = hidden
        slope_ref[:, at] = cdf + pre * (jnp.exp(-0.5 * pre * pre) * (1.0 / math.sqrt(2.0 * math.pi)))
        product = mm(hidden, back[...])
        total = product if total is None else total + product
    next_ref[...] = total


def feed_back_kernel(
    scalars_ref, cot_ref, part_ref, other_ref, xhat_ref, slope_ref, gain_one_ref, shift_one_ref, b_back_ref,
    gain_ref, shift_ref, w_in_ref, w_in_far_ref, w_back_ref, w_back_far_ref,
    next_ref, second_ref, feed_ref, pre_ref, out_ref, sums_ref, sums_in_ref,
):
    normed = xhat_ref[...] * gain_one_ref[...] + shift_one_ref[...]
    second = normed + (part_ref[...] + other_ref[...] + b_back_ref[...])
    xhat, scale = norm_parts(second)
    out_ref[...] = xhat * gain_ref[...] + shift_ref[...]
    grad = cot_ref[0].astype(jnp.float32)
    d_second = norm_back(grad, gain_ref[...], xhat, scale)
    second_ref[...] = d_second
    d_feed = d_second.astype(jnp.bfloat16)
    feed_ref[...] = d_feed
    sums_ref[0:1] = column_sum(d_feed)
    sums_ref[1:2] = column_sum(grad * xhat)
    sums_ref[2:3] = column_sum(grad)
    units = w_in_ref.shape[1]
    total = None
    for side, (into, back) in enumerate(((w_in_ref, w_back_ref), (w_in_far_ref, w_back_far_ref))):
        at = slice(side * units, (side + 1) * units)
        d_pre = (mm_nt(d_feed, back[...]) * slope_ref[:, at]).astype(jnp.bfloat16)
        pre_ref[:, at] = d_pre
        sums_in_ref[side : side + 1] = column_sum(d_pre)
        product = mm_nt(d_pre, into[...])
        total = product if total is None else total + product
    next_ref[...] = total


def on_chunk(kernel, name, chunk, scalars, pages_array, rows, arrays, shapes):
    length, width = pages_array.shape[1:]
    whole = lambda shape: pl.BlockSpec(shape, lambda i, s: (0,) * len(shape))
    return pl.pallas_call(
        kernel,
        out_shape=shapes,
        grid_spec=pltpu.PrefetchScalarGridSpec(
            num_scalar_prefetch=1,
            grid=(1,),
            in_specs=[pl.BlockSpec((1, rows, width), lambda i, s: (s[0], chunk, 0))]
            + [whole(array.shape) for array in arrays],
            out_specs=[whole(shape.shape) for shape in shapes],
        ),
        compiler_params=pltpu.CompilerParams(vmem_limit_bytes=48 << 20),
        cost_estimate=pl.CostEstimate(
            flops=16 * rows * width * width, transcendentals=2 * rows * width, bytes_accessed=40 * rows * width
        ),
        name=name,
    )(scalars, pages_array, *arrays)


def feed_grads_kernel(count, low_ref, pre_ref, hidden_ref, feed_ref, out_ref):
    rows = out_ref.shape[2]

    def put(left, right):
        product = mm_tn(left[...], right[...])
        for block in range(count):
            out_ref[block, 0] = product[block * rows : (block + 1) * rows]

    @pl.when(pl.program_id(0) % 2 == 0)
    def _():
        put(low_ref, pre_ref)

    @pl.when(pl.program_id(0) % 2 == 1)
    def _():
        put(hidden_ref, feed_ref)


def feed_grads(count, low, d_pre, hidden, d_feed):
    length, width = low.shape
    units = hidden.shape[1] // 2
    return pl.pallas_call(
        partial(feed_grads_kernel, count),
        out_shape=jax.ShapeDtypeStruct((count, 4, width // count, units), jnp.float32),
        grid_spec=pl.GridSpec(
            grid=(4,),
            in_specs=[
                pl.BlockSpec((length, width), lambda i: (0, 0)),
                pl.BlockSpec((length, units), lambda i: (0, i // 2)),
                pl.BlockSpec((length, units), lambda i: (0, i // 2)),
                pl.BlockSpec((length, width), lambda i: (0, 0)),
            ],
            out_specs=pl.BlockSpec((count, 1, width // count, units), lambda i: (0, i, 0, 0)),
        ),
        compiler_params=pltpu.CompilerParams(vmem_limit_bytes=40 << 20),
        cost_estimate=pl.CostEstimate(
            flops=8 * length * width * units, transcendentals=0, bytes_accessed=16 * width * units
        ),
        name="feed_grads",
    )(low, d_pre, hidden, d_feed)


def far_proj_kernel(count, x_ref, pos_ref, blocks_ref, proj_ref, wqkv_ref):
    width = x_ref.shape[1]
    rows = width // count
    for part in range(5):
        weight = jnp.concatenate([blocks_ref[block, part] for block in range(count)], axis=0)
        weight = weight.astype(jnp.bfloat16)
        if part < 3:
            wqkv_ref[part] = weight
        left = x_ref if part < 3 else pos_ref
        proj_ref[part] = mm(left[...], weight).astype(jnp.bfloat16)


def far_proj(rows, pos_rows, blocks):
    count, parts, block_rows, columns = blocks.shape
    length, width = rows.shape
    whole = lambda shape: pl.BlockSpec(shape, lambda i: (0,) * len(shape))
    shapes = (
        jax.ShapeDtypeStruct((parts, length, columns), jnp.bfloat16),
        jax.ShapeDtypeStruct((3, width, columns), jnp.bfloat16),
    )
    return pl.pallas_call(
        partial(far_proj_kernel, count),
        out_shape=shapes,
        grid_spec=pl.GridSpec(
            grid=(1,),
            in_specs=[whole(rows.shape), whole(pos_rows.shape), whole(blocks.shape)],
            out_specs=[whole(shape.shape) for shape in shapes],
        ),
        compiler_params=pltpu.CompilerParams(vmem_limit_bytes=40 << 20),
        cost_estimate=pl.CostEstimate(
            flops=2 * parts * length * width * columns, transcendentals=0, bytes_accessed=4 * blocks.size
        ),
        name="far_proj",
    )(rows, pos_rows, blocks)


def attend_back_kernel(
    heads, scalars_ref, part_a, part_b, other_a, other_b, second_a, second_b, xhat_a, xhat_b, scale_a, scale_b,
    gain_ref, w_out_ref, w_out_far_ref, own_ref, far_ref, wqkv_ref, wqkv_far_ref,
    send_ref, base_ref, d_ref, branch_ref, sums_ref, dm_ref, first_ref,
):
    length, low = scalars_ref[1], scalars_ref[2]
    factor = 1.0 / math.sqrt(3.0 * HEAD_DIM)
    columns = heads * HEAD_DIM
    half = part_a.shape[0]
    sums = None
    chunks = ((part_a, other_a, second_a, xhat_a, scale_a), (part_b, other_b, second_b, xhat_b, scale_b))
    for index, (part, other, second, xhat, scale) in enumerate(chunks):
        at = slice(index * half, (index + 1) * half)
        d_normed = second[...] + (part[...] + other[...])
        d_first = norm_back(d_normed, gain_ref[...], xhat[...], scale[...])
        first_ref[at] = d_first
        d_branch = d_first.astype(jnp.bfloat16)
        branch_ref[at] = d_branch
        some = (column_sum(d_branch), column_sum(d_normed * xhat[...]), column_sum(d_normed))
        sums = some if sums is None else tuple(x + y for x, y in zip(sums, some))
        dm_ref[at, :columns] = mm_nt(d_branch, w_out_ref[...]).astype(jnp.bfloat16)
        dm_ref[at, columns:] = mm_nt(d_branch, w_out_far_ref[...]).astype(jnp.bfloat16)
    for index, value in enumerate(sums):
        sums_ref[index : index + 1] = value
    for side, here in enumerate((own_ref, far_ref)):
        for head in range(heads):
            q, k, v, pq, pk = [head_of(here, part, head) for part in range(5)]
            at = side * columns + head * HEAD_DIM
            dm = dm_ref[:, at : at + HEAD_DIM]
            probs = probs_t(q, k, pq, pk, length, factor)
            weights = probs.astype(jnp.bfloat16)
            d_values = mm(weights, dm)
            d_probs = mm_nt(v, dm)
            inner = jnp.sum(d_probs * probs, axis=0, keepdims=True)
            d_scores = (probs * (d_probs - inner)).astype(jnp.bfloat16)
            by_queries = mm(d_scores, jnp.concatenate([q, pq], axis=1))
            by_query, by_pos_query = by_queries[:, :HEAD_DIM], by_queries[:, HEAD_DIM:]
            by_keys = mm_tn(jnp.concatenate([k, pk], axis=1), d_scores).T
            by_key, by_pos_key = by_keys[:, :HEAD_DIM], by_keys[:, HEAD_DIM:]
            grads = (
                (by_key + by_pos_key) * factor,
                (by_query + by_pos_query) * factor,
                d_values,
                by_key * factor,
                by_query * factor,
            )
            for part, value in enumerate(grads):
                d_ref[part, :, at : at + HEAD_DIM] = value.astype(jnp.bfloat16)
    for index, ref in enumerate((base_ref, send_ref)):
        at = pl.multiple_of(jnp.where(low == index, 0, half), half)
        at = pl.ds(at, half)
        total = first_ref[at] if index == 0 else None
        for part in range(3):
            for side, weights in enumerate((wqkv_ref, wqkv_far_ref)):
                left = d_ref[part, at, side * columns : (side + 1) * columns]
                product = mm_nt(left, weights[part])
                total = product if total is None else total + product
        ref[...] = total


def attend_back(scalars, arrays):
    proj = arrays[13]
    parts, length, columns = proj.shape
    half, width = arrays[0].shape
    heads = columns // HEAD_DIM
    whole = lambda shape: pl.BlockSpec(shape, lambda i, s: (0,) * len(shape))
    shapes = (
        jax.ShapeDtypeStruct((half, width), jnp.float32),
        jax.ShapeDtypeStruct((half, width), jnp.float32),
        jax.ShapeDtypeStruct((parts, length, 2 * columns), jnp.bfloat16),
        jax.ShapeDtypeStruct((length, width), jnp.bfloat16),
        jax.ShapeDtypeStruct((3, width), jnp.float32),
    )
    return pl.pallas_call(
        partial(attend_back_kernel, heads),
        out_shape=shapes,
        grid_spec=pltpu.PrefetchScalarGridSpec(
            num_scalar_prefetch=1,
            grid=(1,),
            in_specs=[whole(array.shape) for array in arrays],
            out_specs=[whole(shape.shape) for shape in shapes],
            scratch_shapes=[
                pltpu.VMEM((length, 2 * columns), jnp.bfloat16),
                pltpu.VMEM((length, width), jnp.float32),
            ],
        ),
        compiler_params=pltpu.CompilerParams(vmem_limit_bytes=48 << 20),
        cost_estimate=pl.CostEstimate(
            flops=2 * 2 * heads * length * length * HEAD_DIM * 9 + 20 * length * width * columns,
            transcendentals=2 * heads * length * length,
            bytes_accessed=40 * length * width,
        ),
        name="attend_back",
    )(scalars, *arrays)


def weight_grads_kernel(
    count, scalars_ref, x_ref, pos_ref, d_ref, db_ref, mixed_ref, far_ref, vec_ref, keep_ref, send_ref
):
    group = scalars_ref[0]
    rows = x_ref.shape[1] // count
    mixed = jnp.concatenate([mixed_ref[...], far_ref[...]], axis=1)
    lefts = [x_ref] * 3 + [pos_ref] * 2 + [db_ref]
    odd = group & 1
    for part, left in enumerate(lefts):
        product = mm_tn(left[...], d_ref[part] if part < 5 else mixed)
        at = slice(part * rows, (part + 1) * rows)
        for block in range(count):
            ref, place = (keep_ref, send_ref)[block & 1], (block ^ group) >> 1
            value = product[block * rows : (block + 1) * rows]

            @pl.when(odd == (block & 1))
            def _():
                keep_ref[place, at] = value

            @pl.when(odd != (block & 1))
            def _():
                send_ref[place, at] = value

    at = slice(6 * rows, None)
    keep_ref[:, at] = jnp.zeros((count // 2,) + vec_ref.shape, jnp.float32)
    send_ref[:, at] = jnp.zeros((count // 2,) + vec_ref.shape, jnp.float32)

    @pl.when(odd == 0)
    def _():
        keep_ref[group >> 1, at] = vec_ref[...]

    @pl.when(odd == 1)
    def _():
        send_ref[group >> 1, at] = vec_ref[...]


def weight_grads(count, scalars, rows, pos_rows, d_heads, d_branch, mixed, mixed_far, vectors):
    length, width = rows.shape
    wide = d_heads.shape[2]
    block = 6 * (width // count) + vectors.shape[0]
    shape = jax.ShapeDtypeStruct((count // 2, block, wide), jnp.float32)
    return pl.pallas_call(
        partial(weight_grads_kernel, count),
        out_shape=(shape, shape),
        in_specs=[pl.BlockSpec(memory_space=pltpu.SMEM)] + [pl.BlockSpec(memory_space=pltpu.VMEM)] * 7,
        out_specs=[pl.BlockSpec(memory_space=pltpu.VMEM)] * 2,
        compiler_params=pltpu.CompilerParams(vmem_limit_bytes=48 << 20),
        cost_estimate=pl.CostEstimate(
            flops=12 * length * width * wide,
            transcendentals=0,
            bytes_accessed=4 * count * block * wide + 10 * length * wide + 6 * length * width,
        ),
        name="weight_grads",
    )(scalars, rows, pos_rows, d_heads, d_branch, mixed, mixed_far, vectors)


def place_grads_kernel(
    order, scalars_ref, low_a_ref, low_b_ref, high_a_ref, high_b_ref, qkv_ref, pos_ref, out_ref, vec_ref, turned
):
    group = scalars_ref[0]
    count = 2 * low_a_ref.shape[0]
    rows = qkv_ref.shape[1] // count
    cut = low_a_ref.shape[1]

    def read(place, start, stop):
        upper = (place & 1) == 1
        index = place >> 1
        pieces = []
        if start < cut:
            at = slice(start, min(stop, cut))
            pieces.append(jnp.where(upper, high_a_ref[index, at], low_a_ref[index, at]))
        if stop > cut:
            at = slice(max(start, cut) - cut, stop - cut)
            turned_index = 0
            for bit in range(len(order)):
                turned_index = turned_index | (((index >> bit) & 1) << order[bit])
            pieces.append(jnp.where(upper, high_b_ref[turned_index, at], low_b_ref[turned_index, at]))
        return jnp.concatenate(pieces, axis=0) if len(pieces) > 1 else pieces[0]

    for block in range(count):
        place = block ^ group
        at = slice(block * rows, (block + 1) * rows)
        for part in range(6):
            value = read(place, part * rows, (part + 1) * rows)
            if part < 3:
                qkv_ref[part, at] = value
            elif part < 5:
                pos_ref[part - 3, at] = value
            else:
                turned[at] = value
        if block == 0:
            vec_ref[...] = read(place, 6 * rows, cut + low_b_ref.shape[1])
    out_ref[...] = turned[...].T


def place_grads(scalars, parts, width, vec_rows):
    columns = parts[0].shape[2]
    bits = parts[0].shape[0].bit_length() - 1
    whole = lambda shape: pl.BlockSpec(shape, lambda i: (0,) * len(shape))
    shapes = (
        jax.ShapeDtypeStruct((3, width, columns), jnp.float32),
        jax.ShapeDtypeStruct((2, width, columns), jnp.float32),
        jax.ShapeDtypeStruct((columns, width), jnp.float32),
        jax.ShapeDtypeStruct((vec_rows, columns), jnp.float32),
    )
    return pl.pallas_call(
        partial(place_grads_kernel, tuple(range(bits))[::-1]),
        out_shape=shapes,
        grid_spec=pl.GridSpec(
            grid=(1,),
            in_specs=[pl.BlockSpec(memory_space=pltpu.SMEM)] + [whole(part.shape) for part in parts],
            out_specs=[whole(shape.shape) for shape in shapes],
            scratch_shapes=[pltpu.VMEM((width, columns), jnp.float32)],
        ),
        compiler_params=pltpu.CompilerParams(vmem_limit_bytes=40 << 20),
        cost_estimate=pl.CostEstimate(
            flops=0, transcendentals=0, bytes_accessed=32 * width * columns * 3
        ),
        name="place_grads",
    )(scalars, *parts)


def body(
    dp_size,
    mp_size,
    tokens,
    lengths,
    coords,
    w_qkv,
    w_pos,
    w_out,
    b_out,
    gain_one,
    shift_one,
    w_in,
    b_in,
    w_back,
    b_back,
    gain_two,
    shift_two,
    cotangent,
):
    pages, length, width = tokens.shape
    columns = w_qkv.shape[2]
    units = w_in.shape[1]
    here = lax.axis_index("mp")
    low = here & 1
    page = here >> 1
    group = lax.axis_index("dp")
    f32, bf16 = jnp.float32, jnp.bfloat16
    half = length // 2
    one = jnp.where(lengths[0] > 0, 1.0, 0.0).astype(f32)

    def arrived(value):
        return value * one

    def swap(value, bit):
        pairs = [(i, i ^ bit) for i in range(mp_size)]
        return lax.ppermute(value, "mp", pairs)

    def group_swap(value, bit):
        pairs = [(i, i ^ bit) for i in range(dp_size)]
        return lax.ppermute(value, "dp", pairs)

    def my_rows(value):
        rows = value.shape[0] // dp_size
        return lax.dynamic_slice_in_dim(value, group * rows, rows, 0)

    def gather(value):
        return lax.all_gather(value, "dp", axis=0, tiled=True)

    def take(value, index):
        return lax.dynamic_index_in_dim(value, index, 0, keepdims=False)

    def after(value, *others):
        return lax.optimization_barrier((value,) + others)[0]

    def row(value):
        return value.reshape(1, -1)

    chunk_rows = lambda value: [value[:half], value[half:]]

    unit_rows = jnp.concatenate([my_rows(w_in), my_rows(w_back)], axis=0).astype(f32)
    tail = jnp.concatenate([row(b_in), jnp.zeros((7, units), f32)], axis=0)
    far_rows = swap(jnp.concatenate([unit_rows, tail], axis=0), FAR)
    out_rows = swap(my_rows(w_out).astype(f32), FAR)

    table = jnp.asarray(angle_tables(width))
    mine_scalars = jnp.stack([page, take(lengths, page), low])
    their_scalars = jnp.stack([1 - page, take(lengths, 1 - page), low])
    (mixed_send,) = attend(False, their_scalars, tokens, coords, table, w_qkv, w_pos)
    mixed_far = swap(mixed_send, FAR)
    far_rows = after(far_rows, mixed_send)
    tokens_later = after(tokens, far_rows)
    mixed, proj, pos_rows = attend(True, mine_scalars, tokens_later, coords, table, w_qkv, w_pos)
    w_out_far = arrived(gather(after(out_rows, mixed_send))).astype(bf16)
    count = unit_rows.shape[0]
    b_in_two = jnp.stack([b_in, far_rows[count]])
    blocks = arrived(gather(far_rows[:count])).reshape(dp_size, count, -1)
    in_rows = width // dp_size
    w_in_far = blocks[:, :in_rows].reshape(width, units).astype(bf16)
    w_back_far = blocks[:, in_rows:].reshape(units, width).astype(bf16)

    mixed_far = arrived(mixed_far).astype(bf16)
    part = [
        mm(own, w_out) + mm(far, w_out_far) for own, far in zip(chunk_rows(mixed), chunk_rows(mixed_far))
    ]
    other = [swap(value, NEAR) for value in part]
    head_rows = jnp.concatenate([w_qkv, w_pos], axis=0)
    head_rows = lax.dynamic_slice_in_dim(after(head_rows, part[1]), group * in_rows, in_rows, 1)
    head_rows = swap(head_rows.astype(f32), FAR)

    rows_of = jax.ShapeDtypeStruct((half, width), f32)
    rows_low = jax.ShapeDtypeStruct((half, width), bf16)
    units_of = jax.ShapeDtypeStruct((half, 2 * units), f32)
    units_low = jax.ShapeDtypeStruct((half, 2 * units), bf16)
    scale_of = jax.ShapeDtypeStruct((half, 1), f32)
    fed = []
    for index in range(2):
        arrays = [part[index], other[index], row(b_out), row(gain_one), row(shift_one)]
        arrays += [w_in, w_in_far, b_in_two, w_back, w_back_far]
        shapes = (rows_of, rows_of, scale_of, rows_low, units_low, units_of)
        fed.append(
            on_chunk(feed_kernel, "feed", index, mine_scalars, tokens, half, arrays, shapes)
        )
    part = [value[0] for value in fed]
    other = [swap(value, NEAR) for value in part]
    head_rows = after(head_rows, other[0])
    blocks = gather(head_rows.reshape(-1, columns)).reshape(dp_size, 5, in_rows, columns)
    back = []
    for index in range(2):
        arrays = [part[index], other[index], fed[index][1], fed[index][5], row(gain_one), row(shift_one)]
        arrays += [row(b_back), row(gain_two), row(shift_two), w_in, w_in_far, w_back, w_back_far]
        shapes = (rows_of, rows_of, rows_low, units_low, rows_of)
        shapes += (jax.ShapeDtypeStruct((3, width), f32), jax.ShapeDtypeStruct((2, units), f32))
        back.append(
            on_chunk(feed_back_kernel, "feed_back", index, mine_scalars, cotangent, half, arrays, shapes)
        )
    part = [value[0] for value in back]
    other = [swap(value, NEAR) for value in part]

    rows = take(tokens, page)
    proj_far, w_qkv_far = far_proj(rows, pos_rows, after(blocks, part[1]))
    both = lambda index, source: jnp.concatenate([source[0][index], source[1][index]], axis=0)
    d_feed = after(both(2, back), other[0])
    ffn = feed_grads(dp_size, both(3, fed), both(3, back), both(4, fed), d_feed)
    ffn = lax.psum_scatter(ffn.reshape(-1, units), "dp", scatter_dimension=0, tiled=True)

    arrays = part + other + [back[0][1], back[1][1], fed[0][1], fed[1][1], fed[0][2], fed[1][2]]
    arrays += [row(gain_one), w_out, w_out_far]
    arrays += [proj, proj_far, w_qkv, w_qkv_far]
    send, base, d_heads, d_branch, sums = attend_back(mine_scalars, arrays)

    chunks = 2
    piece = half // chunks

    def pieces(value):
        return [value[k * piece : (k + 1) * piece] for k in range(chunks)]

    def spread(mine, far, rest):
        both = jnp.stack([mine, far])
        out = jnp.stack([jnp.where(low == 0, both, rest), jnp.where(low == 0, rest, both)], axis=1)
        out = out.reshape(pages, length, width)
        return jnp.where(page == 0, out, out[::-1])

    sent = [swap(value, NEAR) for value in pieces(send)]
    mine = [value + other_value for value, other_value in zip(pieces(base), sent)]
    far_mine = [swap(value, FAR) for value in mine]
    rest = [swap(jnp.stack(pair), NEAR) for pair in zip(mine, far_mine)]
    grad_tokens = spread(
        jnp.concatenate(mine, axis=0), jnp.concatenate(far_mine, axis=0), jnp.concatenate(rest, axis=1)
    )

    out_mine = jnp.where(low == 0, back[0][4], back[1][4])
    out_mine = after(out_mine, other[1])
    out_far = after(swap(out_mine, FAR), send)
    out_rest = swap(after(jnp.stack([out_mine, out_far]), mine[-1]), NEAR)
    out_rest = after(out_rest, far_mine[-1])
    layer_out = arrived(spread(out_mine, out_far, out_rest)).astype(bf16)

    vectors = jnp.concatenate([sums, back[0][5] + back[1][5]], axis=0)
    vectors = vectors.reshape(-1, columns)
    vectors = jnp.concatenate([vectors, vectors], axis=1)
    d_b_in = (back[0][6] + back[1][6]).reshape(2, -1, columns)
    vectors = jnp.concatenate([vectors, jnp.concatenate([d_b_in[0], d_b_in[1]], axis=1)], axis=0)
    vectors = jnp.pad(vectors, ((0, -vectors.shape[0] % 16), (0, 0)))
    scalars = jnp.reshape(group, (1,))
    keep, give = weight_grads(
        dp_size, scalars, rows, pos_rows, d_heads, d_branch, mixed, mixed_far, vectors
    )
    bits = [1 << k for k in range(dp_size.bit_length() - 1)]

    def fold(value, bit_list, axis):
        shape = value.shape[1:]
        for bit in bit_list:
            value = value.reshape(((-1, 2) if axis else (2, -1)) + shape)
            kept, given = (value[:, 0], value[:, 1]) if axis else (value[0], value[1])
            value = kept + group_swap(given, bit)
        return value.reshape(shape)

    def unfold(value, bit_list):
        value = value[None]
        for bit in bit_list:
            value = jnp.concatenate([value, group_swap(value, bit)], axis=0)
        return value

    cut = keep.shape[1] // 16 * 8
    total = keep + group_swap(give, bits[0])
    more = bits[1:]
    upper = fold(total[:, :cut], more, 1)
    lower = fold(total[:, cut:], more[::-1], 0)
    total = jnp.concatenate([upper, lower], axis=0)
    total = total[:, :columns] + swap(total[:, columns:], FAR)
    upper = unfold(total[:cut], more)
    lower = unfold(total[cut:], more[::-1])
    parts = [upper, lower, group_swap(upper, bits[0]), group_swap(lower, bits[0])]
    grad_w_qkv, grad_w_pos, grad_w_out, vectors = place_grads(
        scalars, parts, width, vectors.shape[0]
    )
    vectors = vectors[: 7 * width // columns].reshape(7, width)
    grad_b_out, grad_gain_one, grad_shift_one = vectors[0], vectors[1], vectors[2]
    grad_b_back, grad_gain_two, grad_shift_two = vectors[3], vectors[4], vectors[5]
    grad_b_in = vectors[6]

    ffn = after(ffn, mine[-1])
    count = ffn.shape[0] // 2
    ffn = ffn[:count] + after(swap(ffn[count:], FAR), far_mine[0])
    grad_w_in = gather(ffn[:in_rows])
    grad_w_back = gather(ffn[in_rows:])
    return (
        layer_out,
        grad_tokens,
        grad_w_qkv,
        grad_w_pos,
        grad_w_out,
        grad_b_out,
        grad_gain_one,
        grad_shift_one,
        grad_w_in,
        grad_b_in,
        grad_w_back,
        grad_b_back,
        grad_gain_two,
        grad_shift_two,
    )


def solution(mesh):
    placed = (
        P("dp", None, None),
        P("dp"),
        P("dp", None, None),
        P(None, None, "mp"),
        P(None, None, "mp"),
        P("mp", None),
        P(),
        P(),
        P(),
        P(None, "mp"),
        P("mp"),
        P("mp", None),
        P(),
        P(),
        P(),
        P("dp", None, None),
    )
    return jax.shard_map(
        partial(body, mesh.shape["dp"], mesh.shape["mp"]),
        mesh=mesh,
        in_specs=placed,
        out_specs=(
            P("dp", None, None),
            P("dp", None, None),
            P(None, None, "mp"),
            P(None, None, "mp"),
            P("mp", None),
            P(),
            P(),
            P(),
            P(None, "mp"),
            P("mp"),
            P("mp", None),
            P(),
            P(),
            P(),
        ),
        check_vma=False,
    )
```

```python
from functools import partial
import math

import jax
import jax.numpy as jnp
import numpy as np
from jax import lax
from jax.experimental import pallas as pl
from jax.experimental.pallas import tpu as pltpu
from jax.sharding import PartitionSpec as P

HEAD_DIM = 64
STEP_BITS = 5
STEP = 1 << STEP_BITS
NEAR = 1
FAR = 2
MASKED = -1e30


def mm(left, right):
    return jnp.dot(left, right, preferred_element_type=jnp.float32)


def mm_nt(left, right):
    return lax.dot_general(
        left, right, (((1,), (1,)), ((), ())), preferred_element_type=jnp.float32
    )


def mm_tn(left, right):
    return lax.dot_general(
        left, right, (((0,), (0,)), ((), ())), preferred_element_type=jnp.float32
    )


def angle_tables(model_width):
    quarter = model_width // 4
    rate = np.exp(np.arange(quarter) * (-math.log(10000.0) / quarter))
    fine = np.arange(STEP)[:, None] * rate
    coarse = fine * STEP
    zero = np.zeros((STEP, 2 * quarter))
    table = np.concatenate(
        [
            np.concatenate([np.sin(coarse), np.cos(coarse), zero], axis=1),
            np.concatenate([zero, np.sin(fine), np.cos(fine)], axis=1),
        ],
        axis=0,
    )
    parts = []
    rest = table
    for _ in range(3):
        part = rest.astype(jnp.bfloat16)
        parts.append(part)
        rest = rest - part.astype(np.float64)
    return np.concatenate(parts, axis=0)


def sinusoid(coord, table_ref):
    quarter = table_ref.shape[1] // 4
    slot = lax.broadcasted_iota(jnp.int32, (2 * STEP, coord.shape[1]), 0)
    coarse = coord >> STEP_BITS
    fine = (coord & (STEP - 1)) + STEP
    hit = ((slot == coarse) | (slot == fine)).astype(jnp.float32).astype(jnp.bfloat16)
    looked = mm_tn(jnp.concatenate([hit, hit, hit], axis=0), table_ref[...])
    sin_a, cos_a, sin_b, cos_b = [looked[:, k * quarter : (k + 1) * quarter] for k in range(4)]
    return jnp.concatenate([sin_a * cos_b + cos_a * sin_b, cos_a * cos_b - sin_a * sin_b], axis=1)


def probs_t(q, k, pq, pk, length, factor):
    left = jnp.concatenate([k, pk, k], axis=0)
    right = jnp.concatenate([q, q, pq], axis=0)
    scores = mm_tn(left, right) * factor
    visible = lax.broadcasted_iota(jnp.int32, scores.shape, 0) < length
    scores = jnp.where(visible, scores, MASKED)
    raised = jnp.exp(scores - jnp.max(scores, axis=0, keepdims=True))
    return raised * (1.0 / jnp.sum(raised, axis=0, keepdims=True))


def rows_at(head):
    return pl.ds(pl.multiple_of(head * HEAD_DIM, HEAD_DIM), HEAD_DIM)


def attend_kernel(
    heads, scalars_ref, lengths_ref, x_ref, coords_ref, table_ref, wqkv_ref, wpos_ref,
    send_ref, own_ref, proj_ref, pos_ref,
):
    step = pl.program_id(0)
    length = lengths_ref[scalars_ref[0] ^ (1 - step)]
    factor = 1.0 / math.sqrt(3.0 * HEAD_DIM)
    rows = x_ref[0]
    for part in range(3):
        proj_ref[part] = mm_nt(wqkv_ref[part], rows).astype(jnp.bfloat16)
    sides = [sinusoid(coords_ref[0, axis : axis + 1], table_ref) for axis in range(2)]
    position = jnp.concatenate(sides, axis=1).astype(jnp.bfloat16)
    pos_ref[...] = position
    for part in range(2):
        proj_ref[3 + part] = mm_nt(wpos_ref[part], position).astype(jnp.bfloat16)

    def one_head(head, _):
        at = rows_at(head)
        q, k, v, pq, pk = [proj_ref[part, at] for part in range(5)]
        weights = probs_t(q, k, pq, pk, length, factor).astype(jnp.bfloat16)
        mixed = mm(v, weights).astype(jnp.bfloat16)

        @pl.when(step == 0)
        def _():
            send_ref[at] = mixed.astype(jnp.float32)

        @pl.when(step == 1)
        def _():
            own_ref[at] = mixed

        return 0

    lax.fori_loop(0, heads, one_head, 0, unroll=True)


def attend(scalars, lengths, tokens, coords, table, w_qkv, w_pos):
    pages, length, width = tokens.shape
    columns = w_qkv.shape[1]
    whole = lambda shape: pl.BlockSpec(shape, lambda i, s, n: (0,) * len(shape))
    shapes = (
        jax.ShapeDtypeStruct((columns, length), jnp.float32),
        jax.ShapeDtypeStruct((columns, length), jnp.bfloat16),
        jax.ShapeDtypeStruct((5, columns, length), jnp.bfloat16),
        jax.ShapeDtypeStruct((length, width), jnp.bfloat16),
    )
    page = lambda i, s, n: (s[0] ^ (1 - i), 0, 0)
    return pl.pallas_call(
        partial(attend_kernel, columns // HEAD_DIM),
        out_shape=shapes,
        grid_spec=pltpu.PrefetchScalarGridSpec(
            num_scalar_prefetch=2,
            grid=(pages,),
            in_specs=[
                pl.BlockSpec((1, length, width), page),
                pl.BlockSpec((1,) + coords.shape[1:], page),
                whole(table.shape),
                whole(w_qkv.shape),
                whole(w_pos.shape),
            ],
            out_specs=[whole(shape.shape) for shape in shapes],
        ),
        compiler_params=pltpu.CompilerParams(vmem_limit_bytes=40 << 20),
        cost_estimate=pl.CostEstimate(
            flops=2 * pages * length * columns * (5 * width + 4 * length),
            transcendentals=pages * length * length * columns // HEAD_DIM,
            bytes_accessed=pages * length * (4 * width + 14 * columns),
        ),
        name="attend",
    )(scalars, lengths, tokens, coords, table, w_qkv, w_pos)


def norm_parts(values):
    center = values - jnp.mean(values, axis=-1, keepdims=True)
    spread = jnp.mean(center * center, axis=-1, keepdims=True)
    scale = lax.rsqrt(spread + 1e-05)
    return center * scale, scale


def norm_back(grad, gain, xhat, scale):
    up = grad * gain
    mean = jnp.mean(up, axis=-1, keepdims=True)
    along = jnp.mean(up * xhat, axis=-1, keepdims=True)
    return scale * (up - mean - xhat * along)


def column_sum(values):
    return jnp.sum(values.astype(jnp.float32), axis=0, keepdims=True)


def feed_kernel(
    scalars_ref, x_ref, part_ref, other_ref, b_out_ref, gain_ref, shift_ref, w_in_ref, w_in_far_ref, b_in_ref,
    w_back_ref, w_back_far_ref, next_ref, xhat_ref, scale_ref, low_ref, hidden_ref, slope_ref,
):
    first = x_ref[0].astype(jnp.float32) + (part_ref[...] + other_ref[...] + b_out_ref[...])
    xhat, scale = norm_parts(first)
    low = (xhat * gain_ref[...] + shift_ref[...]).astype(jnp.bfloat16)
    xhat_ref[...] = xhat
    scale_ref[...] = scale
    low_ref[...] = low
    units = w_in_ref.shape[1]
    total = None
    for side, (into, back) in enumerate(((w_in_ref, w_back_ref), (w_in_far_ref, w_back_far_ref))):
        at = slice(side * units, (side + 1) * units)
        pre = mm(low, into[...]) + b_in_ref[side : side + 1]
        cdf = 0.5 * (1.0 + lax.erf(pre * math.sqrt(0.5)))
        hidden = (pre * cdf).astype(jnp.bfloat16)
        hidden_ref[:, at] = hidden
        slope_ref[:, at] = cdf + pre * (jnp.exp(-0.5 * pre * pre) * (1.0 / math.sqrt(2.0 * math.pi)))
        product = mm(hidden, back[...])
        total = product if total is None else total + product
    next_ref[...] = total


def feed_back_kernel(
    scalars_ref, cot_ref, part_ref, other_ref, xhat_ref, slope_ref, gain_one_ref, shift_one_ref, b_back_ref,
    gain_ref, shift_ref, w_in_ref, w_in_far_ref, w_back_ref, w_back_far_ref,
    next_ref, second_ref, feed_ref, pre_ref, out_ref, sums_ref, sums_in_ref,
):
    normed = xhat_ref[...] * gain_one_ref[...] + shift_one_ref[...]
    second = normed + (part_ref[...] + other_ref[...] + b_back_ref[...])
    xhat, scale = norm_parts(second)
    out_ref[...] = xhat * gain_ref[...] + shift_ref[...]
    grad = cot_ref[0].astype(jnp.float32)
    d_second = norm_back(grad, gain_ref[...], xhat, scale)
    second_ref[...] = d_second
    d_feed = d_second.astype(jnp.bfloat16)
    feed_ref[...] = d_feed
    sums_ref[0:1] = column_sum(d_feed)
    sums_ref[1:2] = column_sum(grad * xhat)
    sums_ref[2:3] = column_sum(grad)
    units = w_in_ref.shape[1]
    total = None
    for side, (into, back) in enumerate(((w_in_ref, w_back_ref), (w_in_far_ref, w_back_far_ref))):
        at = slice(side * units, (side + 1) * units)
        d_pre = (mm_nt(d_feed, back[...]) * slope_ref[:, at]).astype(jnp.bfloat16)
        pre_ref[:, at] = d_pre
        sums_in_ref[side : side + 1] = column_sum(d_pre)
        product = mm_nt(d_pre, into[...])
        total = product if total is None else total + product
    next_ref[...] = total


def on_chunk(kernel, name, chunk, scalars, pages_array, rows, arrays, shapes):
    length, width = pages_array.shape[1:]
    whole = lambda shape: pl.BlockSpec(shape, lambda i, s: (0,) * len(shape))
    return pl.pallas_call(
        kernel,
        out_shape=shapes,
        grid_spec=pltpu.PrefetchScalarGridSpec(
            num_scalar_prefetch=1,
            grid=(1,),
            in_specs=[pl.BlockSpec((1, rows, width), lambda i, s: (s[0], chunk, 0))]
            + [whole(array.shape) for array in arrays],
            out_specs=[whole(shape.shape) for shape in shapes],
        ),
        compiler_params=pltpu.CompilerParams(vmem_limit_bytes=48 << 20),
        cost_estimate=pl.CostEstimate(
            flops=16 * rows * width * width, transcendentals=2 * rows * width, bytes_accessed=40 * rows * width
        ),
        name=name,
    )(scalars, pages_array, *arrays)


def feed_grads_kernel(count, low_ref, pre_ref, hidden_ref, feed_ref, out_ref):
    rows = out_ref.shape[2]

    def put(left, right):
        product = mm_tn(left[...], right[...])
        for block in range(count):
            out_ref[block, 0] = product[block * rows : (block + 1) * rows]

    @pl.when(pl.program_id(0) % 2 == 0)
    def _():
        put(low_ref, pre_ref)

    @pl.when(pl.program_id(0) % 2 == 1)
    def _():
        put(hidden_ref, feed_ref)


def feed_grads(count, low, d_pre, hidden, d_feed):
    length, width = low.shape
    units = hidden.shape[1] // 2
    return pl.pallas_call(
        partial(feed_grads_kernel, count),
        out_shape=jax.ShapeDtypeStruct((count, 4, width // count, units), jnp.float32),
        grid_spec=pl.GridSpec(
            grid=(4,),
            in_specs=[
                pl.BlockSpec((length, width), lambda i: (0, 0)),
                pl.BlockSpec((length, units), lambda i: (0, i // 2)),
                pl.BlockSpec((length, units), lambda i: (0, i // 2)),
                pl.BlockSpec((length, width), lambda i: (0, 0)),
            ],
            out_specs=pl.BlockSpec((count, 1, width // count, units), lambda i: (0, i, 0, 0)),
        ),
        compiler_params=pltpu.CompilerParams(vmem_limit_bytes=40 << 20),
        cost_estimate=pl.CostEstimate(
            flops=8 * length * width * units, transcendentals=0, bytes_accessed=16 * width * units
        ),
        name="feed_grads",
    )(low, d_pre, hidden, d_feed)


def attend_back_kernel(
    heads, scalars_ref, lengths_ref, part_a, part_b, other_a, other_b, second_a, second_b, xhat_a, xhat_b,
    scale_a, scale_b, gain_ref, w_out_ref, w_out_far_ref, own_ref, wqkv_ref, blocks_ref, x_ref, pos_ref,
    send_ref, base_ref, d_ref, branch_ref, sums_ref, dm_ref, first_ref, proj_ref, wfar_ref,
):
    page, low = scalars_ref[0], scalars_ref[1]
    length = lengths_ref[page]
    factor = 1.0 / math.sqrt(3.0 * HEAD_DIM)
    columns = heads * HEAD_DIM
    half = part_a.shape[0]
    count, _, block_rows, _ = blocks_ref.shape
    for part in range(5):
        for block in range(count):
            at = slice(block * block_rows, (block + 1) * block_rows)
            wfar_ref[part, at] = blocks_ref[block, part]
        weight = wfar_ref[part].astype(jnp.bfloat16)
        left = x_ref if part < 3 else pos_ref
        proj_ref[part, columns:] = mm_nt(weight, left[...]).astype(jnp.bfloat16)
        proj_ref[part, :columns] = own_ref[part]
    sums = None
    chunks = ((part_a, other_a, second_a, xhat_a, scale_a), (part_b, other_b, second_b, xhat_b, scale_b))
    for index, (part, other, second, xhat, scale) in enumerate(chunks):
        at = slice(index * half, (index + 1) * half)
        d_normed = second[...] + (part[...] + other[...])
        d_first = norm_back(d_normed, gain_ref[...], xhat[...], scale[...])
        first_ref[at] = d_first
        d_branch = d_first.astype(jnp.bfloat16)
        branch_ref[at] = d_branch
        some = (column_sum(d_branch), column_sum(d_normed * xhat[...]), column_sum(d_normed))
        sums = some if sums is None else tuple(x + y for x, y in zip(sums, some))
        dm_ref[:columns, at] = mm_nt(w_out_ref[...], d_branch).astype(jnp.bfloat16)
        dm_ref[columns:, at] = mm_nt(w_out_far_ref[...], d_branch).astype(jnp.bfloat16)
    for index, value in enumerate(sums):
        sums_ref[index : index + 1] = value

    def one_head(head, _):
        at = rows_at(head)
        q, k, v, pq, pk = [proj_ref[part, at] for part in range(5)]
        dm = dm_ref[at]
        probs = probs_t(q, k, pq, pk, length, factor)
        weights = probs.astype(jnp.bfloat16)
        d_values = mm(weights, dm.T)
        d_probs = mm_tn(v, dm)
        inner = jnp.sum(d_probs * probs, axis=0, keepdims=True)
        d_scores = (probs * (d_probs - inner)).astype(jnp.bfloat16)
        by_queries = mm(d_scores, jnp.concatenate([q, pq], axis=0).T).T
        by_query, by_pos_query = by_queries[:HEAD_DIM], by_queries[HEAD_DIM:]
        by_keys = mm(jnp.concatenate([k, pk], axis=0), d_scores)
        by_key, by_pos_key = by_keys[:HEAD_DIM], by_keys[HEAD_DIM:]
        grads = (
            (by_key + by_pos_key) * factor,
            (by_query + by_pos_query) * factor,
            d_values.T,
            by_key * factor,
            by_query * factor,
        )
        for part, value in enumerate(grads):
            d_ref[part, at] = value.astype(jnp.bfloat16)
        return 0

    lax.fori_loop(0, 2 * heads, one_head, 0, unroll=2)
    for part in range(3):
        for side in range(2):
            at = slice(side * columns, (side + 1) * columns)
            weight = wqkv_ref[part] if side == 0 else wfar_ref[part].astype(jnp.bfloat16)
            first_ref_part = mm_tn(d_ref[part, at], weight)
            if part == side == 0:
                total = first_ref_part
            else:
                total = total + first_ref_part
    upper, lower = total[:half], total[half:]
    send_ref[...] = jnp.where(low == 0, lower, upper)
    base_ref[...] = jnp.where(low == 0, upper + first_ref[:half], lower + first_ref[half:])


def attend_back(scalars, lengths, arrays):
    proj = arrays[13]
    parts, columns, length = proj.shape
    half, width = arrays[0].shape
    heads = columns // HEAD_DIM
    whole = lambda shape: pl.BlockSpec(shape, lambda i, s, n: (0,) * len(shape))
    shapes = (
        jax.ShapeDtypeStruct((half, width), jnp.float32),
        jax.ShapeDtypeStruct((half, width), jnp.float32),
        jax.ShapeDtypeStruct((parts, 2 * columns, length), jnp.bfloat16),
        jax.ShapeDtypeStruct((length, width), jnp.bfloat16),
        jax.ShapeDtypeStruct((3, width), jnp.float32),
    )
    return pl.pallas_call(
        partial(attend_back_kernel, heads),
        out_shape=shapes,
        grid_spec=pltpu.PrefetchScalarGridSpec(
            num_scalar_prefetch=2,
            grid=(1,),
            in_specs=[whole(array.shape) for array in arrays],
            out_specs=[whole(shape.shape) for shape in shapes],
            scratch_shapes=[
                pltpu.VMEM((2 * columns, length), jnp.bfloat16),
                pltpu.VMEM((length, width), jnp.float32),
                pltpu.VMEM((parts, 2 * columns, length), jnp.bfloat16),
                pltpu.VMEM((parts, columns, width), jnp.float32),
            ],
        ),
        compiler_params=pltpu.CompilerParams(vmem_limit_bytes=52 << 20),
        cost_estimate=pl.CostEstimate(
            flops=2 * 2 * heads * length * length * HEAD_DIM * 9 + 20 * length * width * columns,
            transcendentals=2 * heads * length * length,
            bytes_accessed=40 * length * width,
        ),
        name="attend_back",
    )(scalars, lengths, *arrays)


def weight_grads_kernel(
    count, scalars_ref, x_ref, pos_ref, d_ref, db_ref, mixed_ref, far_ref, vec_ref, keep_ref, send_ref
):
    group = scalars_ref[0]
    columns = mixed_ref.shape[0]
    rows = columns // count
    odd = group & 1
    extra = vec_ref.shape[1]
    side_rows = 6 * rows + extra
    mixed = jnp.concatenate([mixed_ref[...], far_ref[...]], axis=0)
    rights = [x_ref] * 3 + [pos_ref] * 2 + [db_ref]

    def put(block, at, value):
        place = (block ^ group) >> 1

        @pl.when(odd == (block & 1))
        def _():
            keep_ref[place, at] = value

        @pl.when(odd != (block & 1))
        def _():
            send_ref[place, at] = value

    for part, right in enumerate(rights):
        product = mm(d_ref[part] if part < 5 else mixed, right[...])
        for block in range(count):
            for side in range(2):
                start = side * columns + block * rows
                at = side * side_rows + part * rows
                put(block, slice(at, at + rows), product[start : start + rows])
    for block in range(count):
        for side in range(2):
            at = slice(side * side_rows + 6 * rows, (side + 1) * side_rows)
            put(block, at, vec_ref[side] if block == 0 else jnp.zeros(vec_ref.shape[1:], jnp.float32))


def weight_grads(count, scalars, rows, pos_rows, d_heads, d_branch, mixed, mixed_far, vectors):
    length, width = rows.shape
    columns = mixed.shape[0]
    block = 2 * (6 * (columns // count) + vectors.shape[1])
    shape = jax.ShapeDtypeStruct((count // 2, block, width), jnp.float32)
    return pl.pallas_call(
        partial(weight_grads_kernel, count),
        out_shape=(shape, shape),
        in_specs=[pl.BlockSpec(memory_space=pltpu.SMEM)] + [pl.BlockSpec(memory_space=pltpu.VMEM)] * 7,
        out_specs=[pl.BlockSpec(memory_space=pltpu.VMEM)] * 2,
        compiler_params=pltpu.CompilerParams(vmem_limit_bytes=48 << 20),
        cost_estimate=pl.CostEstimate(
            flops=24 * length * width * columns,
            transcendentals=0,
            bytes_accessed=4 * count * block * width + 20 * length * columns + 6 * length * width,
        ),
        name="weight_grads",
    )(scalars, rows, pos_rows, d_heads, d_branch, mixed, mixed_far, vectors)


def place_grads_kernel(
    order, scalars_ref, low_a_ref, low_b_ref, high_a_ref, high_b_ref, qkv_ref, pos_ref, out_ref, vec_ref
):
    group = scalars_ref[0]
    count = 2 * low_a_ref.shape[0]
    rows = qkv_ref.shape[1] // count
    cut = low_a_ref.shape[1]

    def read(place, start, stop):
        upper = (place & 1) == 1
        index = place >> 1
        pieces = []
        if start < cut:
            at = slice(start, min(stop, cut))
            pieces.append(jnp.where(upper, high_a_ref[index, at], low_a_ref[index, at]))
        if stop > cut:
            at = slice(max(start, cut) - cut, stop - cut)
            turned_index = 0
            for bit in range(len(order)):
                turned_index = turned_index | (((index >> bit) & 1) << order[bit])
            pieces.append(jnp.where(upper, high_b_ref[turned_index, at], low_b_ref[turned_index, at]))
        return jnp.concatenate(pieces, axis=0) if len(pieces) > 1 else pieces[0]

    for block in range(count):
        place = block ^ group
        at = slice(block * rows, (block + 1) * rows)
        for part in range(6):
            value = read(place, part * rows, (part + 1) * rows)
            if part < 3:
                qkv_ref[part, at] = value
            elif part < 5:
                pos_ref[part - 3, at] = value
            else:
                out_ref[at] = value
        if block == 0:
            vec_ref[...] = read(place, 6 * rows, cut + low_b_ref.shape[1])


def place_grads(scalars, parts, columns, vec_rows):
    width = parts[0].shape[2]
    bits = parts[0].shape[0].bit_length() - 1
    whole = lambda shape: pl.BlockSpec(shape, lambda i: (0,) * len(shape))
    shapes = (
        jax.ShapeDtypeStruct((3, columns, width), jnp.float32),
        jax.ShapeDtypeStruct((2, columns, width), jnp.float32),
        jax.ShapeDtypeStruct((columns, width), jnp.float32),
        jax.ShapeDtypeStruct((vec_rows, width), jnp.float32),
    )
    return pl.pallas_call(
        partial(place_grads_kernel, tuple(range(bits))[::-1]),
        out_shape=shapes,
        grid_spec=pl.GridSpec(
            grid=(1,),
            in_specs=[pl.BlockSpec(memory_space=pltpu.SMEM)] + [whole(part.shape) for part in parts],
            out_specs=[whole(shape.shape) for shape in shapes],
        ),
        compiler_params=pltpu.CompilerParams(vmem_limit_bytes=40 << 20),
        cost_estimate=pl.CostEstimate(
            flops=0, transcendentals=0, bytes_accessed=32 * width * columns * 3
        ),
        name="place_grads",
    )(scalars, *parts)


def body(
    dp_size,
    mp_size,
    tokens,
    lengths,
    coords,
    w_qkv,
    w_pos,
    w_out,
    b_out,
    gain_one,
    shift_one,
    w_in,
    b_in,
    w_back,
    b_back,
    gain_two,
    shift_two,
    cotangent,
):
    pages, length, width = tokens.shape
    columns = w_qkv.shape[2]
    units = w_in.shape[1]
    here = lax.axis_index("mp")
    low = here & 1
    page = here >> 1
    group = lax.axis_index("dp")
    f32, bf16 = jnp.float32, jnp.bfloat16
    half = length // 2
    one = jnp.where(lengths[0] > 0, 1.0, 0.0).astype(f32)

    def arrived(value):
        return value * one

    def swap(value, bit):
        pairs = [(i, i ^ bit) for i in range(mp_size)]
        return lax.ppermute(value, "mp", pairs)

    def group_swap(value, bit):
        pairs = [(i, i ^ bit) for i in range(dp_size)]
        return lax.ppermute(value, "dp", pairs)

    def my_rows(value):
        rows = value.shape[0] // dp_size
        return lax.dynamic_slice_in_dim(value, group * rows, rows, 0)

    def gather(value):
        return lax.all_gather(value, "dp", axis=0, tiled=True)

    def take(value, index):
        return lax.dynamic_index_in_dim(value, index, 0, keepdims=False)

    def after(value, *others):
        return lax.optimization_barrier((value,) + others)[0]

    def row(value):
        return value.reshape(1, -1)

    chunk_rows = lambda value: [value[:half], value[half:]]

    turn = lambda value: jnp.swapaxes(value, 1, 2)
    w_qkv, w_pos = turn(w_qkv), turn(w_pos)
    out_rows = my_rows(w_out).astype(f32)
    out_rows = jnp.pad(out_rows, ((0, max(0, 48 - out_rows.shape[0])), (0, 0)))
    out_rows = swap(out_rows, FAR)
    unit_rows = jnp.concatenate([my_rows(w_in), my_rows(w_back)], axis=0).astype(f32)
    tail = jnp.concatenate([row(b_in), jnp.zeros((7, units), f32)], axis=0)
    far_rows = swap(jnp.concatenate([unit_rows, tail], axis=0), FAR)
    count = columns // dp_size
    w_out_far = gather(out_rows).reshape(dp_size, -1, width)[:, :count].reshape(columns, width)
    w_out_far = arrived(w_out_far).astype(bf16)

    table = jnp.asarray(angle_tables(width))
    scalars = jnp.stack([page, low])
    mixed_send, mixed, proj, pos_rows = attend(scalars, lengths, tokens, coords, table, w_qkv, w_pos)
    mixed_far = swap(mixed_send, FAR)
    far_rows = after(far_rows, mixed_far)
    count = unit_rows.shape[0]
    b_in_two = jnp.stack([b_in, far_rows[count]])
    blocks = arrived(gather(far_rows[:count])).reshape(dp_size, count, -1)
    in_rows = width // dp_size
    w_in_far = blocks[:, :in_rows].reshape(width, units).astype(bf16)
    w_back_far = blocks[:, in_rows:].reshape(units, width).astype(bf16)

    mixed_far = arrived(mixed_far).astype(bf16)
    chunk_columns = lambda value: [value[:, :half], value[:, half:]]
    part = [
        mm_tn(own, w_out) + mm_tn(far, w_out_far)
        for own, far in zip(chunk_columns(mixed), chunk_columns(mixed_far))
    ]
    other = [swap(value, NEAR) for value in part]
    head_rows = jnp.concatenate([w_qkv, w_pos], axis=0)
    count = columns // dp_size
    head_rows = lax.dynamic_slice_in_dim(after(head_rows, part[1]), group * count, count, 1)
    head_rows = swap(head_rows.astype(f32), FAR)
    part[0] = after(part[0], head_rows)

    rows_of = jax.ShapeDtypeStruct((half, width), f32)
    rows_low = jax.ShapeDtypeStruct((half, width), bf16)
    units_of = jax.ShapeDtypeStruct((half, 2 * units), f32)
    units_low = jax.ShapeDtypeStruct((half, 2 * units), bf16)
    scale_of = jax.ShapeDtypeStruct((half, 1), f32)
    fed = []
    for index in range(2):
        arrays = [part[index], other[index], row(b_out), row(gain_one), row(shift_one)]
        arrays += [w_in, w_in_far, b_in_two, w_back, w_back_far]
        shapes = (rows_of, rows_of, scale_of, rows_low, units_low, units_of)
        fed.append(
            on_chunk(feed_kernel, "feed", index, scalars, tokens, half, arrays, shapes)
        )
    part = [value[0] for value in fed]
    other = [swap(value, NEAR) for value in part]
    blocks = gather(head_rows.reshape(-1, width)).reshape(dp_size, 5, count, width)
    back = []
    for index in range(2):
        arrays = [part[index], other[index], fed[index][1], fed[index][5], row(gain_one), row(shift_one)]
        arrays += [row(b_back), row(gain_two), row(shift_two), w_in, w_in_far, w_back, w_back_far]
        shapes = (rows_of, rows_of, rows_low, units_low, rows_of)
        shapes += (jax.ShapeDtypeStruct((3, width), f32), jax.ShapeDtypeStruct((2, units), f32))
        back.append(
            on_chunk(feed_back_kernel, "feed_back", index, scalars, cotangent, half, arrays, shapes)
        )
    part = [value[0] for value in back]
    other = [swap(value, NEAR) for value in part]

    both = lambda index, source: jnp.concatenate([source[0][index], source[1][index]], axis=0)
    d_feed = after(both(2, back), part[1])
    ffn = feed_grads(dp_size, both(3, fed), both(3, back), both(4, fed), d_feed)
    ffn = lax.psum_scatter(ffn.reshape(-1, units), "dp", scatter_dimension=0, tiled=True)

    rows = take(tokens, page)
    arrays = part + other + [back[0][1], back[1][1], fed[0][1], fed[1][1], fed[0][2], fed[1][2]]
    arrays += [row(gain_one), w_out, w_out_far]
    arrays += [proj, w_qkv, blocks, rows, pos_rows]
    send, base, d_heads, d_branch, sums = attend_back(scalars, lengths, arrays)

    def spread(mine, far, rest):
        both = jnp.stack([mine, far])
        out = jnp.stack([jnp.where(low == 0, both, rest), jnp.where(low == 0, rest, both)], axis=1)
        out = out.reshape(pages, length, width)
        return jnp.where(page == 0, out, out[::-1])

    out_mine = jnp.where(low == 0, back[0][4], back[1][4])
    out_far = swap(after(out_mine, other[1]), FAR)

    bits = [1 << k for k in range(dp_size.bit_length() - 1)]
    near_sum = swap(send, NEAR)
    vectors = jnp.concatenate([sums, back[0][5] + back[1][5]], axis=0)
    d_b_in = back[0][6] + back[1][6]
    spare = jnp.zeros((8 - vectors.shape[0] - 1, width), f32)
    vectors = jnp.stack(
        [jnp.concatenate([vectors, d_b_in[side : side + 1], spare], axis=0) for side in range(2)]
    )
    scalars = jnp.reshape(group, (1,))
    keep, give = weight_grads(
        dp_size, scalars, rows, pos_rows, d_heads, d_branch, mixed, mixed_far, vectors
    )
    total = keep + group_swap(give, bits[0])

    mine = base + near_sum
    mine = after(mine, out_far)
    far_mine = swap(mine, FAR)
    more = bits[1:]

    def fold_two(upper, lower):
        for step in range(len(more)):
            upper = upper.reshape((-1, 2) + upper.shape[1:])
            lower = lower.reshape((2, -1) + lower.shape[1:])
            give_upper, give_lower = after_all(upper[:, 1], lower[1])
            upper = upper[:, 0] + group_swap(give_upper, more[step])
            lower = lower[0] + group_swap(give_lower, more[-1 - step])
        return upper[0], lower[0]

    def after_all(*values):
        return lax.optimization_barrier(values)

    cut = total.shape[1] // 2
    upper, lower = fold_two(total[:, :cut], total[:, cut:])
    far_sum = swap(lower, FAR)

    rest = swap(jnp.stack([mine, far_mine, out_far]), NEAR)
    grad_tokens = spread(mine, far_mine, rest[:2])
    out_rest = jnp.where(low == 0, back[1][4], back[0][4])
    layer_out = spread(out_mine, arrived(out_far), jnp.stack([out_rest, arrived(rest[2])])).astype(bf16)
    total = upper + far_sum
    cut = total.shape[0] // 16 * 8
    upper, lower = total[None, :cut], total[None, cut:]
    for step in range(len(more)):
        got_upper = group_swap(upper, more[step])
        got_lower = group_swap(lower, more[-1 - step])
        upper = jnp.concatenate([upper, got_upper], axis=0)
        lower = jnp.concatenate([lower, got_lower], axis=0)
    parts = [upper, lower, group_swap(upper, bits[0]), group_swap(lower, bits[0])]
    grad_w_qkv, grad_w_pos, grad_w_out, vectors = place_grads(scalars, parts, columns, 8)
    grad_w_qkv, grad_w_pos = turn(grad_w_qkv), turn(grad_w_pos)
    grad_b_out, grad_gain_one, grad_shift_one = vectors[0], vectors[1], vectors[2]
    grad_b_back, grad_gain_two, grad_shift_two = vectors[3], vectors[4], vectors[5]
    grad_b_in = vectors[6]

    ffn = after(ffn, mine)
    count = ffn.shape[0] // 2
    ffn = ffn[:count] + swap(ffn[count:], FAR)
    grad_w_in = gather(ffn[:in_rows])
    grad_w_back = gather(ffn[in_rows:])
    return (
        layer_out,
        grad_tokens,
        grad_w_qkv,
        grad_w_pos,
        grad_w_out,
        grad_b_out,
        grad_gain_one,
        grad_shift_one,
        grad_w_in,
        grad_b_in,
        grad_w_back,
        grad_b_back,
        grad_gain_two,
        grad_shift_two,
    )


def solution(mesh):
    placed = (
        P("dp", None, None),
        P("dp"),
        P("dp", None, None),
        P(None, None, "mp"),
        P(None, None, "mp"),
        P("mp", None),
        P(),
        P(),
        P(),
        P(None, "mp"),
        P("mp"),
        P("mp", None),
        P(),
        P(),
        P(),
        P("dp", None, None),
    )
    return jax.shard_map(
        partial(body, mesh.shape["dp"], mesh.shape["mp"]),
        mesh=mesh,
        in_specs=placed,
        out_specs=(
            P("dp", None, None),
            P("dp", None, None),
            P(None, None, "mp"),
            P(None, None, "mp"),
            P("mp", None),
            P(),
            P(),
            P(),
            P(None, "mp"),
            P("mp"),
            P("mp", None),
            P(),
            P(),
            P(),
        ),
        check_vma=False,
    )
```

```python
from functools import partial
import math

import jax
import jax.numpy as jnp
import numpy as np
from jax import lax
from jax.experimental import pallas as pl
from jax.experimental.pallas import tpu as pltpu
from jax.sharding import PartitionSpec as P

HEAD_DIM = 64
STEP_BITS = 5
STEP = 1 << STEP_BITS
NEAR = 1
MP = ("far", "near")
FAR = 2
MASKED = -1e30


def mm(left, right):
    return jnp.dot(left, right, preferred_element_type=jnp.float32)


def mm_nt(left, right):
    return lax.dot_general(
        left, right, (((1,), (1,)), ((), ())), preferred_element_type=jnp.float32
    )


def mm_tn(left, right):
    return lax.dot_general(
        left, right, (((0,), (0,)), ((), ())), preferred_element_type=jnp.float32
    )


def angle_tables(model_width):
    quarter = model_width // 4
    rate = np.exp(np.arange(quarter) * (-math.log(10000.0) / quarter))
    fine = np.arange(STEP)[:, None] * rate
    coarse = fine * STEP
    zero = np.zeros((STEP, 2 * quarter))
    table = np.concatenate(
        [
            np.concatenate([np.sin(coarse), np.cos(coarse), zero], axis=1),
            np.concatenate([zero, np.sin(fine), np.cos(fine)], axis=1),
        ],
        axis=0,
    )
    parts = []
    rest = table
    for _ in range(3):
        part = rest.astype(jnp.bfloat16)
        parts.append(part)
        rest = rest - part.astype(np.float64)
    return np.concatenate(parts, axis=0)


def sinusoid(coord, table_ref):
    quarter = table_ref.shape[1] // 4
    slot = lax.broadcasted_iota(jnp.int32, (2 * STEP, coord.shape[1]), 0)
    coarse = coord >> STEP_BITS
    fine = (coord & (STEP - 1)) + STEP
    hit = ((slot == coarse) | (slot == fine)).astype(jnp.float32).astype(jnp.bfloat16)
    looked = mm_tn(jnp.concatenate([hit, hit, hit], axis=0), table_ref[...])
    sin_a, cos_a, sin_b, cos_b = [looked[:, k * quarter : (k + 1) * quarter] for k in range(4)]
    return jnp.concatenate([sin_a * cos_b + cos_a * sin_b, cos_a * cos_b - sin_a * sin_b], axis=1)


def probs_t(q, k, pq, pk, length, factor):
    left = jnp.concatenate([k, pk, k], axis=0)
    right = jnp.concatenate([q, q, pq], axis=0)
    scores = mm_tn(left, right) * factor
    visible = lax.broadcasted_iota(jnp.int32, scores.shape, 0) < length
    scores = jnp.where(visible, scores, MASKED)
    raised = jnp.exp(scores - jnp.max(scores, axis=0, keepdims=True))
    return raised * (1.0 / jnp.sum(raised, axis=0, keepdims=True))


def rows_at(head):
    return pl.ds(pl.multiple_of(head * HEAD_DIM, HEAD_DIM), HEAD_DIM)


def attend_kernel(
    heads, scalars_ref, lengths_ref, x_ref, coords_ref, table_ref, wqkv_ref, wpos_ref,
    send_ref, own_ref, proj_ref, pos_ref,
):
    step = pl.program_id(0)
    length = lengths_ref[scalars_ref[0] ^ (1 - step)]
    factor = 1.0 / math.sqrt(3.0 * HEAD_DIM)
    rows = x_ref[0]
    for part in range(3):
        proj_ref[part] = mm_nt(wqkv_ref[part], rows).astype(jnp.bfloat16)
    sides = [sinusoid(coords_ref[0, axis : axis + 1], table_ref) for axis in range(2)]
    position = jnp.concatenate(sides, axis=1).astype(jnp.bfloat16)
    pos_ref[...] = position
    for part in range(2):
        proj_ref[3 + part] = mm_nt(wpos_ref[part], position).astype(jnp.bfloat16)

    def one_head(head, _):
        at = rows_at(head)
        q, k, v, pq, pk = [proj_ref[part, at] for part in range(5)]
        weights = probs_t(q, k, pq, pk, length, factor).astype(jnp.bfloat16)
        mixed = mm(v, weights).astype(jnp.bfloat16)

        @pl.when(step == 0)
        def _():
            send_ref[at] = mixed.astype(jnp.float32)

        @pl.when(step == 1)
        def _():
            own_ref[at] = mixed

        return 0

    lax.fori_loop(0, heads, one_head, 0, unroll=True)


def attend(scalars, lengths, tokens, coords, table, w_qkv, w_pos):
    pages, length, width = tokens.shape
    columns = w_qkv.shape[1]
    whole = lambda shape: pl.BlockSpec(shape, lambda i, s, n: (0,) * len(shape))
    shapes = (
        jax.ShapeDtypeStruct((columns, length), jnp.float32),
        jax.ShapeDtypeStruct((columns, length), jnp.bfloat16),
        jax.ShapeDtypeStruct((5, columns, length), jnp.bfloat16),
        jax.ShapeDtypeStruct((length, width), jnp.bfloat16),
    )
    page = lambda i, s, n: (s[0] ^ (1 - i), 0, 0)
    return pl.pallas_call(
        partial(attend_kernel, columns // HEAD_DIM),
        out_shape=shapes,
        grid_spec=pltpu.PrefetchScalarGridSpec(
            num_scalar_prefetch=2,
            grid=(pages,),
            in_specs=[
                pl.BlockSpec((1, length, width), page),
                pl.BlockSpec((1,) + coords.shape[1:], page),
                whole(table.shape),
                whole(w_qkv.shape),
                whole(w_pos.shape),
            ],
            out_specs=[whole(shape.shape) for shape in shapes],
        ),
        compiler_params=pltpu.CompilerParams(vmem_limit_bytes=40 << 20),
        cost_estimate=pl.CostEstimate(
            flops=2 * pages * length * columns * (5 * width + 4 * length),
            transcendentals=pages * length * length * columns // HEAD_DIM,
            bytes_accessed=pages * length * (4 * width + 14 * columns),
        ),
        name="attend",
    )(scalars, lengths, tokens, coords, table, w_qkv, w_pos)


def norm_parts(values):
    center = values - jnp.mean(values, axis=-1, keepdims=True)
    spread = jnp.mean(center * center, axis=-1, keepdims=True)
    scale = lax.rsqrt(spread + 1e-05)
    return center * scale, scale


def norm_back(grad, gain, xhat, scale):
    up = grad * gain
    mean = jnp.mean(up, axis=-1, keepdims=True)
    along = jnp.mean(up * xhat, axis=-1, keepdims=True)
    return scale * (up - mean - xhat * along)


def column_sum(values):
    return jnp.sum(values.astype(jnp.float32), axis=0, keepdims=True)


def feed_kernel(
    scalars_ref, x_ref, part_ref, other_ref, b_out_ref, gain_ref, shift_ref, w_in_ref, w_in_far_ref, b_in_ref,
    w_back_ref, w_back_far_ref, xhat_ref, scale_ref, low_ref, hidden_ref, slope_ref, next_ref,
):
    first = x_ref[0].astype(jnp.float32) + (part_ref[...] + other_ref[...] + b_out_ref[...])
    xhat, scale = norm_parts(first)
    low = (xhat * gain_ref[...] + shift_ref[...]).astype(jnp.bfloat16)
    xhat_ref[...] = xhat
    scale_ref[...] = scale
    low_ref[...] = low
    units = w_in_ref.shape[1]
    total = None
    for side, (into, back) in enumerate(((w_in_ref, w_back_ref), (w_in_far_ref, w_back_far_ref))):
        at = slice(side * units, (side + 1) * units)
        pre = mm(low, into[...]) + b_in_ref[side : side + 1]
        cdf = 0.5 * (1.0 + lax.erf(pre * math.sqrt(0.5)))
        hidden = (pre * cdf).astype(jnp.bfloat16)
        hidden_ref[:, at] = hidden
        slope_ref[:, at] = cdf + pre * (jnp.exp(-0.5 * pre * pre) * (1.0 / math.sqrt(2.0 * math.pi)))
        product = mm(hidden, back[...])
        total = product if total is None else total + product
    next_ref[...] = total


def feed_back_kernel(
    scalars_ref, cot_ref, part_ref, other_ref, xhat_ref, slope_ref, gain_one_ref, shift_one_ref, b_back_ref,
    gain_ref, shift_ref, w_in_ref, w_in_far_ref, w_back_ref, w_back_far_ref,
    next_ref, second_ref, feed_ref, pre_ref, out_ref, sums_ref, sums_in_ref,
):
    normed = xhat_ref[...] * gain_one_ref[...] + shift_one_ref[...]
    second = normed + (part_ref[...] + other_ref[...] + b_back_ref[...])
    xhat, scale = norm_parts(second)
    out_ref[...] = xhat * gain_ref[...] + shift_ref[...]
    grad = cot_ref[0].astype(jnp.float32)
    d_second = norm_back(grad, gain_ref[...], xhat, scale)
    second_ref[...] = d_second
    d_feed = d_second.astype(jnp.bfloat16)
    feed_ref[...] = d_feed
    sums_ref[0:1] = column_sum(d_feed)
    sums_ref[1:2] = column_sum(grad * xhat)
    sums_ref[2:3] = column_sum(grad)
    units = w_in_ref.shape[1]
    total = None
    for side, (into, back) in enumerate(((w_in_ref, w_back_ref), (w_in_far_ref, w_back_far_ref))):
        at = slice(side * units, (side + 1) * units)
        d_pre = (mm_nt(d_feed, back[...]) * slope_ref[:, at]).astype(jnp.bfloat16)
        pre_ref[:, at] = d_pre
        sums_in_ref[side : side + 1] = column_sum(d_pre)
        product = mm_nt(d_pre, into[...])
        total = product if total is None else total + product
    next_ref[...] = total


def without(kernel, first, count):
    def call(*refs):
        return kernel(*refs[:first], *refs[first + count :])

    return call


def on_chunk(kernel, name, chunk, scalars, pages_array, rows, arrays, shapes, before=()):
    length, width = pages_array.shape[1:]

    def rows_of(array):
        if array.shape[0] == length and len(array.shape) == 2:
            return pl.BlockSpec((rows, array.shape[1]), lambda i, s: (chunk, 0))
        return pl.BlockSpec(array.shape, lambda i, s: (0,) * len(array.shape))

    inputs = 2 + len(arrays)
    return pl.pallas_call(
        without(kernel, inputs, len(before)),
        out_shape=shapes,
        grid_spec=pltpu.PrefetchScalarGridSpec(
            num_scalar_prefetch=1,
            grid=(1,),
            in_specs=[pl.BlockSpec((1, rows, width), lambda i, s: (s[0], chunk, 0))]
            + [rows_of(array) for array in arrays]
            + [pl.BlockSpec(memory_space=pl.ANY)] * len(before),
            out_specs=[rows_of(shape) for shape in shapes],
        ),
        input_output_aliases={inputs + index: index for index in range(len(before))},
        compiler_params=pltpu.CompilerParams(vmem_limit_bytes=48 << 20),
        cost_estimate=pl.CostEstimate(
            flops=16 * rows * width * width, transcendentals=2 * rows * width, bytes_accessed=40 * rows * width
        ),
        name=name,
    )(scalars, pages_array, *arrays, *before)


def feed_grads_kernel(count, low_ref, pre_ref, hidden_ref, feed_ref, out_ref):
    rows = out_ref.shape[2]

    def put(left, right):
        product = mm_tn(left[...], right[...])
        for block in range(count):
            out_ref[block, 0] = product[block * rows : (block + 1) * rows]

    @pl.when(pl.program_id(0) % 2 == 0)
    def _():
        put(low_ref, pre_ref)

    @pl.when(pl.program_id(0) % 2 == 1)
    def _():
        put(hidden_ref, feed_ref)


def feed_grads(count, low, d_pre, hidden, d_feed):
    length, width = low.shape
    units = hidden.shape[1] // 2
    return pl.pallas_call(
        partial(feed_grads_kernel, count),
        out_shape=pltpu.HBM((count, 4, width // count, units), jnp.float32),
        grid_spec=pl.GridSpec(
            grid=(4,),
            in_specs=[
                pl.BlockSpec((length, width), lambda i: (0, 0)),
                pl.BlockSpec((length, units), lambda i: (0, i // 2)),
                pl.BlockSpec((length, units), lambda i: (0, i // 2)),
                pl.BlockSpec((length, width), lambda i: (0, 0)),
            ],
            out_specs=pl.BlockSpec((count, 1, width // count, units), lambda i: (0, i, 0, 0)),
        ),
        compiler_params=pltpu.CompilerParams(vmem_limit_bytes=40 << 20),
        cost_estimate=pl.CostEstimate(
            flops=8 * length * width * units, transcendentals=0, bytes_accessed=16 * width * units
        ),
        name="feed_grads",
    )(low, d_pre, hidden, d_feed)


def weight_grads(count, group, x_ref, pos_ref, d_ref, db_ref, mixed_ref, far_ref, vec_ref, keep_ref, send_ref):
    columns = mixed_ref.shape[0]
    rows = columns // count
    odd = group & 1
    extra = vec_ref.shape[1]
    side_rows = 6 * rows + extra
    mixed = jnp.concatenate([mixed_ref[...], far_ref[...]], axis=0)
    rights = [x_ref] * 3 + [pos_ref] * 2 + [db_ref]

    def put(block, at, value):
        place = (block ^ group) >> 1

        @pl.when(odd == (block & 1))
        def _():
            keep_ref[place, at] = value

        @pl.when(odd != (block & 1))
        def _():
            send_ref[place, at] = value

    for part, right in enumerate(rights):
        product = mm(d_ref[part] if part < 5 else mixed, right[...])
        for block in range(count):
            for side in range(2):
                start = side * columns + block * rows
                at = side * side_rows + part * rows
                put(block, slice(at, at + rows), product[start : start + rows])
    for block in range(count):
        for side in range(2):
            at = slice(side * side_rows + 6 * rows, (side + 1) * side_rows)
            put(block, at, vec_ref[side] if block == 0 else jnp.zeros(vec_ref.shape[1:], jnp.float32))


def attend_back_kernel(
    heads, count, scalars_ref, lengths_ref, part_ref, other_ref, second_ref, xhat_ref, scale_ref, gain_ref, w_out_ref, w_out_far_ref, own_ref, wqkv_ref, blocks_ref, x_ref, pos_ref, mixed_ref, mixed_far_ref, more_ref,
    send_ref, base_ref, keep_ref, give_ref, d_ref, branch_ref, dm_ref, first_ref, proj_ref, wfar_ref, vec_ref,
):
    page, low = scalars_ref[0], scalars_ref[1]
    length = lengths_ref[page]
    factor = 1.0 / math.sqrt(3.0 * HEAD_DIM)
    columns = heads * HEAD_DIM
    half = part_ref.shape[0] // 2
    block_rows = blocks_ref.shape[3]
    for part in range(5):
        for block in range(count):
            at = slice(block * block_rows, (block + 1) * block_rows)
            wfar_ref[part, at] = blocks_ref[0, block, part]
        weight = wfar_ref[part].astype(jnp.bfloat16)
        left = x_ref if part < 3 else pos_ref
        proj_ref[part, columns:] = mm_nt(weight, left[...]).astype(jnp.bfloat16)
        proj_ref[part, :columns] = own_ref[part]
    sums = None
    for index in range(2):
        at = slice(index * half, (index + 1) * half)
        xhat = xhat_ref[at]
        d_normed = second_ref[at] + (part_ref[at] + other_ref[at])
        d_first = norm_back(d_normed, gain_ref[...], xhat, scale_ref[at])
        first_ref[at] = d_first
        d_branch = d_first.astype(jnp.bfloat16)
        branch_ref[at] = d_branch
        some = (column_sum(d_branch), column_sum(d_normed * xhat), column_sum(d_normed))
        sums = some if sums is None else tuple(x + y for x, y in zip(sums, some))
        dm_ref[:columns, at] = mm_nt(w_out_ref[...], d_branch).astype(jnp.bfloat16)
        dm_ref[columns:, at] = mm_nt(w_out_far_ref[...], d_branch).astype(jnp.bfloat16)
    for side in range(2):
        for index, value in enumerate(sums):
            vec_ref[side, index : index + 1] = value
        vec_ref[side, len(sums) :] = more_ref[side]

    def one_head(head, _):
        at = rows_at(head)
        q, k, v, pq, pk = [proj_ref[part, at] for part in range(5)]
        dm = dm_ref[at]
        probs = probs_t(q, k, pq, pk, length, factor)
        weights = probs.astype(jnp.bfloat16)
        d_values = mm(weights, dm.T)
        d_probs = mm_tn(v, dm)
        inner = jnp.sum(d_probs * probs, axis=0, keepdims=True)
        d_scores = (probs * (d_probs - inner)).astype(jnp.bfloat16)
        by_queries = mm(d_scores, jnp.concatenate([q, pq], axis=0).T).T
        by_query, by_pos_query = by_queries[:HEAD_DIM], by_queries[HEAD_DIM:]
        by_keys = mm(jnp.concatenate([k, pk], axis=0), d_scores)
        by_key, by_pos_key = by_keys[:HEAD_DIM], by_keys[HEAD_DIM:]
        grads = (
            (by_key + by_pos_key) * factor,
            (by_query + by_pos_query) * factor,
            d_values.T,
            by_key * factor,
            by_query * factor,
        )
        for part, value in enumerate(grads):
            d_ref[part, at] = value.astype(jnp.bfloat16)
        return 0

    lax.fori_loop(0, 2 * heads, one_head, 0, unroll=2)
    for part in range(3):
        for side in range(2):
            at = slice(side * columns, (side + 1) * columns)
            weight = wqkv_ref[part] if side == 0 else wfar_ref[part].astype(jnp.bfloat16)
            first_ref_part = mm_tn(d_ref[part, at], weight)
            if part == side == 0:
                total = first_ref_part
            else:
                total = total + first_ref_part
    upper, lower = total[:half], total[half:]
    send_ref[...] = jnp.where(low == 0, lower, upper)
    base_ref[...] = jnp.where(low == 0, upper + first_ref[:half], lower + first_ref[half:])
    weight_grads(
        count, scalars_ref[2], x_ref, pos_ref, d_ref, branch_ref, mixed_ref, mixed_far_ref, vec_ref, keep_ref, give_ref
    )


def attend_back(count, scalars, lengths, arrays):
    proj = arrays[8]
    parts, columns, length = proj.shape
    half, width = length // 2, arrays[0].shape[1]
    heads = columns // HEAD_DIM
    whole = lambda shape: pl.BlockSpec(shape, lambda i, s, n: (0,) * len(shape))
    shapes = (
        jax.ShapeDtypeStruct((half, width), jnp.float32),
        jax.ShapeDtypeStruct((half, width), jnp.float32),
    ) + 2 * (jax.ShapeDtypeStruct((count // 2, 2 * (6 * (columns // count) + 8), width), jnp.float32),)
    return pl.pallas_call(
        partial(attend_back_kernel, heads, count),
        out_shape=shapes,
        grid_spec=pltpu.PrefetchScalarGridSpec(
            num_scalar_prefetch=2,
            grid=(1,),
            in_specs=[
                whole(array.shape)
                if len(array.shape) < 5
                else pl.BlockSpec((1,) + array.shape[1:], lambda i, s, n: (0, 0, 0, 0, 0))
                for array in arrays
            ],
            out_specs=[whole(shape.shape) for shape in shapes],
            scratch_shapes=[
                pltpu.VMEM((parts, 2 * columns, length), jnp.bfloat16),
                pltpu.VMEM((length, width), jnp.bfloat16),
                pltpu.VMEM((2 * columns, length), jnp.bfloat16),
                pltpu.VMEM((length, width), jnp.float32),
                pltpu.VMEM((parts, 2 * columns, length), jnp.bfloat16),
                pltpu.VMEM((parts, columns, width), jnp.float32),
                pltpu.VMEM((2, 8, width), jnp.float32),
            ],
        ),
        compiler_params=pltpu.CompilerParams(vmem_limit_bytes=58 << 20),
        cost_estimate=pl.CostEstimate(
            flops=2 * 2 * heads * length * length * HEAD_DIM * 9 + 20 * length * width * columns,
            transcendentals=2 * heads * length * length,
            bytes_accessed=40 * length * width,
        ),
        name="attend_back",
    )(scalars, lengths, *arrays)


def place_grads_kernel(
    order, scalars_ref, low_a_ref, low_b_ref, high_a_ref, high_b_ref, qkv_ref, pos_ref, out_ref, vec_ref
):
    group = scalars_ref[0]
    count = 2 * low_a_ref.shape[0]
    rows = qkv_ref.shape[1] // count
    cut = low_a_ref.shape[1]

    def read(place, start, stop):
        upper = (place & 1) == 1
        index = place >> 1
        pieces = []
        if start < cut:
            at = slice(start, min(stop, cut))
            pieces.append(jnp.where(upper, high_a_ref[index, at], low_a_ref[index, at]))
        if stop > cut:
            at = slice(max(start, cut) - cut, stop - cut)
            turned_index = 0
            for bit in range(len(order)):
                turned_index = turned_index | (((index >> bit) & 1) << order[bit])
            pieces.append(jnp.where(upper, high_b_ref[turned_index, at], low_b_ref[turned_index, at]))
        return jnp.concatenate(pieces, axis=0) if len(pieces) > 1 else pieces[0]

    for block in range(count):
        place = block ^ group
        at = slice(block * rows, (block + 1) * rows)
        for part in range(6):
            value = read(place, part * rows, (part + 1) * rows)
            if part < 3:
                qkv_ref[part, at] = value
            elif part < 5:
                pos_ref[part - 3, at] = value
            else:
                out_ref[at] = value
        if block == 0:
            vec_ref[...] = read(place, 6 * rows, cut + low_b_ref.shape[1])


def place_grads(scalars, parts, columns, vec_rows):
    width = parts[0].shape[2]
    bits = parts[0].shape[0].bit_length() - 1
    whole = lambda shape: pl.BlockSpec(shape, lambda i: (0,) * len(shape))
    shapes = (
        jax.ShapeDtypeStruct((3, columns, width), jnp.float32),
        jax.ShapeDtypeStruct((2, columns, width), jnp.float32),
        jax.ShapeDtypeStruct((columns, width), jnp.float32),
        jax.ShapeDtypeStruct((vec_rows, width), jnp.float32),
    )
    return pl.pallas_call(
        partial(place_grads_kernel, tuple(range(bits))[::-1]),
        out_shape=shapes,
        grid_spec=pl.GridSpec(
            grid=(1,),
            in_specs=[pl.BlockSpec(memory_space=pltpu.SMEM)] + [whole(part.shape) for part in parts],
            out_specs=[whole(shape.shape) for shape in shapes],
        ),
        compiler_params=pltpu.CompilerParams(vmem_limit_bytes=40 << 20),
        cost_estimate=pl.CostEstimate(
            flops=0, transcendentals=0, bytes_accessed=32 * width * columns * 3
        ),
        name="place_grads",
    )(scalars, *parts)


def body(
    dp_size,
    mp_size,
    tokens,
    lengths,
    coords,
    w_qkv,
    w_pos,
    w_out,
    b_out,
    gain_one,
    shift_one,
    w_in,
    b_in,
    w_back,
    b_back,
    gain_two,
    shift_two,
    cotangent,
):
    pages, length, width = tokens.shape
    columns = w_qkv.shape[2]
    units = w_in.shape[1]
    here = lax.axis_index(MP)
    low = here & 1
    page = here >> 1
    group = lax.axis_index("dp")
    f32, bf16 = jnp.float32, jnp.bfloat16
    half = length // 2
    one = jnp.where(lengths[0] > 0, 1.0, 0.0).astype(f32)

    def arrived(value):
        return value * one

    def swap(value, bit):
        pairs = [(i, i ^ bit) for i in range(mp_size)]
        return lax.ppermute(value, MP, pairs)

    def group_swap(value, bit):
        pairs = [(i, i ^ bit) for i in range(dp_size)]
        return lax.ppermute(value, "dp", pairs)

    def my_rows(value):
        rows = value.shape[0] // dp_size
        return lax.dynamic_slice_in_dim(value, group * rows, rows, 0)

    def gather(value):
        return lax.all_gather(value, "dp", axis=0, tiled=True)

    def take(value, index):
        return lax.dynamic_index_in_dim(value, index, 0, keepdims=False)

    def after(value, *others):
        return lax.optimization_barrier((value,) + others)[0]

    def row(value):
        return value.reshape(1, -1)

    chunk_rows = lambda value: [value[:half], value[half:]]

    turn = lambda value: jnp.swapaxes(value, 1, 2)
    w_qkv, w_pos = turn(w_qkv), turn(w_pos)
    out_rows = swap(my_rows(w_out).astype(f32), FAR)
    out_rows = jnp.pad(out_rows, ((0, max(0, 48 - out_rows.shape[0])), (0, 0)))
    unit_rows = jnp.concatenate([my_rows(w_in), my_rows(w_back)], axis=0).astype(f32)
    tail = jnp.concatenate([row(b_in), jnp.zeros((7, units), f32)], axis=0)
    far_rows = swap(jnp.concatenate([unit_rows, tail], axis=0), FAR)
    count = columns // dp_size

    table = jnp.asarray(angle_tables(width))
    scalars = jnp.stack([page, low])
    mixed_send, mixed, proj, pos_rows = attend(scalars, lengths, tokens, coords, table, w_qkv, w_pos)
    w_out_far = gather(out_rows).reshape(dp_size, -1, width)[:, : columns // dp_size]
    w_out_far = arrived(w_out_far.reshape(columns, width)).astype(bf16)
    mixed_far = swap(mixed_send, FAR)
    far_rows = after(far_rows, mixed_far)
    count = unit_rows.shape[0]
    b_in_two = jnp.stack([b_in, far_rows[count]])
    blocks = arrived(gather(far_rows[:count])).reshape(dp_size, count, -1)
    in_rows = width // dp_size
    w_in_far = blocks[:, :in_rows].reshape(width, units).astype(bf16)
    w_back_far = blocks[:, in_rows:].reshape(units, width).astype(bf16)

    mixed_far = arrived(mixed_far).astype(bf16)
    part = mm_tn(jnp.concatenate([mixed, mixed_far], axis=0), jnp.concatenate([w_out, w_out_far], axis=0))
    other = swap(part, NEAR)
    head_rows = jnp.concatenate([w_qkv, w_pos], axis=0)
    count = columns // dp_size
    head_rows = lax.dynamic_slice_in_dim(after(head_rows, part), group * count, count, 1)
    blocks = gather(swap(head_rows.astype(f32), FAR).reshape(-1, width))
    blocks = blocks.reshape(1, dp_size, 5, count, width)

    rows_f32 = jax.ShapeDtypeStruct((length, width), f32)
    rows_low = jax.ShapeDtypeStruct((length, width), bf16)
    units_f32 = jax.ShapeDtypeStruct((length, 2 * units), f32)
    units_low = jax.ShapeDtypeStruct((length, 2 * units), bf16)
    chunk_f32 = jax.ShapeDtypeStruct((half, width), f32)
    scale_of = jax.ShapeDtypeStruct((length, 1), f32)
    shapes = (rows_f32, scale_of, rows_low, units_low, units_f32, chunk_f32)
    arrays = [part, other, row(b_out), row(gain_one), row(shift_one)]
    arrays += [w_in, w_in_far, b_in_two, w_back, w_back_far]
    part, other = [], []
    fed = ()
    for index in range(2):
        *fed, product = on_chunk(
            feed_kernel, "feed", index, scalars, tokens, half, arrays, shapes, tuple(fed)
        )
        part.append(product)
        other.append(swap(product, NEAR))
    xhat_one, scale_one, normed_low, hidden, slope = fed
    shapes = (rows_f32, rows_f32, rows_low, units_low, rows_f32)
    shapes += (jax.ShapeDtypeStruct((3, width), f32), jax.ShapeDtypeStruct((2, units), f32))
    back, sums_two, sums_in = (), [], []
    for index in range(2):
        arrays = [part[index], other[index], xhat_one, slope, row(gain_one), row(shift_one)]
        arrays += [row(b_back), row(gain_two), row(shift_two), w_in, w_in_far, w_back, w_back_far]
        *back, some, some_in = on_chunk(
            feed_back_kernel, "feed_back", index, scalars, cotangent, half, arrays, shapes, tuple(back)
        )
        sums_two.append(some)
        sums_in.append(some_in)
    part, d_second, d_feed, d_pre, output = back
    other = swap(part, NEAR)

    ffn = feed_grads(dp_size, normed_low, d_pre, hidden, d_feed)
    ffn = lax.psum_scatter(ffn.reshape(-1, units), "dp", scatter_dimension=0, tiled=True)

    rows = take(tokens, page)
    arrays = [part, other, d_second, xhat_one, scale_one]
    arrays += [row(gain_one), w_out, w_out_far]
    vectors = sums_two[0] + sums_two[1]
    d_b_in = sums_in[0] + sums_in[1]
    spare = jnp.zeros((1, width), f32)
    vectors = jnp.stack(
        [jnp.concatenate([vectors, d_b_in[side : side + 1], spare], axis=0) for side in range(2)]
    )
    arrays += [proj, w_qkv, blocks, rows, pos_rows, mixed, mixed_far, vectors]
    send, base, keep, give = attend_back(dp_size, jnp.stack([page, low, group]), lengths, arrays)

    def spread(mine, far, rest):
        both = jnp.stack([mine, far])
        out = jnp.stack([jnp.where(low == 0, both, rest), jnp.where(low == 0, rest, both)], axis=1)
        out = out.reshape(pages, length, width)
        return jnp.where(page == 0, out, out[::-1])

    half_of = lambda value, index: lax.dynamic_slice_in_dim(value, index * half, half, 0)
    quarter = half // 2
    out_mine = half_of(output, low)
    out_far = [swap(after(out_mine[:quarter], other), FAR)]

    bits = [1 << k for k in range(dp_size.bit_length() - 1)]
    send, give, _ = lax.optimization_barrier((send, give, out_far[0]))
    near_sum = swap(send, NEAR)
    out_far.append(swap(after(out_mine[quarter:], send), FAR))
    out_far = jnp.concatenate(out_far, axis=0)
    mine = base + near_sum

    group_scalar = jnp.reshape(group, (1,))
    out_turned = swap(out_far, NEAR)
    ffn_rows = ffn.shape[0] // 2
    crossed = swap(jnp.concatenate([mine, ffn[ffn_rows:]], axis=0), FAR)
    ffn = ffn[:ffn_rows] + crossed[half:]
    far_mine = crossed[:half]
    total = after(keep + group_swap(give, bits[0]), near_sum, out_far)
    more = bits[1:]

    def after_all(*values):
        return lax.optimization_barrier(values)

    cut = total.shape[1] // 2
    upper, lower = total[:, :cut], total[:, cut:]
    for step in range(len(more)):
        upper = upper.reshape((-1, 2) + upper.shape[1:])
        lower = lower.reshape((2, -1) + lower.shape[1:])
        give_upper, give_lower = after_all(upper[:, 1], lower[1], *([out_turned] if step else []))[:2]
        got_upper = group_swap(give_upper, more[step])
        got_lower = group_swap(give_lower, more[-1 - step])
        upper = upper[:, 0] + got_upper
        lower = lower[0] + got_lower
    upper, lower = upper[0], lower[0]
    far_sum = swap(after(lower, crossed), FAR)
    ffn = after(ffn, got_upper, got_lower)

    rest = swap(after(jnp.stack([mine, far_mine]), far_sum), NEAR)
    grad_tokens = spread(mine, far_mine, rest)
    out_rest = half_of(output, 1 - low)
    layer_out = spread(out_mine, arrived(out_far), jnp.stack([out_rest, arrived(out_turned)])).astype(bf16)
    total = upper + far_sum
    cut = total.shape[0] // 16 * 8
    upper, lower = total[None, :cut], total[None, cut:]
    for step in range(len(more)):
        got_upper = group_swap(upper, more[step])
        got_lower = group_swap(lower, more[-1 - step])
        upper = jnp.concatenate([upper, got_upper], axis=0)
        lower = jnp.concatenate([lower, got_lower], axis=0)
    upper, lower, _ = lax.optimization_barrier((upper, lower, rest))
    parts = [upper, lower, group_swap(upper, bits[0]), group_swap(lower, bits[0])]
    grad_w_qkv, grad_w_pos, grad_w_out, vectors = place_grads(group_scalar, parts, columns, 8)
    grad_w_qkv, grad_w_pos = turn(grad_w_qkv), turn(grad_w_pos)
    grad_b_out, grad_gain_one, grad_shift_one = vectors[0], vectors[1], vectors[2]
    grad_b_back, grad_gain_two, grad_shift_two = vectors[3], vectors[4], vectors[5]
    grad_b_in = vectors[6]

    ffn = gather(ffn).reshape(dp_size, ffn_rows, units)
    grad_w_in = ffn[:, :in_rows].reshape(width, units)
    grad_w_back = ffn[:, in_rows:].reshape(units, width)
    return (
        layer_out,
        grad_tokens,
        grad_w_qkv,
        grad_w_pos,
        grad_w_out,
        grad_b_out,
        grad_gain_one,
        grad_shift_one,
        grad_w_in,
        grad_b_in,
        grad_w_back,
        grad_b_back,
        grad_gain_two,
        grad_shift_two,
    )


def solution(mesh):
    mp_size = mesh.shape["mp"]
    dp_size = mesh.devices.size // mp_size
    split = jax.sharding.Mesh(mesh.devices.reshape(dp_size, mp_size // 2, 2), ("dp",) + MP)
    placed = (
        P("dp", None, None),
        P("dp"),
        P("dp", None, None),
        P(None, None, MP),
        P(None, None, MP),
        P(MP, None),
        P(),
        P(),
        P(),
        P(None, MP),
        P(MP),
        P(MP, None),
        P(),
        P(),
        P(),
        P("dp", None, None),
    )
    return jax.shard_map(
        partial(body, dp_size, mp_size),
        mesh=split,
        in_specs=placed,
        out_specs=(
            P("dp", None, None),
            P("dp", None, None),
            P(None, None, MP),
            P(None, None, MP),
            P(MP, None),
            P(),
            P(),
            P(),
            P(None, MP),
            P(MP),
            P(MP, None),
            P(),
            P(),
            P(),
        ),
        check_vma=False,
    )
```

```python
from functools import partial
import math

import jax
import jax.numpy as jnp
import numpy as np
from jax import lax
from jax.experimental import pallas as pl
from jax.experimental.pallas import tpu as pltpu
from jax.sharding import PartitionSpec as P

HEAD_DIM = 64
STEP_BITS = 5
STEP = 1 << STEP_BITS
NEAR = 1
MP = ("far", "near")
FAR = 2
MASKED = -1e30


def mm(left, right):
    return jnp.dot(left, right, preferred_element_type=jnp.float32)


def mm_nt(left, right):
    return lax.dot_general(
        left, right, (((1,), (1,)), ((), ())), preferred_element_type=jnp.float32
    )


def mm_tn(left, right):
    return lax.dot_general(
        left, right, (((0,), (0,)), ((), ())), preferred_element_type=jnp.float32
    )


def angle_tables(model_width):
    quarter = model_width // 4
    rate = np.exp(np.arange(quarter) * (-math.log(10000.0) / quarter))
    fine = np.arange(STEP)[:, None] * rate
    coarse = fine * STEP
    zero = np.zeros((STEP, 2 * quarter))
    table = np.concatenate(
        [
            np.concatenate([np.sin(coarse), np.cos(coarse), zero], axis=1),
            np.concatenate([zero, np.sin(fine), np.cos(fine)], axis=1),
        ],
        axis=0,
    )
    parts = []
    rest = table
    for _ in range(3):
        part = rest.astype(jnp.bfloat16)
        parts.append(part)
        rest = rest - part.astype(np.float64)
    return np.concatenate(parts, axis=0)


def sinusoid(coord, table_ref):
    quarter = table_ref.shape[1] // 4
    slot = lax.broadcasted_iota(jnp.int32, (2 * STEP, coord.shape[1]), 0)
    coarse = coord >> STEP_BITS
    fine = (coord & (STEP - 1)) + STEP
    hit = ((slot == coarse) | (slot == fine)).astype(jnp.float32).astype(jnp.bfloat16)
    looked = mm_tn(jnp.concatenate([hit, hit, hit], axis=0), table_ref[...])
    sin_a, cos_a, sin_b, cos_b = [looked[:, k * quarter : (k + 1) * quarter] for k in range(4)]
    return jnp.concatenate([sin_a * cos_b + cos_a * sin_b, cos_a * cos_b - sin_a * sin_b], axis=1)


def probs_t(q, k, pq, pk, length, factor):
    left = jnp.concatenate([k, pk, k], axis=0)
    right = jnp.concatenate([q, q, pq], axis=0)
    scores = mm_tn(left, right) * factor
    visible = lax.broadcasted_iota(jnp.int32, scores.shape, 0) < length
    scores = jnp.where(visible, scores, MASKED)
    raised = jnp.exp(scores - jnp.max(scores, axis=0, keepdims=True))
    return raised * (1.0 / jnp.sum(raised, axis=0, keepdims=True))


def rows_at(head):
    return pl.ds(pl.multiple_of(head * HEAD_DIM, HEAD_DIM), HEAD_DIM)


def attend_kernel(
    heads, scalars_ref, lengths_ref, x_ref, coords_ref, table_ref, wqkv_ref, wpos_ref,
    send_ref, own_ref, proj_ref, pos_ref,
):
    step = pl.program_id(0)
    length = lengths_ref[scalars_ref[0] ^ (1 - step)]
    factor = 1.0 / math.sqrt(3.0 * HEAD_DIM)
    rows = x_ref[0]
    for part in range(3):
        proj_ref[part] = mm_nt(wqkv_ref[part], rows).astype(jnp.bfloat16)
    sides = [sinusoid(coords_ref[0, axis : axis + 1], table_ref) for axis in range(2)]
    position = jnp.concatenate(sides, axis=1).astype(jnp.bfloat16)
    pos_ref[...] = position
    for part in range(2):
        proj_ref[3 + part] = mm_nt(wpos_ref[part], position).astype(jnp.bfloat16)

    def one_head(head, _):
        at = rows_at(head)
        q, k, v, pq, pk = [proj_ref[part, at] for part in range(5)]
        weights = probs_t(q, k, pq, pk, length, factor).astype(jnp.bfloat16)
        mixed = mm(v, weights).astype(jnp.bfloat16)

        @pl.when(step == 0)
        def _():
            send_ref[at] = mixed.astype(jnp.float32)

        @pl.when(step == 1)
        def _():
            own_ref[at] = mixed

        return 0

    lax.fori_loop(0, heads, one_head, 0)


def attend(scalars, lengths, tokens, coords, table, w_qkv, w_pos):
    pages, length, width = tokens.shape
    columns = w_qkv.shape[1]
    whole = lambda shape: pl.BlockSpec(shape, lambda i, s, n: (0,) * len(shape))
    shapes = (
        jax.ShapeDtypeStruct((columns, length), jnp.float32),
        jax.ShapeDtypeStruct((columns, length), jnp.bfloat16),
        jax.ShapeDtypeStruct((5, columns, length), jnp.bfloat16),
        jax.ShapeDtypeStruct((length, width), jnp.bfloat16),
    )
    page = lambda i, s, n: (s[0] ^ (1 - i), 0, 0)
    return pl.pallas_call(
        partial(attend_kernel, columns // HEAD_DIM),
        out_shape=shapes,
        grid_spec=pltpu.PrefetchScalarGridSpec(
            num_scalar_prefetch=2,
            grid=(pages,),
            in_specs=[
                pl.BlockSpec((1, length, width), page),
                pl.BlockSpec((1,) + coords.shape[1:], page),
                whole(table.shape),
                whole(w_qkv.shape),
                whole(w_pos.shape),
            ],
            out_specs=[whole(shape.shape) for shape in shapes],
        ),
        compiler_params=pltpu.CompilerParams(vmem_limit_bytes=40 << 20),
        cost_estimate=pl.CostEstimate(
            flops=2 * pages * length * columns * (5 * width + 4 * length),
            transcendentals=pages * length * length * columns // HEAD_DIM,
            bytes_accessed=pages * length * (4 * width + 14 * columns),
        ),
        name="attend",
    )(scalars, lengths, tokens, coords, table, w_qkv, w_pos)


def norm_parts(values):
    center = values - jnp.mean(values, axis=-1, keepdims=True)
    spread = jnp.mean(center * center, axis=-1, keepdims=True)
    scale = lax.rsqrt(spread + 1e-05)
    return center * scale, scale


def norm_back(grad, gain, xhat, scale):
    up = grad * gain
    mean = jnp.mean(up, axis=-1, keepdims=True)
    along = jnp.mean(up * xhat, axis=-1, keepdims=True)
    return scale * (up - mean - xhat * along)


def column_sum(values):
    return jnp.sum(values.astype(jnp.float32), axis=0, keepdims=True)


def feed_kernel(
    scalars_ref, x_ref, part_ref, other_ref, b_out_ref, gain_ref, shift_ref, w_in_ref, w_in_far_ref, b_in_ref,
    w_back_ref, w_back_far_ref, xhat_ref, scale_ref, low_ref, hidden_ref, slope_ref, next_ref,
):
    first = x_ref[0].astype(jnp.float32) + (part_ref[...] + other_ref[...] + b_out_ref[...])
    xhat, scale = norm_parts(first)
    low = (xhat * gain_ref[...] + shift_ref[...]).astype(jnp.bfloat16)
    xhat_ref[...] = xhat
    scale_ref[...] = scale
    low_ref[...] = low
    units = w_in_ref.shape[1]
    total = None
    for side, (into, back) in enumerate(((w_in_ref, w_back_ref), (w_in_far_ref, w_back_far_ref))):
        at = slice(side * units, (side + 1) * units)
        pre = mm(low, into[...]) + b_in_ref[side : side + 1]
        cdf = 0.5 * (1.0 + lax.erf(pre * math.sqrt(0.5)))
        hidden = (pre * cdf).astype(jnp.bfloat16)
        hidden_ref[:, at] = hidden
        slope_ref[:, at] = cdf + pre * (jnp.exp(-0.5 * pre * pre) * (1.0 / math.sqrt(2.0 * math.pi)))
        product = mm(hidden, back[...])
        total = product if total is None else total + product
    next_ref[...] = total


def feed_back_kernel(
    scalars_ref, cot_ref, part_ref, other_ref, xhat_ref, slope_ref, gain_one_ref, shift_one_ref, b_back_ref,
    gain_ref, shift_ref, w_in_ref, w_in_far_ref, w_back_ref, w_back_far_ref,
    next_ref, second_ref, feed_ref, pre_ref, out_ref, sums_ref, sums_in_ref,
):
    normed = xhat_ref[...] * gain_one_ref[...] + shift_one_ref[...]
    second = normed + (part_ref[...] + other_ref[...] + b_back_ref[...])
    xhat, scale = norm_parts(second)
    out_ref[...] = xhat * gain_ref[...] + shift_ref[...]
    grad = cot_ref[0].astype(jnp.float32)
    d_second = norm_back(grad, gain_ref[...], xhat, scale)
    second_ref[...] = d_second
    d_feed = d_second.astype(jnp.bfloat16)
    feed_ref[...] = d_feed
    sums_ref[0:1] = column_sum(d_feed)
    sums_ref[1:2] = column_sum(grad * xhat)
    sums_ref[2:3] = column_sum(grad)
    units = w_in_ref.shape[1]
    total = None
    for side, (into, back) in enumerate(((w_in_ref, w_back_ref), (w_in_far_ref, w_back_far_ref))):
        at = slice(side * units, (side + 1) * units)
        d_pre = (mm_nt(d_feed, back[...]) * slope_ref[:, at]).astype(jnp.bfloat16)
        pre_ref[:, at] = d_pre
        sums_in_ref[side : side + 1] = column_sum(d_pre)
        product = mm_nt(d_pre, into[...])
        total = product if total is None else total + product
    next_ref[...] = total


def without(kernel, first, count):
    def call(*refs):
        return kernel(*refs[:first], *refs[first + count :])

    return call


def on_chunk(kernel, name, chunk, scalars, pages_array, rows, arrays, shapes, before=()):
    length, width = pages_array.shape[1:]

    def rows_of(array):
        if array.shape[0] == length and len(array.shape) == 2:
            return pl.BlockSpec((rows, array.shape[1]), lambda i, s: (chunk, 0))
        return pl.BlockSpec(array.shape, lambda i, s: (0,) * len(array.shape))

    inputs = 2 + len(arrays)
    return pl.pallas_call(
        without(kernel, inputs, len(before)),
        out_shape=shapes,
        grid_spec=pltpu.PrefetchScalarGridSpec(
            num_scalar_prefetch=1,
            grid=(1,),
            in_specs=[pl.BlockSpec((1, rows, width), lambda i, s: (s[0], chunk, 0))]
            + [rows_of(array) for array in arrays]
            + [pl.BlockSpec(memory_space=pl.ANY)] * len(before),
            out_specs=[rows_of(shape) for shape in shapes],
        ),
        input_output_aliases={inputs + index: index for index in range(len(before))},
        compiler_params=pltpu.CompilerParams(vmem_limit_bytes=48 << 20),
        cost_estimate=pl.CostEstimate(
            flops=16 * rows * width * width, transcendentals=2 * rows * width, bytes_accessed=40 * rows * width
        ),
        name=name,
    )(scalars, pages_array, *arrays, *before)


def feed_grads_kernel(count, low_ref, pre_ref, hidden_ref, feed_ref, out_ref):
    rows = out_ref.shape[2]

    def put(left, right):
        product = mm_tn(left[...], right[...])
        for block in range(count):
            out_ref[block, 0] = product[block * rows : (block + 1) * rows]

    @pl.when(pl.program_id(0) % 2 == 0)
    def _():
        put(low_ref, pre_ref)

    @pl.when(pl.program_id(0) % 2 == 1)
    def _():
        put(hidden_ref, feed_ref)


def feed_grads(count, low, d_pre, hidden, d_feed):
    length, width = low.shape
    units = hidden.shape[1] // 2
    return pl.pallas_call(
        partial(feed_grads_kernel, count),
        out_shape=pltpu.HBM((count, 4, width // count, units), jnp.float32),
        grid_spec=pl.GridSpec(
            grid=(4,),
            in_specs=[
                pl.BlockSpec((length, width), lambda i: (0, 0)),
                pl.BlockSpec((length, units), lambda i: (0, i // 2)),
                pl.BlockSpec((length, units), lambda i: (0, i // 2)),
                pl.BlockSpec((length, width), lambda i: (0, 0)),
            ],
            out_specs=pl.BlockSpec((count, 1, width // count, units), lambda i: (0, i, 0, 0)),
        ),
        compiler_params=pltpu.CompilerParams(vmem_limit_bytes=40 << 20),
        cost_estimate=pl.CostEstimate(
            flops=8 * length * width * units, transcendentals=0, bytes_accessed=16 * width * units
        ),
        name="feed_grads",
    )(low, d_pre, hidden, d_feed)


def weight_grads(count, group, x_ref, pos_ref, d_ref, db_ref, mixed_ref, far_ref, vec_ref, keep_ref, send_ref):
    columns = mixed_ref.shape[0]
    rows = columns // count
    odd = group & 1
    extra = vec_ref.shape[1]
    side_rows = 6 * rows + extra
    mixed = jnp.concatenate([mixed_ref[...], far_ref[...]], axis=0)
    rights = [x_ref] * 3 + [pos_ref] * 2 + [db_ref]

    def put(block, at, value):
        place = (block ^ group) >> 1

        @pl.when(odd == (block & 1))
        def _():
            keep_ref[place, at] = value

        @pl.when(odd != (block & 1))
        def _():
            send_ref[place, at] = value

    for part, right in enumerate(rights):
        product = mm(d_ref[part] if part < 5 else mixed, right[...])
        for block in range(count):
            for side in range(2):
                start = side * columns + block * rows
                at = side * side_rows + part * rows
                put(block, slice(at, at + rows), product[start : start + rows])
    for block in range(count):
        for side in range(2):
            at = slice(side * side_rows + 6 * rows, (side + 1) * side_rows)
            put(block, at, vec_ref[side] if block == 0 else jnp.zeros(vec_ref.shape[1:], jnp.float32))


def attend_back_kernel(
    heads, count, scalars_ref, lengths_ref, part_ref, other_ref, second_ref, xhat_ref, scale_ref, gain_ref, w_out_ref, w_out_far_ref, own_ref, wqkv_ref, blocks_ref, x_ref, pos_ref, mixed_ref, mixed_far_ref, more_ref,
    send_ref, base_ref, keep_ref, give_ref, d_ref, branch_ref, dm_ref, first_ref, proj_ref, wfar_ref, vec_ref,
):
    page, low = scalars_ref[0], scalars_ref[1]
    length = lengths_ref[page]
    factor = 1.0 / math.sqrt(3.0 * HEAD_DIM)
    columns = heads * HEAD_DIM
    half = part_ref.shape[0] // 2
    block_rows = blocks_ref.shape[3]
    for part in range(5):
        for block in range(count):
            at = slice(block * block_rows, (block + 1) * block_rows)
            wfar_ref[part, at] = blocks_ref[0, block, part]
        weight = wfar_ref[part].astype(jnp.bfloat16)
        left = x_ref if part < 3 else pos_ref
        proj_ref[part, columns:] = mm_nt(weight, left[...]).astype(jnp.bfloat16)
        proj_ref[part, :columns] = own_ref[part]
    sums = None
    for index in range(2):
        at = slice(index * half, (index + 1) * half)
        xhat = xhat_ref[at]
        d_normed = second_ref[at] + (part_ref[at] + other_ref[at])
        d_first = norm_back(d_normed, gain_ref[...], xhat, scale_ref[at])
        first_ref[at] = d_first
        d_branch = d_first.astype(jnp.bfloat16)
        branch_ref[at] = d_branch
        some = (column_sum(d_branch), column_sum(d_normed * xhat), column_sum(d_normed))
        sums = some if sums is None else tuple(x + y for x, y in zip(sums, some))
        dm_ref[:columns, at] = mm_nt(w_out_ref[...], d_branch).astype(jnp.bfloat16)
        dm_ref[columns:, at] = mm_nt(w_out_far_ref[...], d_branch).astype(jnp.bfloat16)
    for side in range(2):
        for index, value in enumerate(sums):
            vec_ref[side, index : index + 1] = value
        vec_ref[side, len(sums) :] = more_ref[side]

    def one_head(head, _):
        at = rows_at(head)
        q, k, v, pq, pk = [proj_ref[part, at] for part in range(5)]
        dm = dm_ref[at]
        probs = probs_t(q, k, pq, pk, length, factor)
        weights = probs.astype(jnp.bfloat16)
        d_values = mm(weights, dm.T)
        d_probs = mm_tn(v, dm)
        inner = jnp.sum(d_probs * probs, axis=0, keepdims=True)
        d_scores = (probs * (d_probs - inner)).astype(jnp.bfloat16)
        by_queries = mm(d_scores, jnp.concatenate([q, pq], axis=0).T).T
        by_query, by_pos_query = by_queries[:HEAD_DIM], by_queries[HEAD_DIM:]
        by_keys = mm(jnp.concatenate([k, pk], axis=0), d_scores)
        by_key, by_pos_key = by_keys[:HEAD_DIM], by_keys[HEAD_DIM:]
        grads = (
            (by_key + by_pos_key) * factor,
            (by_query + by_pos_query) * factor,
            d_values.T,
            by_key * factor,
            by_query * factor,
        )
        for part, value in enumerate(grads):
            d_ref[part, at] = value.astype(jnp.bfloat16)
        return 0

    lax.fori_loop(0, 2 * heads, one_head, 0)
    for part in range(3):
        for side in range(2):
            at = slice(side * columns, (side + 1) * columns)
            weight = wqkv_ref[part] if side == 0 else wfar_ref[part].astype(jnp.bfloat16)
            first_ref_part = mm_tn(d_ref[part, at], weight)
            if part == side == 0:
                total = first_ref_part
            else:
                total = total + first_ref_part
    upper, lower = total[:half], total[half:]
    send_ref[...] = jnp.where(low == 0, lower, upper)
    base_ref[...] = jnp.where(low == 0, upper + first_ref[:half], lower + first_ref[half:])
    weight_grads(
        count, scalars_ref[2], x_ref, pos_ref, d_ref, branch_ref, mixed_ref, mixed_far_ref, vec_ref, keep_ref, give_ref
    )


def attend_back(count, scalars, lengths, arrays):
    proj = arrays[8]
    parts, columns, length = proj.shape
    half, width = length // 2, arrays[0].shape[1]
    heads = columns // HEAD_DIM
    whole = lambda shape: pl.BlockSpec(shape, lambda i, s, n: (0,) * len(shape))
    shapes = (
        jax.ShapeDtypeStruct((half, width), jnp.float32),
        jax.ShapeDtypeStruct((half, width), jnp.float32),
    ) + 2 * (jax.ShapeDtypeStruct((count // 2, 2 * (6 * (columns // count) + 8), width), jnp.float32),)
    return pl.pallas_call(
        partial(attend_back_kernel, heads, count),
        out_shape=shapes,
        grid_spec=pltpu.PrefetchScalarGridSpec(
            num_scalar_prefetch=2,
            grid=(1,),
            in_specs=[
                whole(array.shape)
                if len(array.shape) < 5
                else pl.BlockSpec((1,) + array.shape[1:], lambda i, s, n: (0, 0, 0, 0, 0))
                for array in arrays
            ],
            out_specs=[whole(shape.shape) for shape in shapes],
            scratch_shapes=[
                pltpu.VMEM((parts, 2 * columns, length), jnp.bfloat16),
                pltpu.VMEM((length, width), jnp.bfloat16),
                pltpu.VMEM((2 * columns, length), jnp.bfloat16),
                pltpu.VMEM((length, width), jnp.float32),
                pltpu.VMEM((parts, 2 * columns, length), jnp.bfloat16),
                pltpu.VMEM((parts, columns, width), jnp.float32),
                pltpu.VMEM((2, 8, width), jnp.float32),
            ],
        ),
        compiler_params=pltpu.CompilerParams(vmem_limit_bytes=58 << 20),
        cost_estimate=pl.CostEstimate(
            flops=2 * 2 * heads * length * length * HEAD_DIM * 9 + 20 * length * width * columns,
            transcendentals=2 * heads * length * length,
            bytes_accessed=40 * length * width,
        ),
        name="attend_back",
    )(scalars, lengths, *arrays)


def split_blocks_kernel(in_ref, first_ref, second_ref):
    count, both, _ = in_ref.shape
    rows = both // 2
    for block in range(count):
        at = slice(block * rows, (block + 1) * rows)
        first_ref[at] = in_ref[block, :rows]
        second_ref[at] = in_ref[block, rows:]


def split_blocks(blocks):
    count, both, width = blocks.shape
    lanes = width // 3 if width % 384 == 0 else width
    shape = pltpu.HBM((count * both // 2, width), blocks.dtype)
    out_spec = pl.BlockSpec((count * both // 2, lanes), lambda i: (0, i))
    return pl.pallas_call(
        split_blocks_kernel,
        out_shape=(shape, shape),
        grid_spec=pl.GridSpec(
            grid=(width // lanes,),
            in_specs=[pl.BlockSpec((count, both, lanes), lambda i: (0, 0, i))],
            out_specs=[out_spec, out_spec],
        ),
        compiler_params=pltpu.CompilerParams(vmem_limit_bytes=24 << 20),
        cost_estimate=pl.CostEstimate(flops=0, transcendentals=0, bytes_accessed=8 * blocks.size),
        name="split_blocks",
    )(blocks)


def place_grads_kernel(
    order, scalars_ref, low_a_ref, low_b_ref, high_a_ref, high_b_ref, qkv_ref, pos_ref, out_ref, vec_ref
):
    group = scalars_ref[0]
    count = 2 * low_a_ref.shape[0]
    rows = qkv_ref.shape[1] // count
    cut = low_a_ref.shape[1]

    def read(place, start, stop):
        upper = (place & 1) == 1
        index = place >> 1
        pieces = []
        if start < cut:
            at = slice(start, min(stop, cut))
            pieces.append(jnp.where(upper, high_a_ref[index, at], low_a_ref[index, at]))
        if stop > cut:
            at = slice(max(start, cut) - cut, stop - cut)
            turned_index = 0
            for bit in range(len(order)):
                turned_index = turned_index | (((index >> bit) & 1) << order[bit])
            pieces.append(jnp.where(upper, high_b_ref[turned_index, at], low_b_ref[turned_index, at]))
        return jnp.concatenate(pieces, axis=0) if len(pieces) > 1 else pieces[0]

    for block in range(count):
        place = block ^ group
        at = slice(block * rows, (block + 1) * rows)
        for part in range(6):
            value = read(place, part * rows, (part + 1) * rows)
            if part < 3:
                qkv_ref[part, at] = value
            elif part < 5:
                pos_ref[part - 3, at] = value
            else:
                out_ref[at] = value
        if block == 0:
            vec_ref[...] = read(place, 6 * rows, cut + low_b_ref.shape[1])


def place_grads(scalars, parts, columns, vec_rows):
    width = parts[0].shape[2]
    bits = parts[0].shape[0].bit_length() - 1
    whole = lambda shape: pl.BlockSpec(shape, lambda i: (0,) * len(shape))
    shapes = (
        jax.ShapeDtypeStruct((3, columns, width), jnp.float32),
        jax.ShapeDtypeStruct((2, columns, width), jnp.float32),
        jax.ShapeDtypeStruct((columns, width), jnp.float32),
        jax.ShapeDtypeStruct((vec_rows, width), jnp.float32),
    )
    return pl.pallas_call(
        partial(place_grads_kernel, tuple(range(bits))[::-1]),
        out_shape=shapes,
        grid_spec=pl.GridSpec(
            grid=(1,),
            in_specs=[pl.BlockSpec(memory_space=pltpu.SMEM)] + [whole(part.shape) for part in parts],
            out_specs=[whole(shape.shape) for shape in shapes],
        ),
        compiler_params=pltpu.CompilerParams(vmem_limit_bytes=40 << 20),
        cost_estimate=pl.CostEstimate(
            flops=0, transcendentals=0, bytes_accessed=32 * width * columns * 3
        ),
        name="place_grads",
    )(scalars, *parts)


def body(
    dp_size,
    mp_size,
    tokens,
    lengths,
    coords,
    w_qkv,
    w_pos,
    w_out,
    b_out,
    gain_one,
    shift_one,
    w_in,
    b_in,
    w_back,
    b_back,
    gain_two,
    shift_two,
    cotangent,
):
    pages, length, width = tokens.shape
    columns = w_qkv.shape[2]
    units = w_in.shape[1]
    here = lax.axis_index(MP)
    low = here & 1
    page = here >> 1
    group = lax.axis_index("dp")
    f32, bf16 = jnp.float32, jnp.bfloat16
    half = length // 2
    one = jnp.where(lengths[0] > 0, 1.0, 0.0).astype(f32)

    def arrived(value):
        return value * one

    def swap(value, bit):
        pairs = [(i, i ^ bit) for i in range(mp_size)]
        return lax.ppermute(value, MP, pairs)

    def group_swap(value, bit):
        pairs = [(i, i ^ bit) for i in range(dp_size)]
        return lax.ppermute(value, "dp", pairs)

    def my_rows(value):
        rows = value.shape[0] // dp_size
        return lax.dynamic_slice_in_dim(value, group * rows, rows, 0)

    def gather(value):
        return lax.all_gather(value, "dp", axis=0, tiled=True)

    def take(value, index):
        return lax.dynamic_index_in_dim(value, index, 0, keepdims=False)

    def after(value, *others):
        return lax.optimization_barrier((value,) + others)[0]

    def row(value):
        return value.reshape(1, -1)

    chunk_rows = lambda value: [value[:half], value[half:]]

    turn = lambda value: jnp.swapaxes(value, 1, 2)
    w_qkv, w_pos = turn(w_qkv), turn(w_pos)
    out_rows = swap(my_rows(w_out).astype(f32), FAR)
    out_rows = jnp.pad(out_rows, ((0, max(0, 48 - out_rows.shape[0])), (0, 0)))
    unit_rows = jnp.concatenate([my_rows(w_in), my_rows(w_back)], axis=0).astype(f32)
    tail = jnp.concatenate([row(b_in), jnp.zeros((7, units), f32)], axis=0)
    far_rows = swap(jnp.concatenate([unit_rows, tail], axis=0), FAR)
    count = columns // dp_size

    table = jnp.asarray(angle_tables(width))
    scalars = jnp.stack([page, low])
    mixed_send, mixed, proj, pos_rows = attend(scalars, lengths, tokens, coords, table, w_qkv, w_pos)
    w_out_far = gather(out_rows).reshape(dp_size, -1, width)[:, : columns // dp_size]
    w_out_far = arrived(w_out_far.reshape(columns, width)).astype(bf16)
    mixed_far = swap(mixed_send, FAR)
    far_rows = after(far_rows, mixed_far)
    count = unit_rows.shape[0]
    b_in_two = jnp.stack([b_in, far_rows[count]])
    blocks = arrived(gather(far_rows[:count])).reshape(dp_size, count, -1)
    in_rows = width // dp_size
    w_in_far = blocks[:, :in_rows].reshape(width, units).astype(bf16)
    w_back_far = blocks[:, in_rows:].reshape(units, width).astype(bf16)

    mixed_far = arrived(mixed_far).astype(bf16)
    part = mm_tn(jnp.concatenate([mixed, mixed_far], axis=0), jnp.concatenate([w_out, w_out_far], axis=0))
    other = swap(part, NEAR)
    head_rows = jnp.concatenate([w_qkv, w_pos], axis=0)
    count = columns // dp_size
    head_rows = lax.dynamic_slice_in_dim(after(head_rows, part), group * count, count, 1)
    blocks = gather(swap(head_rows.astype(f32), FAR).reshape(-1, width))
    blocks = blocks.reshape(1, dp_size, 5, count, width)

    rows_f32 = jax.ShapeDtypeStruct((length, width), f32)
    rows_low = jax.ShapeDtypeStruct((length, width), bf16)
    units_f32 = jax.ShapeDtypeStruct((length, 2 * units), f32)
    units_low = jax.ShapeDtypeStruct((length, 2 * units), bf16)
    chunk_f32 = jax.ShapeDtypeStruct((half, width), f32)
    scale_of = jax.ShapeDtypeStruct((length, 1), f32)
    shapes = (rows_f32, scale_of, rows_low, units_low, units_f32, chunk_f32)
    arrays = [part, other, row(b_out), row(gain_one), row(shift_one)]
    arrays += [w_in, w_in_far, b_in_two, w_back, w_back_far]
    part, other = [], []
    fed = ()
    for index in range(2):
        *fed, product = on_chunk(
            feed_kernel, "feed", index, scalars, tokens, half, arrays, shapes, tuple(fed)
        )
        part.append(product)
        other.append(swap(product, NEAR))
    xhat_one, scale_one, normed_low, hidden, slope = fed
    shapes = (rows_f32, rows_f32, rows_low, units_low, rows_f32)
    shapes += (jax.ShapeDtypeStruct((3, width), f32), jax.ShapeDtypeStruct((2, units), f32))
    back, sums_two, sums_in = (), [], []
    for index in range(2):
        arrays = [part[index], other[index], xhat_one, slope, row(gain_one), row(shift_one)]
        arrays += [row(b_back), row(gain_two), row(shift_two), w_in, w_in_far, w_back, w_back_far]
        *back, some, some_in = on_chunk(
            feed_back_kernel, "feed_back", index, scalars, cotangent, half, arrays, shapes, tuple(back)
        )
        sums_two.append(some)
        sums_in.append(some_in)
    part, d_second, d_feed, d_pre, output = back
    other = swap(part, NEAR)

    ffn = feed_grads(dp_size, normed_low, d_pre, hidden, d_feed)
    ffn = lax.psum_scatter(ffn.reshape(-1, units), "dp", scatter_dimension=0, tiled=True)

    rows = take(tokens, page)
    arrays = [part, other, d_second, xhat_one, scale_one]
    arrays += [row(gain_one), w_out, w_out_far]
    vectors = sums_two[0] + sums_two[1]
    d_b_in = sums_in[0] + sums_in[1]
    spare = jnp.zeros((1, width), f32)
    vectors = jnp.stack(
        [jnp.concatenate([vectors, d_b_in[side : side + 1], spare], axis=0) for side in range(2)]
    )
    arrays += [proj, w_qkv, blocks, rows, pos_rows, mixed, mixed_far, vectors]
    send, base, keep, give = attend_back(dp_size, jnp.stack([page, low, group]), lengths, arrays)

    def spread(mine, far, rest):
        both = jnp.stack([mine, far])
        out = jnp.stack([jnp.where(low == 0, both, rest), jnp.where(low == 0, rest, both)], axis=1)
        out = out.reshape(pages, length, width)
        return jnp.where(page == 0, out, out[::-1])

    half_of = lambda value, index: lax.dynamic_slice_in_dim(value, index * half, half, 0)
    out_mine = half_of(output, low)
    out_far = swap(after(out_mine, other), FAR)

    bits = [1 << k for k in range(dp_size.bit_length() - 1)]
    give = after(give, out_far)
    near_sum = swap(send, NEAR)
    mine = base + near_sum

    group_scalar = jnp.reshape(group, (1,))
    out_turned = swap(out_far, NEAR)
    ffn_rows = ffn.shape[0] // 2
    crossed = swap(jnp.concatenate([mine, ffn[ffn_rows:]], axis=0), FAR)
    ffn = ffn[:ffn_rows] + crossed[half:]
    far_mine = crossed[:half]
    total = keep + group_swap(give, bits[0])
    more = bits[1:]

    def after_all(*values):
        return lax.optimization_barrier(values)

    cut = total.shape[1] // 2
    upper, lower = total[:, :cut], total[:, cut:]
    for step in range(len(more)):
        upper = upper.reshape((-1, 2) + upper.shape[1:])
        lower = lower.reshape((2, -1) + lower.shape[1:])
        give_upper, give_lower = after_all(upper[:, 1], lower[1], *([out_turned] if step else []))[:2]
        got_upper = group_swap(give_upper, more[step])
        got_lower = group_swap(give_lower, more[-1 - step])
        upper = upper[:, 0] + got_upper
        lower = lower[0] + got_lower
    upper, lower = upper[0], lower[0]
    far_sum = swap(after(lower, crossed), FAR)
    ffn = after(ffn, got_upper, got_lower)

    rest = swap(after(jnp.stack([mine, far_mine]), far_sum), NEAR)
    grad_tokens = spread(mine, far_mine, rest)
    out_rest = half_of(output, 1 - low)
    layer_out = spread(out_mine, arrived(out_far), jnp.stack([out_rest, arrived(out_turned)])).astype(bf16)
    total = upper + far_sum
    cut = total.shape[0] // 16 * 8
    upper, lower = total[None, :cut], total[None, cut:]
    for step in range(len(more)):
        got_upper = group_swap(upper, more[step])
        got_lower = group_swap(lower, more[-1 - step])
        upper = jnp.concatenate([upper, got_upper], axis=0)
        lower = jnp.concatenate([lower, got_lower], axis=0)
    grad_w_in, grad_w_back = split_blocks(gather(ffn).reshape(dp_size, ffn_rows, units))
    upper, lower = after_all(upper, lower, rest, grad_w_in)[:2]
    parts = [upper, lower, group_swap(upper, bits[0]), group_swap(lower, bits[0])]
    grad_w_qkv, grad_w_pos, grad_w_out, vectors = place_grads(group_scalar, parts, columns, 8)
    grad_w_qkv, grad_w_pos = turn(grad_w_qkv), turn(grad_w_pos)
    grad_b_out, grad_gain_one, grad_shift_one = vectors[0], vectors[1], vectors[2]
    grad_b_back, grad_gain_two, grad_shift_two = vectors[3], vectors[4], vectors[5]
    grad_b_in = vectors[6]

    return (
        layer_out,
        grad_tokens,
        grad_w_qkv,
        grad_w_pos,
        grad_w_out,
        grad_b_out,
        grad_gain_one,
        grad_shift_one,
        grad_w_in,
        grad_b_in,
        grad_w_back,
        grad_b_back,
        grad_gain_two,
        grad_shift_two,
    )


def solution(mesh):
    mp_size = mesh.shape["mp"]
    dp_size = mesh.devices.size // mp_size
    split = jax.sharding.Mesh(mesh.devices.reshape(dp_size, mp_size // 2, 2), ("dp",) + MP)
    placed = (
        P("dp", None, None),
        P("dp"),
        P("dp", None, None),
        P(None, None, MP),
        P(None, None, MP),
        P(MP, None),
        P(),
        P(),
        P(),
        P(None, MP),
        P(MP),
        P(MP, None),
        P(),
        P(),
        P(),
        P("dp", None, None),
    )
    return jax.shard_map(
        partial(body, dp_size, mp_size),
        mesh=split,
        in_specs=placed,
        out_specs=(
            P("dp", None, None),
            P("dp", None, None),
            P(None, None, MP),
            P(None, None, MP),
            P(MP, None),
            P(),
            P(),
            P(),
            P(None, MP),
            P(MP),
            P(MP, None),
            P(),
            P(),
            P(),
        ),
        check_vma=False,
    )
```

```python
from functools import partial
import math

import jax
import jax.numpy as jnp
import numpy as np
from jax import lax
from jax.experimental import pallas as pl
from jax.experimental.pallas import tpu as pltpu
from jax.sharding import PartitionSpec as P

HEAD_DIM = 64
STEP_BITS = 5
STEP = 1 << STEP_BITS
NEAR = 1
MP = ("far", "near")
FAR = 2
MASKED = -1e30


def mm(left, right):
    return jnp.dot(left, right, preferred_element_type=jnp.float32)


def mm_nt(left, right):
    return lax.dot_general(
        left, right, (((1,), (1,)), ((), ())), preferred_element_type=jnp.float32
    )


def mm_tn(left, right):
    return lax.dot_general(
        left, right, (((0,), (0,)), ((), ())), preferred_element_type=jnp.float32
    )


def angle_tables(model_width):
    quarter = model_width // 4
    rate = np.exp(np.arange(quarter) * (-math.log(10000.0) / quarter))
    fine = np.arange(STEP)[:, None] * rate
    coarse = fine * STEP
    zero = np.zeros((STEP, 2 * quarter))
    table = np.concatenate(
        [
            np.concatenate([np.sin(coarse), np.cos(coarse), zero], axis=1),
            np.concatenate([zero, np.sin(fine), np.cos(fine)], axis=1),
        ],
        axis=0,
    )
    parts = []
    rest = table
    for _ in range(3):
        part = rest.astype(jnp.bfloat16)
        parts.append(part)
        rest = rest - part.astype(np.float64)
    return np.concatenate(parts, axis=0)


def sinusoid(coord, table_ref):
    quarter = table_ref.shape[1] // 4
    slot = lax.broadcasted_iota(jnp.int32, (2 * STEP, coord.shape[1]), 0)
    coarse = coord >> STEP_BITS
    fine = (coord & (STEP - 1)) + STEP
    hit = ((slot == coarse) | (slot == fine)).astype(jnp.float32).astype(jnp.bfloat16)
    looked = mm_tn(jnp.concatenate([hit, hit, hit], axis=0), table_ref[...])
    sin_a, cos_a, sin_b, cos_b = [looked[:, k * quarter : (k + 1) * quarter] for k in range(4)]
    return jnp.concatenate([sin_a * cos_b + cos_a * sin_b, cos_a * cos_b - sin_a * sin_b], axis=1)


def probs_t(q, k, pq, pk, length, factor):
    left = jnp.concatenate([k, pk, k], axis=0)
    right = jnp.concatenate([q, q, pq], axis=0)
    scores = mm_tn(left, right) * factor
    visible = lax.broadcasted_iota(jnp.int32, scores.shape, 0) < length
    scores = jnp.where(visible, scores, MASKED)
    raised = jnp.exp(scores - jnp.max(scores, axis=0, keepdims=True))
    return raised * (1.0 / jnp.sum(raised, axis=0, keepdims=True))


def rows_at(head):
    return pl.ds(pl.multiple_of(head * HEAD_DIM, HEAD_DIM), HEAD_DIM)


def attend_kernel(
    heads, scalars_ref, lengths_ref, x_ref, coords_ref, table_ref, wqkv_ref, wpos_ref,
    send_ref, own_ref, proj_ref, pos_ref,
):
    step = pl.program_id(0)
    length = lengths_ref[scalars_ref[0] ^ (1 - step)]
    factor = 1.0 / math.sqrt(3.0 * HEAD_DIM)
    rows = x_ref[0]
    for part in range(3):
        proj_ref[part] = mm_nt(wqkv_ref[part], rows).astype(jnp.bfloat16)
    sides = [sinusoid(coords_ref[0, axis : axis + 1], table_ref) for axis in range(2)]
    position = jnp.concatenate(sides, axis=1).astype(jnp.bfloat16)
    pos_ref[...] = position
    for part in range(2):
        proj_ref[3 + part] = mm_nt(wpos_ref[part], position).astype(jnp.bfloat16)

    def one_head(head, _):
        at = rows_at(head)
        q, k, v, pq, pk = [proj_ref[part, at] for part in range(5)]
        weights = probs_t(q, k, pq, pk, length, factor).astype(jnp.bfloat16)
        mixed = mm(v, weights).astype(jnp.bfloat16)

        @pl.when(step == 0)
        def _():
            send_ref[at] = mixed.astype(jnp.float32)

        @pl.when(step == 1)
        def _():
            own_ref[at] = mixed

        return 0

    lax.fori_loop(0, heads, one_head, 0)


def attend(scalars, lengths, tokens, coords, table, w_qkv, w_pos):
    pages, length, width = tokens.shape
    columns = w_qkv.shape[1]
    whole = lambda shape: pl.BlockSpec(shape, lambda i, s, n: (0,) * len(shape))
    shapes = (
        jax.ShapeDtypeStruct((columns, length), jnp.float32),
        jax.ShapeDtypeStruct((columns, length), jnp.bfloat16),
        jax.ShapeDtypeStruct((5, columns, length), jnp.bfloat16),
        jax.ShapeDtypeStruct((length, width), jnp.bfloat16),
    )
    page = lambda i, s, n: (s[0] ^ (1 - i), 0, 0)
    return pl.pallas_call(
        partial(attend_kernel, columns // HEAD_DIM),
        out_shape=shapes,
        grid_spec=pltpu.PrefetchScalarGridSpec(
            num_scalar_prefetch=2,
            grid=(pages,),
            in_specs=[
                pl.BlockSpec((1, length, width), page),
                pl.BlockSpec((1,) + coords.shape[1:], page),
                whole(table.shape),
                whole(w_qkv.shape),
                whole(w_pos.shape),
            ],
            out_specs=[whole(shape.shape) for shape in shapes],
        ),
        compiler_params=pltpu.CompilerParams(vmem_limit_bytes=40 << 20),
        cost_estimate=pl.CostEstimate(
            flops=2 * pages * length * columns * (5 * width + 4 * length),
            transcendentals=pages * length * length * columns // HEAD_DIM,
            bytes_accessed=pages * length * (4 * width + 14 * columns),
        ),
        name="attend",
    )(scalars, lengths, tokens, coords, table, w_qkv, w_pos)


def norm_parts(values):
    center = values - jnp.mean(values, axis=-1, keepdims=True)
    spread = jnp.mean(center * center, axis=-1, keepdims=True)
    scale = lax.rsqrt(spread + 1e-05)
    return center * scale, scale


def norm_back(grad, gain, xhat, scale):
    up = grad * gain
    mean = jnp.mean(up, axis=-1, keepdims=True)
    along = jnp.mean(up * xhat, axis=-1, keepdims=True)
    return scale * (up - mean - xhat * along)


def column_sum(values):
    return jnp.sum(values.astype(jnp.float32), axis=0, keepdims=True)


def feed_kernel(
    scalars_ref, x_ref, part_ref, other_ref, b_out_ref, gain_ref, shift_ref, w_in_ref, w_in_far_ref, b_in_ref,
    w_back_ref, w_back_far_ref, xhat_ref, scale_ref, low_ref, hidden_ref, slope_ref, next_ref,
):
    first = x_ref[0].astype(jnp.float32) + (part_ref[...] + other_ref[...] + b_out_ref[...])
    xhat, scale = norm_parts(first)
    low = (xhat * gain_ref[...] + shift_ref[...]).astype(jnp.bfloat16)
    xhat_ref[...] = xhat
    scale_ref[...] = scale
    low_ref[...] = low
    units = w_in_ref.shape[1]
    total = None
    for side, (into, back) in enumerate(((w_in_ref, w_back_ref), (w_in_far_ref, w_back_far_ref))):
        at = slice(side * units, (side + 1) * units)
        pre = mm(low, into[...]) + b_in_ref[side : side + 1]
        cdf = 0.5 * (1.0 + lax.erf(pre * math.sqrt(0.5)))
        hidden = (pre * cdf).astype(jnp.bfloat16)
        hidden_ref[:, at] = hidden
        slope_ref[:, at] = cdf + pre * (jnp.exp(-0.5 * pre * pre) * (1.0 / math.sqrt(2.0 * math.pi)))
        product = mm(hidden, back[...])
        total = product if total is None else total + product
    next_ref[...] = total


def feed_back_kernel(
    scalars_ref, cot_ref, part_ref, other_ref, xhat_ref, slope_ref, gain_one_ref, shift_one_ref, b_back_ref,
    gain_ref, shift_ref, w_in_ref, w_in_far_ref, w_back_ref, w_back_far_ref,
    next_ref, second_ref, feed_ref, pre_ref, out_ref, sums_ref, sums_in_ref,
):
    normed = xhat_ref[...] * gain_one_ref[...] + shift_one_ref[...]
    second = normed + (part_ref[...] + other_ref[...] + b_back_ref[...])
    xhat, scale = norm_parts(second)
    out_ref[...] = xhat * gain_ref[...] + shift_ref[...]
    grad = cot_ref[0].astype(jnp.float32)
    d_second = norm_back(grad, gain_ref[...], xhat, scale)
    second_ref[...] = d_second
    d_feed = d_second.astype(jnp.bfloat16)
    feed_ref[...] = d_feed
    sums_ref[0:1] = column_sum(d_feed)
    sums_ref[1:2] = column_sum(grad * xhat)
    sums_ref[2:3] = column_sum(grad)
    units = w_in_ref.shape[1]
    total = None
    for side, (into, back) in enumerate(((w_in_ref, w_back_ref), (w_in_far_ref, w_back_far_ref))):
        at = slice(side * units, (side + 1) * units)
        d_pre = (mm_nt(d_feed, back[...]) * slope_ref[:, at]).astype(jnp.bfloat16)
        pre_ref[:, at] = d_pre
        sums_in_ref[side : side + 1] = column_sum(d_pre)
        product = mm_nt(d_pre, into[...])
        total = product if total is None else total + product
    next_ref[...] = total


def without(kernel, first, count):
    def call(*refs):
        return kernel(*refs[:first], *refs[first + count :])

    return call


def on_chunk(kernel, name, chunk, scalars, pages_array, rows, arrays, shapes, before=()):
    length, width = pages_array.shape[1:]

    def rows_of(array):
        if array.shape[0] == length and len(array.shape) == 2:
            return pl.BlockSpec((rows, array.shape[1]), lambda i, s: (chunk, 0))
        return pl.BlockSpec(array.shape, lambda i, s: (0,) * len(array.shape))

    inputs = 2 + len(arrays)
    return pl.pallas_call(
        without(kernel, inputs, len(before)),
        out_shape=shapes,
        grid_spec=pltpu.PrefetchScalarGridSpec(
            num_scalar_prefetch=1,
            grid=(1,),
            in_specs=[pl.BlockSpec((1, rows, width), lambda i, s: (s[0], chunk, 0))]
            + [rows_of(array) for array in arrays]
            + [pl.BlockSpec(memory_space=pl.ANY)] * len(before),
            out_specs=[rows_of(shape) for shape in shapes],
        ),
        input_output_aliases={inputs + index: index for index in range(len(before))},
        compiler_params=pltpu.CompilerParams(vmem_limit_bytes=48 << 20),
        cost_estimate=pl.CostEstimate(
            flops=16 * rows * width * width, transcendentals=2 * rows * width, bytes_accessed=40 * rows * width
        ),
        name=name,
    )(scalars, pages_array, *arrays, *before)


def feed_grads_kernel(count, low_ref, pre_ref, hidden_ref, feed_ref, out_ref):
    rows = out_ref.shape[2]

    def put(left, right):
        product = mm_tn(left[...], right[...])
        for block in range(count):
            out_ref[block, 0] = product[block * rows : (block + 1) * rows]

    @pl.when(pl.program_id(0) % 2 == 0)
    def _():
        put(low_ref, pre_ref)

    @pl.when(pl.program_id(0) % 2 == 1)
    def _():
        put(hidden_ref, feed_ref)


def feed_grads(count, low, d_pre, hidden, d_feed):
    length, width = low.shape
    units = hidden.shape[1] // 2
    return pl.pallas_call(
        partial(feed_grads_kernel, count),
        out_shape=pltpu.HBM((count, 4, width // count, units), jnp.float32),
        grid_spec=pl.GridSpec(
            grid=(4,),
            in_specs=[
                pl.BlockSpec((length, width), lambda i: (0, 0)),
                pl.BlockSpec((length, units), lambda i: (0, i // 2)),
                pl.BlockSpec((length, units), lambda i: (0, i // 2)),
                pl.BlockSpec((length, width), lambda i: (0, 0)),
            ],
            out_specs=pl.BlockSpec((count, 1, width // count, units), lambda i: (0, i, 0, 0)),
        ),
        compiler_params=pltpu.CompilerParams(vmem_limit_bytes=40 << 20),
        cost_estimate=pl.CostEstimate(
            flops=8 * length * width * units, transcendentals=0, bytes_accessed=16 * width * units
        ),
        name="feed_grads",
    )(low, d_pre, hidden, d_feed)


def weight_grads(count, group, x_ref, pos_ref, d_ref, db_ref, mixed_ref, far_ref, vec_ref, keep_ref, send_ref):
    columns = mixed_ref.shape[0]
    rows = columns // count
    odd = group & 1
    extra = vec_ref.shape[1]
    side_rows = 6 * rows + extra
    mixed = jnp.concatenate([mixed_ref[...], far_ref[...]], axis=0)
    rights = [x_ref] * 3 + [pos_ref] * 2 + [db_ref]

    def put(block, at, value):
        place = (block ^ group) >> 1

        @pl.when(odd == (block & 1))
        def _():
            keep_ref[place, at] = value

        @pl.when(odd != (block & 1))
        def _():
            send_ref[place, at] = value

    for part, right in enumerate(rights):
        product = mm(d_ref[part] if part < 5 else mixed, right[...])
        for block in range(count):
            for side in range(2):
                start = side * columns + block * rows
                at = side * side_rows + part * rows
                put(block, slice(at, at + rows), product[start : start + rows])
    for block in range(count):
        for side in range(2):
            at = slice(side * side_rows + 6 * rows, (side + 1) * side_rows)
            put(block, at, vec_ref[side] if block == 0 else jnp.zeros(vec_ref.shape[1:], jnp.float32))


def attend_back_kernel(
    heads, count, scalars_ref, lengths_ref, part_ref, other_ref, second_ref, xhat_ref, scale_ref, gain_ref, w_out_ref, w_out_far_ref, own_ref, wqkv_ref, blocks_ref, x_ref, pos_ref, mixed_ref, mixed_far_ref, more_ref,
    send_ref, base_ref, keep_ref, give_ref, d_ref, branch_ref, dm_ref, first_ref, proj_ref, wfar_ref, vec_ref,
):
    page, low = scalars_ref[0], scalars_ref[1]
    length = lengths_ref[page]
    factor = 1.0 / math.sqrt(3.0 * HEAD_DIM)
    columns = heads * HEAD_DIM
    half = part_ref.shape[0] // 2
    block_rows = blocks_ref.shape[3]
    for part in range(5):
        for block in range(count):
            at = slice(block * block_rows, (block + 1) * block_rows)
            wfar_ref[part, at] = blocks_ref[0, block, part]
        weight = wfar_ref[part].astype(jnp.bfloat16)
        left = x_ref if part < 3 else pos_ref
        proj_ref[part, columns:] = mm_nt(weight, left[...]).astype(jnp.bfloat16)
        proj_ref[part, :columns] = own_ref[part]
    sums = None
    for index in range(2):
        at = slice(index * half, (index + 1) * half)
        xhat = xhat_ref[at]
        d_normed = second_ref[at] + (part_ref[at] + other_ref[at])
        d_first = norm_back(d_normed, gain_ref[...], xhat, scale_ref[at])
        first_ref[at] = d_first
        d_branch = d_first.astype(jnp.bfloat16)
        branch_ref[at] = d_branch
        some = (column_sum(d_branch), column_sum(d_normed * xhat), column_sum(d_normed))
        sums = some if sums is None else tuple(x + y for x, y in zip(sums, some))
        dm_ref[:columns, at] = mm_nt(w_out_ref[...], d_branch).astype(jnp.bfloat16)
        dm_ref[columns:, at] = mm_nt(w_out_far_ref[...], d_branch).astype(jnp.bfloat16)
    for side in range(2):
        for index, value in enumerate(sums):
            vec_ref[side, index : index + 1] = value
        vec_ref[side, len(sums) :] = more_ref[side]

    def one_head(head, _):
        at = rows_at(head)
        q, k, v, pq, pk = [proj_ref[part, at] for part in range(5)]
        dm = dm_ref[at]
        probs = probs_t(q, k, pq, pk, length, factor)
        weights = probs.astype(jnp.bfloat16)
        d_values = mm(weights, dm.T)
        d_probs = mm_tn(v, dm)
        inner = jnp.sum(d_probs * probs, axis=0, keepdims=True)
        d_scores = (probs * (d_probs - inner)).astype(jnp.bfloat16)
        by_queries = mm(d_scores, jnp.concatenate([q, pq], axis=0).T).T
        by_query, by_pos_query = by_queries[:HEAD_DIM], by_queries[HEAD_DIM:]
        by_keys = mm(jnp.concatenate([k, pk], axis=0), d_scores)
        by_key, by_pos_key = by_keys[:HEAD_DIM], by_keys[HEAD_DIM:]
        grads = (
            (by_key + by_pos_key) * factor,
            (by_query + by_pos_query) * factor,
            d_values.T,
            by_key * factor,
            by_query * factor,
        )
        for part, value in enumerate(grads):
            d_ref[part, at] = value.astype(jnp.bfloat16)
        return 0

    lax.fori_loop(0, 2 * heads, one_head, 0)
    for part in range(3):
        for side in range(2):
            at = slice(side * columns, (side + 1) * columns)
            weight = wqkv_ref[part] if side == 0 else wfar_ref[part].astype(jnp.bfloat16)
            first_ref_part = mm_tn(d_ref[part, at], weight)
            if part == side == 0:
                total = first_ref_part
            else:
                total = total + first_ref_part
    upper, lower = total[:half], total[half:]
    send_ref[...] = jnp.where(low == 0, lower, upper)
    base_ref[...] = jnp.where(low == 0, upper + first_ref[:half], lower + first_ref[half:])
    weight_grads(
        count, scalars_ref[2], x_ref, pos_ref, d_ref, branch_ref, mixed_ref, mixed_far_ref, vec_ref, keep_ref, give_ref
    )


def attend_back(count, scalars, lengths, arrays):
    proj = arrays[8]
    parts, columns, length = proj.shape
    half, width = length // 2, arrays[0].shape[1]
    heads = columns // HEAD_DIM
    whole = lambda shape: pl.BlockSpec(shape, lambda i, s, n: (0,) * len(shape))
    shapes = (
        jax.ShapeDtypeStruct((half, width), jnp.float32),
        jax.ShapeDtypeStruct((half, width), jnp.float32),
    ) + 2 * (jax.ShapeDtypeStruct((count // 2, 2 * (6 * (columns // count) + 8), width), jnp.float32),)
    return pl.pallas_call(
        partial(attend_back_kernel, heads, count),
        out_shape=shapes,
        grid_spec=pltpu.PrefetchScalarGridSpec(
            num_scalar_prefetch=2,
            grid=(1,),
            in_specs=[
                whole(array.shape)
                if len(array.shape) < 5
                else pl.BlockSpec((1,) + array.shape[1:], lambda i, s, n: (0, 0, 0, 0, 0))
                for array in arrays
            ],
            out_specs=[whole(shape.shape) for shape in shapes],
            scratch_shapes=[
                pltpu.VMEM((parts, 2 * columns, length), jnp.bfloat16),
                pltpu.VMEM((length, width), jnp.bfloat16),
                pltpu.VMEM((2 * columns, length), jnp.bfloat16),
                pltpu.VMEM((length, width), jnp.float32),
                pltpu.VMEM((parts, 2 * columns, length), jnp.bfloat16),
                pltpu.VMEM((parts, columns, width), jnp.float32),
                pltpu.VMEM((2, 8, width), jnp.float32),
            ],
        ),
        compiler_params=pltpu.CompilerParams(vmem_limit_bytes=58 << 20),
        cost_estimate=pl.CostEstimate(
            flops=2 * 2 * heads * length * length * HEAD_DIM * 9 + 20 * length * width * columns,
            transcendentals=2 * heads * length * length,
            bytes_accessed=40 * length * width,
        ),
        name="attend_back",
    )(scalars, lengths, *arrays)


def spread_kernel(scalars_ref, *refs):
    *pieces, out_ref = refs
    if len(pieces) == 3:
        pieces = [pieces[0], pieces[1], pieces[2].at[0], pieces[2].at[1]]
    mine_ref, far_ref, rest_mine_ref, rest_far_ref = pieces
    for step, ref in enumerate((mine_ref, rest_mine_ref, far_ref, rest_far_ref)):

        @pl.when(pl.program_id(0) == step)
        def _():
            out_ref[0] = ref[...].astype(out_ref.dtype)


def spread(scalars, pieces, kind):
    half, width = pieces[0].shape
    return pl.pallas_call(
        spread_kernel,
        out_shape=pltpu.HBM((2, 2 * half, width), kind),
        grid_spec=pltpu.PrefetchScalarGridSpec(
            num_scalar_prefetch=1,
            grid=(4,),
            in_specs=[pl.BlockSpec(memory_space=pltpu.VMEM)] * len(pieces),
            out_specs=pl.BlockSpec((1, half, width), lambda i, s: (s[0] ^ (i // 2), s[1] ^ (i % 2), 0)),
        ),
        compiler_params=pltpu.CompilerParams(vmem_limit_bytes=16 << 20),
        cost_estimate=pl.CostEstimate(flops=0, transcendentals=0, bytes_accessed=32 * half * width),
        name="spread",
    )(scalars, *pieces)


def split_blocks_kernel(in_ref, first_ref, second_ref):
    count, both, _ = in_ref.shape
    rows = both // 2
    for block in range(count):
        at = slice(block * rows, (block + 1) * rows)
        first_ref[at] = in_ref[block, :rows]
        second_ref[at] = in_ref[block, rows:]


def split_blocks(blocks):
    count, both, width = blocks.shape
    lanes = width // 3 if width % 384 == 0 else width
    shape = pltpu.HBM((count * both // 2, width), blocks.dtype)
    out_spec = pl.BlockSpec((count * both // 2, lanes), lambda i: (0, i))
    return pl.pallas_call(
        split_blocks_kernel,
        out_shape=(shape, shape),
        grid_spec=pl.GridSpec(
            grid=(width // lanes,),
            in_specs=[pl.BlockSpec((count, both, lanes), lambda i: (0, 0, i))],
            out_specs=[out_spec, out_spec],
        ),
        compiler_params=pltpu.CompilerParams(vmem_limit_bytes=24 << 20),
        cost_estimate=pl.CostEstimate(flops=0, transcendentals=0, bytes_accessed=8 * blocks.size),
        name="split_blocks",
    )(blocks)


def place_grads_kernel(
    order, scalars_ref, low_a_ref, low_b_ref, high_a_ref, high_b_ref, qkv_ref, pos_ref, out_ref, vec_ref
):
    group = scalars_ref[0]
    count = 2 * low_a_ref.shape[0]
    rows = qkv_ref.shape[1] // count
    cut = low_a_ref.shape[1]

    def read(place, start, stop):
        upper = (place & 1) == 1
        index = place >> 1
        pieces = []
        if start < cut:
            at = slice(start, min(stop, cut))
            pieces.append(jnp.where(upper, high_a_ref[index, at], low_a_ref[index, at]))
        if stop > cut:
            at = slice(max(start, cut) - cut, stop - cut)
            turned_index = 0
            for bit in range(len(order)):
                turned_index = turned_index | (((index >> bit) & 1) << order[bit])
            pieces.append(jnp.where(upper, high_b_ref[turned_index, at], low_b_ref[turned_index, at]))
        return jnp.concatenate(pieces, axis=0) if len(pieces) > 1 else pieces[0]

    for block in range(count):
        place = block ^ group
        at = slice(block * rows, (block + 1) * rows)
        for part in range(6):
            value = read(place, part * rows, (part + 1) * rows)
            if part < 3:
                qkv_ref[part, at] = value
            elif part < 5:
                pos_ref[part - 3, at] = value
            else:
                out_ref[at] = value
        if block == 0:
            vec_ref[...] = read(place, 6 * rows, cut + low_b_ref.shape[1])


def place_grads(scalars, parts, columns, vec_rows):
    width = parts[0].shape[2]
    bits = parts[0].shape[0].bit_length() - 1
    whole = lambda shape: pl.BlockSpec(shape, lambda i: (0,) * len(shape))
    shapes = (
        jax.ShapeDtypeStruct((3, columns, width), jnp.float32),
        jax.ShapeDtypeStruct((2, columns, width), jnp.float32),
        jax.ShapeDtypeStruct((columns, width), jnp.float32),
        jax.ShapeDtypeStruct((vec_rows, width), jnp.float32),
    )
    return pl.pallas_call(
        partial(place_grads_kernel, tuple(range(bits))[::-1]),
        out_shape=shapes,
        grid_spec=pl.GridSpec(
            grid=(1,),
            in_specs=[pl.BlockSpec(memory_space=pltpu.SMEM)] + [whole(part.shape) for part in parts],
            out_specs=[whole(shape.shape) for shape in shapes],
        ),
        compiler_params=pltpu.CompilerParams(vmem_limit_bytes=40 << 20),
        cost_estimate=pl.CostEstimate(
            flops=0, transcendentals=0, bytes_accessed=32 * width * columns * 3
        ),
        name="place_grads",
    )(scalars, *parts)


def body(
    dp_size,
    mp_size,
    tokens,
    lengths,
    coords,
    w_qkv,
    w_pos,
    w_out,
    b_out,
    gain_one,
    shift_one,
    w_in,
    b_in,
    w_back,
    b_back,
    gain_two,
    shift_two,
    cotangent,
):
    pages, length, width = tokens.shape
    columns = w_qkv.shape[2]
    units = w_in.shape[1]
    here = lax.axis_index(MP)
    low = here & 1
    page = here >> 1
    group = lax.axis_index("dp")
    f32, bf16 = jnp.float32, jnp.bfloat16
    half = length // 2
    one = jnp.where(lengths[0] > 0, 1.0, 0.0).astype(f32)

    def arrived(value):
        return value * one

    def swap(value, bit):
        pairs = [(i, i ^ bit) for i in range(mp_size)]
        return lax.ppermute(value, MP, pairs)

    def group_swap(value, bit):
        pairs = [(i, i ^ bit) for i in range(dp_size)]
        return lax.ppermute(value, "dp", pairs)

    def my_rows(value):
        rows = value.shape[0] // dp_size
        return lax.dynamic_slice_in_dim(value, group * rows, rows, 0)

    def gather(value):
        return lax.all_gather(value, "dp", axis=0, tiled=True)

    def take(value, index):
        return lax.dynamic_index_in_dim(value, index, 0, keepdims=False)

    def after(value, *others):
        return lax.optimization_barrier((value,) + others)[0]

    def row(value):
        return value.reshape(1, -1)

    chunk_rows = lambda value: [value[:half], value[half:]]

    turn = lambda value: jnp.swapaxes(value, 1, 2)
    w_qkv, w_pos = turn(w_qkv), turn(w_pos)
    out_rows = swap(my_rows(w_out).astype(f32), FAR)
    out_rows = jnp.pad(out_rows, ((0, max(0, 48 - out_rows.shape[0])), (0, 0)))
    unit_rows = jnp.concatenate([my_rows(w_in), my_rows(w_back)], axis=0).astype(f32)
    tail = jnp.concatenate([row(b_in), jnp.zeros((7, units), f32)], axis=0)
    far_rows = swap(jnp.concatenate([unit_rows, tail], axis=0), FAR)
    count = columns // dp_size

    table = jnp.asarray(angle_tables(width))
    scalars = jnp.stack([page, low])
    mixed_send, mixed, proj, pos_rows = attend(scalars, lengths, tokens, coords, table, w_qkv, w_pos)
    w_out_far = gather(out_rows).reshape(dp_size, -1, width)[:, : columns // dp_size]
    w_out_far = arrived(w_out_far.reshape(columns, width)).astype(bf16)
    mixed_far = swap(mixed_send, FAR)
    far_rows = after(far_rows, mixed_send)
    count = unit_rows.shape[0]
    b_in_two = jnp.stack([b_in, far_rows[count]])
    blocks = arrived(gather(far_rows[:count])).reshape(dp_size, count, -1)
    in_rows = width // dp_size
    w_in_far = blocks[:, :in_rows].reshape(width, units).astype(bf16)
    w_back_far = blocks[:, in_rows:].reshape(units, width).astype(bf16)

    mixed_far = arrived(mixed_far).astype(bf16)
    part = mm_tn(jnp.concatenate([mixed, mixed_far], axis=0), jnp.concatenate([w_out, w_out_far], axis=0))
    other = swap(part, NEAR)
    head_rows = jnp.concatenate([w_qkv, w_pos], axis=0)
    count = columns // dp_size
    head_rows = lax.dynamic_slice_in_dim(after(head_rows, part), group * count, count, 1)
    blocks = gather(swap(head_rows.astype(f32), FAR).reshape(-1, width))
    blocks = blocks.reshape(1, dp_size, 5, count, width)

    rows_f32 = jax.ShapeDtypeStruct((length, width), f32)
    rows_low = jax.ShapeDtypeStruct((length, width), bf16)
    units_f32 = jax.ShapeDtypeStruct((length, 2 * units), f32)
    units_low = jax.ShapeDtypeStruct((length, 2 * units), bf16)
    chunk_f32 = jax.ShapeDtypeStruct((half, width), f32)
    scale_of = jax.ShapeDtypeStruct((length, 1), f32)
    shapes = (rows_f32, scale_of, rows_low, units_low, units_f32, chunk_f32)
    arrays = [part, other, row(b_out), row(gain_one), row(shift_one)]
    arrays += [w_in, w_in_far, b_in_two, w_back, w_back_far]
    part, other = [], []
    fed = ()
    for index in range(2):
        *fed, product = on_chunk(
            feed_kernel, "feed", index, scalars, tokens, half, arrays, shapes, tuple(fed)
        )
        part.append(product)
        other.append(swap(product, NEAR))
    xhat_one, scale_one, normed_low, hidden, slope = fed
    shapes = (rows_f32, rows_f32, rows_low, units_low, rows_f32)
    shapes += (jax.ShapeDtypeStruct((3, width), f32), jax.ShapeDtypeStruct((2, units), f32))
    back, sums_two, sums_in = (), [], []
    for index in range(2):
        arrays = [part[index], other[index], xhat_one, slope, row(gain_one), row(shift_one)]
        arrays += [row(b_back), row(gain_two), row(shift_two), w_in, w_in_far, w_back, w_back_far]
        *back, some, some_in = on_chunk(
            feed_back_kernel, "feed_back", index, scalars, cotangent, half, arrays, shapes, tuple(back)
        )
        sums_two.append(some)
        sums_in.append(some_in)
    part, d_second, d_feed, d_pre, output = back
    other = swap(part, NEAR)

    ffn = feed_grads(dp_size, normed_low, d_pre, hidden, d_feed)
    ffn = lax.psum_scatter(ffn.reshape(-1, units), "dp", scatter_dimension=0, tiled=True)

    rows = take(tokens, page)
    arrays = [part, other, d_second, xhat_one, scale_one]
    arrays += [row(gain_one), w_out, w_out_far]
    vectors = sums_two[0] + sums_two[1]
    d_b_in = sums_in[0] + sums_in[1]
    spare = jnp.zeros((1, width), f32)
    vectors = jnp.stack(
        [jnp.concatenate([vectors, d_b_in[side : side + 1], spare], axis=0) for side in range(2)]
    )
    arrays += [proj, w_qkv, blocks, rows, pos_rows, mixed, mixed_far, vectors]
    send, base, keep, give = attend_back(dp_size, jnp.stack([page, low, group]), lengths, arrays)

    half_of = lambda value, index: lax.dynamic_slice_in_dim(value, index * half, half, 0)
    out_mine = half_of(output, low)
    out_far = swap(after(out_mine, other), FAR)

    bits = [1 << k for k in range(dp_size.bit_length() - 1)]
    give = after(give, out_far)
    near_sum = swap(send, NEAR)
    mine = base + near_sum

    group_scalar = jnp.reshape(group, (1,))
    out_turned = swap(out_far, NEAR)
    ffn_rows = ffn.shape[0] // 2
    crossed = swap(jnp.concatenate([mine, ffn[ffn_rows:]], axis=0), FAR)
    ffn = ffn[:ffn_rows] + crossed[half:]
    far_mine = crossed[:half]
    total = keep + group_swap(give, bits[0])
    more = bits[1:]

    def after_all(*values):
        return lax.optimization_barrier(values)

    cut = total.shape[1] // 2
    upper, lower = total[:, :cut], total[:, cut:]
    for step in range(len(more)):
        upper = upper.reshape((-1, 2) + upper.shape[1:])
        lower = lower.reshape((2, -1) + lower.shape[1:])
        give_upper, give_lower = after_all(upper[:, 1], lower[1], *([out_turned] if step else []))[:2]
        got_upper = group_swap(give_upper, more[step])
        got_lower = group_swap(give_lower, more[-1 - step])
        upper = upper[:, 0] + got_upper
        lower = lower[0] + got_lower
    upper, lower = upper[0], lower[0]
    far_sum = swap(after(lower, crossed), FAR)
    ffn = after(ffn, got_upper, got_lower)

    rest = swap(after(jnp.stack([mine, far_mine]), far_sum), NEAR)
    grad_tokens = spread(scalars, (mine, far_mine, rest), f32)
    out_rest = half_of(output, 1 - low)
    layer_out = spread(scalars, (out_mine, out_far, out_rest, after(out_turned, far_sum)), bf16)
    total = upper + far_sum
    cut = total.shape[0] // 16 * 8
    upper, lower = total[None, :cut], total[None, cut:]
    for step in range(len(more)):
        if step:
            upper, lower = after_all(upper, lower, layer_out)[:2]
        got_upper = group_swap(upper, more[step])
        got_lower = group_swap(lower, more[-1 - step])
        upper = jnp.concatenate([upper, got_upper], axis=0)
        lower = jnp.concatenate([lower, got_lower], axis=0)
    grad_w_in, grad_w_back = split_blocks(gather(ffn).reshape(dp_size, ffn_rows, units))
    upper, lower = after_all(upper, lower, rest, grad_w_in)[:2]
    parts = [upper, lower, group_swap(upper, bits[0]), group_swap(lower, bits[0])]
    grad_w_qkv, grad_w_pos, grad_w_out, vectors = place_grads(group_scalar, parts, columns, 8)
    grad_w_qkv, grad_w_pos = turn(grad_w_qkv), turn(grad_w_pos)
    grad_b_out, grad_gain_one, grad_shift_one = vectors[0], vectors[1], vectors[2]
    grad_b_back, grad_gain_two, grad_shift_two = vectors[3], vectors[4], vectors[5]
    grad_b_in = vectors[6]

    return (
        layer_out,
        grad_tokens,
        grad_w_qkv,
        grad_w_pos,
        grad_w_out,
        grad_b_out,
        grad_gain_one,
        grad_shift_one,
        grad_w_in,
        grad_b_in,
        grad_w_back,
        grad_b_back,
        grad_gain_two,
        grad_shift_two,
    )


def solution(mesh):
    mp_size = mesh.shape["mp"]
    dp_size = mesh.devices.size // mp_size
    split = jax.sharding.Mesh(mesh.devices.reshape(dp_size, mp_size // 2, 2), ("dp",) + MP)
    placed = (
        P("dp", None, None),
        P("dp"),
        P("dp", None, None),
        P(None, None, MP),
        P(None, None, MP),
        P(MP, None),
        P(),
        P(),
        P(),
        P(None, MP),
        P(MP),
        P(MP, None),
        P(),
        P(),
        P(),
        P("dp", None, None),
    )
    return jax.shard_map(
        partial(body, dp_size, mp_size),
        mesh=split,
        in_specs=placed,
        out_specs=(
            P("dp", None, None),
            P("dp", None, None),
            P(None, None, MP),
            P(None, None, MP),
            P(MP, None),
            P(),
            P(),
            P(),
            P(None, MP),
            P(MP),
            P(MP, None),
            P(),
            P(),
            P(),
        ),
        check_vma=False,
    )
```

```python
from functools import partial
import math

import jax
import jax.numpy as jnp
import numpy as np
from jax import lax
from jax.experimental import pallas as pl
from jax.experimental.pallas import tpu as pltpu
from jax.sharding import PartitionSpec as P

HEAD_DIM = 64
STEP_BITS = 5
STEP = 1 << STEP_BITS
NEAR = 1
MP = ("far", "near")
FAR = 2
MASKED = -1e30


def mm(left, right):
    return jnp.dot(left, right, preferred_element_type=jnp.float32)


def mm_nt(left, right):
    return lax.dot_general(
        left, right, (((1,), (1,)), ((), ())), preferred_element_type=jnp.float32
    )


def mm_tn(left, right):
    return lax.dot_general(
        left, right, (((0,), (0,)), ((), ())), preferred_element_type=jnp.float32
    )


def angle_tables(model_width):
    quarter = model_width // 4
    rate = np.exp(np.arange(quarter) * (-math.log(10000.0) / quarter))
    fine = np.arange(STEP)[:, None] * rate
    coarse = fine * STEP
    zero = np.zeros((STEP, 2 * quarter))
    table = np.concatenate(
        [
            np.concatenate([np.sin(coarse), np.cos(coarse), zero], axis=1),
            np.concatenate([zero, np.sin(fine), np.cos(fine)], axis=1),
        ],
        axis=0,
    )
    parts = []
    rest = table
    for _ in range(3):
        part = rest.astype(jnp.bfloat16)
        parts.append(part)
        rest = rest - part.astype(np.float64)
    return np.concatenate(parts, axis=0)


def sinusoid(coord, table_ref):
    quarter = table_ref.shape[1] // 4
    slot = lax.broadcasted_iota(jnp.int32, (2 * STEP, coord.shape[1]), 0)
    coarse = coord >> STEP_BITS
    fine = (coord & (STEP - 1)) + STEP
    hit = ((slot == coarse) | (slot == fine)).astype(jnp.float32).astype(jnp.bfloat16)
    looked = mm_tn(jnp.concatenate([hit, hit, hit], axis=0), table_ref[...])
    sin_a, cos_a, sin_b, cos_b = [looked[:, k * quarter : (k + 1) * quarter] for k in range(4)]
    return jnp.concatenate([sin_a * cos_b + cos_a * sin_b, cos_a * cos_b - sin_a * sin_b], axis=1)


def probs_t(q, k, pq, pk, length, factor):
    left = jnp.concatenate([k, pk, k], axis=0)
    right = jnp.concatenate([q, q, pq], axis=0)
    scores = mm_tn(left, right) * factor
    visible = lax.broadcasted_iota(jnp.int32, scores.shape, 0) < length
    scores = jnp.where(visible, scores, MASKED)
    raised = jnp.exp(scores - jnp.max(scores, axis=0, keepdims=True))
    return raised * (1.0 / jnp.sum(raised, axis=0, keepdims=True))


def rows_at(head):
    return pl.ds(pl.multiple_of(head * HEAD_DIM, HEAD_DIM), HEAD_DIM)


def attend_kernel(
    heads, scalars_ref, lengths_ref, x_ref, coords_ref, table_ref, wqkv_ref, wpos_ref,
    send_ref, own_ref, proj_ref, pos_ref,
):
    step = pl.program_id(0)
    length = lengths_ref[scalars_ref[0] ^ (1 - step)]
    factor = 1.0 / math.sqrt(3.0 * HEAD_DIM)
    rows = x_ref[0]
    for part in range(3):
        proj_ref[part] = mm_nt(wqkv_ref[part], rows).astype(jnp.bfloat16)
    sides = [sinusoid(coords_ref[0, axis : axis + 1], table_ref) for axis in range(2)]
    position = jnp.concatenate(sides, axis=1).astype(jnp.bfloat16)
    pos_ref[...] = position
    for part in range(2):
        proj_ref[3 + part] = mm_nt(wpos_ref[part], position).astype(jnp.bfloat16)

    def one_head(head, _):
        at = rows_at(head)
        q, k, v, pq, pk = [proj_ref[part, at] for part in range(5)]
        weights = probs_t(q, k, pq, pk, length, factor).astype(jnp.bfloat16)
        mixed = mm(v, weights).astype(jnp.bfloat16)

        @pl.when(step == 0)
        def _():
            send_ref[at] = mixed.astype(jnp.float32)

        @pl.when(step == 1)
        def _():
            own_ref[at] = mixed

        return 0

    lax.fori_loop(0, heads, one_head, 0)


def attend(scalars, lengths, tokens, coords, table, w_qkv, w_pos):
    pages, length, width = tokens.shape
    columns = w_qkv.shape[1]
    whole = lambda shape: pl.BlockSpec(shape, lambda i, s, n: (0,) * len(shape))
    shapes = (
        jax.ShapeDtypeStruct((columns, length), jnp.float32),
        jax.ShapeDtypeStruct((columns, length), jnp.bfloat16),
        jax.ShapeDtypeStruct((5, columns, length), jnp.bfloat16),
        jax.ShapeDtypeStruct((length, width), jnp.bfloat16),
    )
    page = lambda i, s, n: (s[0] ^ (1 - i), 0, 0)
    return pl.pallas_call(
        partial(attend_kernel, columns // HEAD_DIM),
        out_shape=shapes,
        grid_spec=pltpu.PrefetchScalarGridSpec(
            num_scalar_prefetch=2,
            grid=(pages,),
            in_specs=[
                pl.BlockSpec((1, length, width), page),
                pl.BlockSpec((1,) + coords.shape[1:], page),
                whole(table.shape),
                whole(w_qkv.shape),
                whole(w_pos.shape),
            ],
            out_specs=[whole(shape.shape) for shape in shapes],
        ),
        compiler_params=pltpu.CompilerParams(vmem_limit_bytes=40 << 20),
        cost_estimate=pl.CostEstimate(
            flops=2 * pages * length * columns * (5 * width + 4 * length),
            transcendentals=pages * length * length * columns // HEAD_DIM,
            bytes_accessed=pages * length * (4 * width + 14 * columns),
        ),
        name="attend",
    )(scalars, lengths, tokens, coords, table, w_qkv, w_pos)


def norm_parts(values):
    center = values - jnp.mean(values, axis=-1, keepdims=True)
    spread = jnp.mean(center * center, axis=-1, keepdims=True)
    scale = lax.rsqrt(spread + 1e-05)
    return center * scale, scale


def norm_back(grad, gain, xhat, scale):
    up = grad * gain
    mean = jnp.mean(up, axis=-1, keepdims=True)
    along = jnp.mean(up * xhat, axis=-1, keepdims=True)
    return scale * (up - mean - xhat * along)


def column_sum(values):
    return jnp.sum(values.astype(jnp.float32), axis=0, keepdims=True)


def feed_kernel(
    scalars_ref, x_ref, part_ref, other_ref, b_out_ref, gain_ref, shift_ref, w_in_ref, w_in_far_ref, b_in_ref,
    w_back_ref, w_back_far_ref, xhat_ref, scale_ref, low_ref, hidden_ref, slope_ref, next_ref,
):
    first = x_ref[0].astype(jnp.float32) + (part_ref[...] + other_ref[...] + b_out_ref[...])
    xhat, scale = norm_parts(first)
    low = (xhat * gain_ref[...] + shift_ref[...]).astype(jnp.bfloat16)
    xhat_ref[...] = xhat
    scale_ref[...] = scale
    low_ref[...] = low
    units = w_in_ref.shape[1]
    total = None
    for side, (into, back) in enumerate(((w_in_ref, w_back_ref), (w_in_far_ref, w_back_far_ref))):
        at = slice(side * units, (side + 1) * units)
        pre = mm(low, into[...]) + b_in_ref[side : side + 1]
        cdf = 0.5 * (1.0 + lax.erf(pre * math.sqrt(0.5)))
        hidden = (pre * cdf).astype(jnp.bfloat16)
        hidden_ref[:, at] = hidden
        slope_ref[:, at] = cdf + pre * (jnp.exp(-0.5 * pre * pre) * (1.0 / math.sqrt(2.0 * math.pi)))
        product = mm(hidden, back[...])
        total = product if total is None else total + product
    next_ref[...] = total


def feed_back_kernel(
    scalars_ref, cot_ref, part_ref, other_ref, xhat_ref, slope_ref, gain_one_ref, shift_one_ref, b_back_ref,
    gain_ref, shift_ref, w_in_ref, w_in_far_ref, w_back_ref, w_back_far_ref,
    next_ref, second_ref, feed_ref, pre_ref, out_ref, sums_ref, sums_in_ref,
):
    normed = xhat_ref[...] * gain_one_ref[...] + shift_one_ref[...]
    second = normed + (part_ref[...] + other_ref[...] + b_back_ref[...])
    xhat, scale = norm_parts(second)
    out_ref[...] = xhat * gain_ref[...] + shift_ref[...]
    grad = cot_ref[0].astype(jnp.float32)
    d_second = norm_back(grad, gain_ref[...], xhat, scale)
    second_ref[...] = d_second
    d_feed = d_second.astype(jnp.bfloat16)
    feed_ref[...] = d_feed
    sums_ref[0:1] = column_sum(d_feed)
    sums_ref[1:2] = column_sum(grad * xhat)
    sums_ref[2:3] = column_sum(grad)
    units = w_in_ref.shape[1]
    total = None
    for side, (into, back) in enumerate(((w_in_ref, w_back_ref), (w_in_far_ref, w_back_far_ref))):
        at = slice(side * units, (side + 1) * units)
        d_pre = (mm_nt(d_feed, back[...]) * slope_ref[:, at]).astype(jnp.bfloat16)
        pre_ref[:, at] = d_pre
        sums_in_ref[side : side + 1] = column_sum(d_pre)
        product = mm_nt(d_pre, into[...])
        total = product if total is None else total + product
    next_ref[...] = total


def without(kernel, first, count):
    def call(*refs):
        return kernel(*refs[:first], *refs[first + count :])

    return call


def on_chunk(kernel, name, chunk, scalars, pages_array, rows, arrays, shapes, before=()):
    length, width = pages_array.shape[1:]

    def rows_of(array):
        if array.shape[0] == length and len(array.shape) == 2:
            return pl.BlockSpec((rows, array.shape[1]), lambda i, s: (chunk, 0))
        return pl.BlockSpec(array.shape, lambda i, s: (0,) * len(array.shape))

    inputs = 2 + len(arrays)
    return pl.pallas_call(
        without(kernel, inputs, len(before)),
        out_shape=shapes,
        grid_spec=pltpu.PrefetchScalarGridSpec(
            num_scalar_prefetch=1,
            grid=(1,),
            in_specs=[pl.BlockSpec((1, rows, width), lambda i, s: (s[0], chunk, 0))]
            + [rows_of(array) for array in arrays]
            + [pl.BlockSpec(memory_space=pl.ANY)] * len(before),
            out_specs=[rows_of(shape) for shape in shapes],
        ),
        input_output_aliases={inputs + index: index for index in range(len(before))},
        compiler_params=pltpu.CompilerParams(vmem_limit_bytes=48 << 20),
        cost_estimate=pl.CostEstimate(
            flops=16 * rows * width * width, transcendentals=2 * rows * width, bytes_accessed=40 * rows * width
        ),
        name=name,
    )(scalars, pages_array, *arrays, *before)


def feed_grads_kernel(count, low_ref, pre_ref, hidden_ref, feed_ref, out_ref):
    rows = out_ref.shape[2]

    def put(left, right):
        product = mm_tn(left[...], right[...])
        for block in range(count):
            out_ref[block, 0] = product[block * rows : (block + 1) * rows]

    @pl.when(pl.program_id(0) % 2 == 0)
    def _():
        put(low_ref, pre_ref)

    @pl.when(pl.program_id(0) % 2 == 1)
    def _():
        put(hidden_ref, feed_ref)


def feed_grads(count, low, d_pre, hidden, d_feed):
    length, width = low.shape
    units = hidden.shape[1] // 2
    return pl.pallas_call(
        partial(feed_grads_kernel, count),
        out_shape=pltpu.HBM((count, 4, width // count, units), jnp.float32),
        grid_spec=pl.GridSpec(
            grid=(4,),
            in_specs=[
                pl.BlockSpec((length, width), lambda i: (0, 0)),
                pl.BlockSpec((length, units), lambda i: (0, i // 2)),
                pl.BlockSpec((length, units), lambda i: (0, i // 2)),
                pl.BlockSpec((length, width), lambda i: (0, 0)),
            ],
            out_specs=pl.BlockSpec((count, 1, width // count, units), lambda i: (0, i, 0, 0)),
        ),
        compiler_params=pltpu.CompilerParams(vmem_limit_bytes=40 << 20),
        cost_estimate=pl.CostEstimate(
            flops=8 * length * width * units, transcendentals=0, bytes_accessed=16 * width * units
        ),
        name="feed_grads",
    )(low, d_pre, hidden, d_feed)


def weight_grads(count, group, x_ref, pos_ref, d_ref, db_ref, mixed_ref, far_ref, vec_ref, keep_ref, send_ref):
    columns = mixed_ref.shape[0]
    rows = columns // count
    odd = group & 1
    extra = vec_ref.shape[1]
    side_rows = 6 * rows + extra
    mixed = jnp.concatenate([mixed_ref[...], far_ref[...]], axis=0)
    rights = [x_ref] * 3 + [pos_ref] * 2 + [db_ref]

    def put(block, at, value):
        place = (block ^ group) >> 1

        @pl.when(odd == (block & 1))
        def _():
            keep_ref[place, at] = value

        @pl.when(odd != (block & 1))
        def _():
            send_ref[place, at] = value

    for part, right in enumerate(rights):
        product = mm(d_ref[part] if part < 5 else mixed, right[...])
        for block in range(count):
            for side in range(2):
                start = side * columns + block * rows
                at = side * side_rows + part * rows
                put(block, slice(at, at + rows), product[start : start + rows])
    for block in range(count):
        for side in range(2):
            at = slice(side * side_rows + 6 * rows, (side + 1) * side_rows)
            put(block, at, vec_ref[side] if block == 0 else jnp.zeros(vec_ref.shape[1:], jnp.float32))


def attend_back_kernel(
    heads, count, scalars_ref, lengths_ref, part_ref, other_ref, second_ref, xhat_ref, scale_ref, gain_ref, w_out_ref, w_out_far_ref, own_ref, wqkv_ref, blocks_ref, x_ref, pos_ref, mixed_ref, mixed_far_ref, more_ref,
    send_ref, base_ref, keep_ref, give_ref, d_ref, branch_ref, dm_ref, first_ref, proj_ref, wfar_ref, vec_ref,
):
    page, low = scalars_ref[0], scalars_ref[1]
    length = lengths_ref[page]
    factor = 1.0 / math.sqrt(3.0 * HEAD_DIM)
    columns = heads * HEAD_DIM
    half = part_ref.shape[0] // 2
    block_rows = blocks_ref.shape[3]
    for part in range(5):
        for block in range(count):
            at = slice(block * block_rows, (block + 1) * block_rows)
            wfar_ref[part, at] = blocks_ref[0, block, part]
        weight = wfar_ref[part].astype(jnp.bfloat16)
        left = x_ref if part < 3 else pos_ref
        proj_ref[part, columns:] = mm_nt(weight, left[...]).astype(jnp.bfloat16)
        proj_ref[part, :columns] = own_ref[part]
    sums = None
    for index in range(2):
        at = slice(index * half, (index + 1) * half)
        xhat = xhat_ref[at]
        d_normed = second_ref[at] + (part_ref[at] + other_ref[at])
        d_first = norm_back(d_normed, gain_ref[...], xhat, scale_ref[at])
        first_ref[at] = d_first
        d_branch = d_first.astype(jnp.bfloat16)
        branch_ref[at] = d_branch
        some = (column_sum(d_branch), column_sum(d_normed * xhat), column_sum(d_normed))
        sums = some if sums is None else tuple(x + y for x, y in zip(sums, some))
        dm_ref[:columns, at] = mm_nt(w_out_ref[...], d_branch).astype(jnp.bfloat16)
        dm_ref[columns:, at] = mm_nt(w_out_far_ref[...], d_branch).astype(jnp.bfloat16)
    for side in range(2):
        for index, value in enumerate(sums):
            vec_ref[side, index : index + 1] = value
        vec_ref[side, len(sums) :] = more_ref[side]

    def one_head(head, _):
        at = rows_at(head)
        q, k, v, pq, pk = [proj_ref[part, at] for part in range(5)]
        dm = dm_ref[at]
        probs = probs_t(q, k, pq, pk, length, factor)
        weights = probs.astype(jnp.bfloat16)
        d_values = mm(weights, dm.T)
        d_probs = mm_tn(v, dm)
        inner = jnp.sum(d_probs * probs, axis=0, keepdims=True)
        d_scores = (probs * (d_probs - inner)).astype(jnp.bfloat16)
        by_queries = mm(d_scores, jnp.concatenate([q, pq], axis=0).T).T
        by_query, by_pos_query = by_queries[:HEAD_DIM], by_queries[HEAD_DIM:]
        by_keys = mm(jnp.concatenate([k, pk], axis=0), d_scores)
        by_key, by_pos_key = by_keys[:HEAD_DIM], by_keys[HEAD_DIM:]
        grads = (
            (by_key + by_pos_key) * factor,
            (by_query + by_pos_query) * factor,
            d_values.T,
            by_key * factor,
            by_query * factor,
        )
        for part, value in enumerate(grads):
            d_ref[part, at] = value.astype(jnp.bfloat16)
        return 0

    lax.fori_loop(0, 2 * heads, one_head, 0)
    for part in range(3):
        for side in range(2):
            at = slice(side * columns, (side + 1) * columns)
            weight = wqkv_ref[part] if side == 0 else wfar_ref[part].astype(jnp.bfloat16)
            first_ref_part = mm_tn(d_ref[part, at], weight)
            if part == side == 0:
                total = first_ref_part
            else:
                total = total + first_ref_part
    upper, lower = total[:half], total[half:]
    send_ref[...] = jnp.where(low == 0, lower, upper)
    base_ref[...] = jnp.where(low == 0, upper + first_ref[:half], lower + first_ref[half:])
    weight_grads(
        count, scalars_ref[2], x_ref, pos_ref, d_ref, branch_ref, mixed_ref, mixed_far_ref, vec_ref, keep_ref, give_ref
    )


def attend_back(count, scalars, lengths, arrays):
    proj = arrays[8]
    parts, columns, length = proj.shape
    half, width = length // 2, arrays[0].shape[1]
    heads = columns // HEAD_DIM
    whole = lambda shape: pl.BlockSpec(shape, lambda i, s, n: (0,) * len(shape))
    shapes = (
        jax.ShapeDtypeStruct((half, width), jnp.float32),
        jax.ShapeDtypeStruct((half, width), jnp.float32),
    ) + 2 * (jax.ShapeDtypeStruct((count // 2, 2 * (6 * (columns // count) + 8), width), jnp.float32),)
    return pl.pallas_call(
        partial(attend_back_kernel, heads, count),
        out_shape=shapes,
        grid_spec=pltpu.PrefetchScalarGridSpec(
            num_scalar_prefetch=2,
            grid=(1,),
            in_specs=[
                whole(array.shape)
                if len(array.shape) < 5
                else pl.BlockSpec((1,) + array.shape[1:], lambda i, s, n: (0, 0, 0, 0, 0))
                for array in arrays
            ],
            out_specs=[whole(shape.shape) for shape in shapes],
            scratch_shapes=[
                pltpu.VMEM((parts, 2 * columns, length), jnp.bfloat16),
                pltpu.VMEM((length, width), jnp.bfloat16),
                pltpu.VMEM((2 * columns, length), jnp.bfloat16),
                pltpu.VMEM((length, width), jnp.float32),
                pltpu.VMEM((parts, 2 * columns, length), jnp.bfloat16),
                pltpu.VMEM((parts, columns, width), jnp.float32),
                pltpu.VMEM((2, 8, width), jnp.float32),
            ],
        ),
        compiler_params=pltpu.CompilerParams(vmem_limit_bytes=58 << 20),
        cost_estimate=pl.CostEstimate(
            flops=2 * 2 * heads * length * length * HEAD_DIM * 9 + 20 * length * width * columns,
            transcendentals=2 * heads * length * length,
            bytes_accessed=40 * length * width,
        ),
        name="attend_back",
    )(scalars, lengths, *arrays)


def spread_kernel(scalars_ref, *refs):
    *pieces, out_ref = refs
    if len(pieces) == 3:
        pieces = [pieces[0], pieces[1], pieces[2].at[0], pieces[2].at[1]]
    mine_ref, far_ref, rest_mine_ref, rest_far_ref = pieces
    for step, ref in enumerate((mine_ref, rest_mine_ref, far_ref, rest_far_ref)):

        @pl.when(pl.program_id(0) == step)
        def _():
            out_ref[0] = ref[...].astype(out_ref.dtype)


def spread(scalars, pieces, kind):
    half, width = pieces[0].shape
    return pl.pallas_call(
        spread_kernel,
        out_shape=pltpu.HBM((2, 2 * half, width), kind),
        grid_spec=pltpu.PrefetchScalarGridSpec(
            num_scalar_prefetch=1,
            grid=(4,),
            in_specs=[pl.BlockSpec(memory_space=pltpu.VMEM)] * len(pieces),
            out_specs=pl.BlockSpec((1, half, width), lambda i, s: (s[0] ^ (i // 2), s[1] ^ (i % 2), 0)),
        ),
        compiler_params=pltpu.CompilerParams(vmem_limit_bytes=16 << 20),
        cost_estimate=pl.CostEstimate(flops=0, transcendentals=0, bytes_accessed=32 * half * width),
        name="spread",
    )(scalars, *pieces)


def split_blocks_kernel(in_ref, first_ref, second_ref):
    count, both, _ = in_ref.shape
    rows = both // 2
    for block in range(count):
        at = slice(block * rows, (block + 1) * rows)
        first_ref[at] = in_ref[block, :rows]
        second_ref[at] = in_ref[block, rows:]


def split_blocks(blocks):
    count, both, width = blocks.shape
    lanes = width // 3 if width % 384 == 0 else width
    shape = pltpu.HBM((count * both // 2, width), blocks.dtype)
    out_spec = pl.BlockSpec((count * both // 2, lanes), lambda i: (0, i))
    return pl.pallas_call(
        split_blocks_kernel,
        out_shape=(shape, shape),
        grid_spec=pl.GridSpec(
            grid=(width // lanes,),
            in_specs=[pl.BlockSpec((count, both, lanes), lambda i: (0, 0, i))],
            out_specs=[out_spec, out_spec],
        ),
        compiler_params=pltpu.CompilerParams(vmem_limit_bytes=24 << 20),
        cost_estimate=pl.CostEstimate(flops=0, transcendentals=0, bytes_accessed=8 * blocks.size),
        name="split_blocks",
    )(blocks)


def place_grads_kernel(
    order, scalars_ref, low_a_ref, low_b_ref, high_a_ref, high_b_ref, qkv_ref, pos_ref, out_ref, vec_ref
):
    group = scalars_ref[0]
    count = 2 * low_a_ref.shape[0]
    rows = qkv_ref.shape[1] // count
    cut = low_a_ref.shape[1]

    def read(place, start, stop):
        upper = (place & 1) == 1
        index = place >> 1
        pieces = []
        if start < cut:
            at = slice(start, min(stop, cut))
            pieces.append(jnp.where(upper, high_a_ref[index, at], low_a_ref[index, at]))
        if stop > cut:
            at = slice(max(start, cut) - cut, stop - cut)
            turned_index = 0
            for bit in range(len(order)):
                turned_index = turned_index | (((index >> bit) & 1) << order[bit])
            pieces.append(jnp.where(upper, high_b_ref[turned_index, at], low_b_ref[turned_index, at]))
        return jnp.concatenate(pieces, axis=0) if len(pieces) > 1 else pieces[0]

    for block in range(count):
        place = block ^ group
        at = slice(block * rows, (block + 1) * rows)
        for part in range(6):
            value = read(place, part * rows, (part + 1) * rows)
            if part < 3:
                qkv_ref[part, at] = value
            elif part < 5:
                pos_ref[part - 3, at] = value
            else:
                out_ref[at] = value
        if block == 0:
            vec_ref[...] = read(place, 6 * rows, cut + low_b_ref.shape[1])


def place_grads(scalars, parts, columns, vec_rows):
    width = parts[0].shape[2]
    bits = parts[0].shape[0].bit_length() - 1
    whole = lambda shape: pl.BlockSpec(shape, lambda i: (0,) * len(shape))
    shapes = (
        jax.ShapeDtypeStruct((3, columns, width), jnp.float32),
        jax.ShapeDtypeStruct((2, columns, width), jnp.float32),
        jax.ShapeDtypeStruct((columns, width), jnp.float32),
        jax.ShapeDtypeStruct((vec_rows, width), jnp.float32),
    )
    return pl.pallas_call(
        partial(place_grads_kernel, tuple(range(bits))[::-1]),
        out_shape=shapes,
        grid_spec=pl.GridSpec(
            grid=(1,),
            in_specs=[pl.BlockSpec(memory_space=pltpu.SMEM)] + [whole(part.shape) for part in parts],
            out_specs=[whole(shape.shape) for shape in shapes],
        ),
        compiler_params=pltpu.CompilerParams(vmem_limit_bytes=40 << 20),
        cost_estimate=pl.CostEstimate(
            flops=0, transcendentals=0, bytes_accessed=32 * width * columns * 3
        ),
        name="place_grads",
    )(scalars, *parts)


def body(
    dp_size,
    mp_size,
    tokens,
    lengths,
    coords,
    w_qkv,
    w_pos,
    w_out,
    b_out,
    gain_one,
    shift_one,
    w_in,
    b_in,
    w_back,
    b_back,
    gain_two,
    shift_two,
    cotangent,
):
    pages, length, width = tokens.shape
    columns = w_qkv.shape[2]
    units = w_in.shape[1]
    here = lax.axis_index(MP)
    low = here & 1
    page = here >> 1
    group = lax.axis_index("dp")
    f32, bf16 = jnp.float32, jnp.bfloat16
    half = length // 2
    one = jnp.where(lengths[0] > 0, 1.0, 0.0).astype(f32)

    def arrived(value):
        return value * one

    def swap(value, bit):
        pairs = [(i, i ^ bit) for i in range(mp_size)]
        return lax.ppermute(value, MP, pairs)

    def group_swap(value, bit):
        pairs = [(i, i ^ bit) for i in range(dp_size)]
        return lax.ppermute(value, "dp", pairs)

    def my_rows(value):
        rows = value.shape[0] // dp_size
        return lax.dynamic_slice_in_dim(value, group * rows, rows, 0)

    def gather(value):
        return lax.all_gather(value, "dp", axis=0, tiled=True)

    def take(value, index):
        return lax.dynamic_index_in_dim(value, index, 0, keepdims=False)

    def after(value, *others):
        return lax.optimization_barrier((value,) + others)[0]

    def row(value):
        return value.reshape(1, -1)

    chunk_rows = lambda value: [value[:half], value[half:]]

    turn = lambda value: jnp.swapaxes(value, 1, 2)
    w_qkv, w_pos = turn(w_qkv), turn(w_pos)
    out_rows = swap(my_rows(w_out).astype(f32), FAR)
    out_rows = jnp.pad(out_rows, ((0, max(0, 48 - out_rows.shape[0])), (0, 0)))
    unit_rows = jnp.concatenate([my_rows(w_in), my_rows(w_back)], axis=0).astype(f32)
    tail = jnp.concatenate([row(b_in), jnp.zeros((7, units), f32)], axis=0)
    far_rows = swap(jnp.concatenate([unit_rows, tail], axis=0), FAR)
    count = columns // dp_size

    table = jnp.asarray(angle_tables(width))
    scalars = jnp.stack([page, low])
    mixed_send, mixed, proj, pos_rows = attend(scalars, lengths, tokens, coords, table, w_qkv, w_pos)
    w_out_far = gather(out_rows).reshape(dp_size, -1, width)[:, : columns // dp_size]
    w_out_far = arrived(w_out_far.reshape(columns, width)).astype(bf16)
    mixed_far = swap(mixed_send, FAR)
    far_rows = after(far_rows, mixed_send)
    count = unit_rows.shape[0]
    b_in_two = jnp.stack([b_in, far_rows[count]])
    blocks = arrived(gather(far_rows)).reshape(dp_size, count + 8, -1)
    in_rows = width // dp_size
    w_in_far = blocks[:, :in_rows].reshape(width, units).astype(bf16)
    w_back_far = blocks[:, in_rows:count].reshape(units, width).astype(bf16)

    mixed_far = arrived(mixed_far).astype(bf16)
    part = mm_tn(jnp.concatenate([mixed, mixed_far], axis=0), jnp.concatenate([w_out, w_out_far], axis=0))
    other = swap(part, NEAR)
    head_rows = jnp.concatenate([w_qkv, w_pos], axis=0)
    count = columns // dp_size
    head_rows = lax.dynamic_slice_in_dim(head_rows, group * count, count, 1).astype(f32)
    blocks = gather(swap(after(head_rows, part), FAR).reshape(-1, width))
    blocks = blocks.reshape(1, dp_size, 5, count, width)

    rows_f32 = jax.ShapeDtypeStruct((length, width), f32)
    rows_low = jax.ShapeDtypeStruct((length, width), bf16)
    units_f32 = jax.ShapeDtypeStruct((length, 2 * units), f32)
    units_low = jax.ShapeDtypeStruct((length, 2 * units), bf16)
    chunk_f32 = jax.ShapeDtypeStruct((half, width), f32)
    scale_of = jax.ShapeDtypeStruct((length, 1), f32)
    shapes = (rows_f32, scale_of, rows_low, units_low, units_f32, chunk_f32)
    arrays = [part, other, row(b_out), row(gain_one), row(shift_one)]
    arrays += [w_in, w_in_far, b_in_two, w_back, w_back_far]
    part, other = [], []
    fed = ()
    for index in range(2):
        *fed, product = on_chunk(
            feed_kernel, "feed", index, scalars, tokens, half, arrays, shapes, tuple(fed)
        )
        part.append(product)
        other.append(swap(product, NEAR))
    xhat_one, scale_one, normed_low, hidden, slope = fed
    shapes = (rows_f32, rows_f32, rows_low, units_low, rows_f32)
    shapes += (jax.ShapeDtypeStruct((3, width), f32), jax.ShapeDtypeStruct((2, units), f32))
    back, sums_two, sums_in = (), [], []
    for index in range(2):
        arrays = [part[index], other[index], xhat_one, slope, row(gain_one), row(shift_one)]
        arrays += [row(b_back), row(gain_two), row(shift_two), w_in, w_in_far, w_back, w_back_far]
        *back, some, some_in = on_chunk(
            feed_back_kernel, "feed_back", index, scalars, cotangent, half, arrays, shapes, tuple(back)
        )
        sums_two.append(some)
        sums_in.append(some_in)
    part, d_second, d_feed, d_pre, output = back
    other = swap(part, NEAR)

    ffn = feed_grads(dp_size, normed_low, d_pre, hidden, d_feed)
    ffn = lax.psum_scatter(ffn.reshape(-1, units), "dp", scatter_dimension=0, tiled=True)

    rows = take(tokens, page)
    arrays = [part, other, d_second, xhat_one, scale_one]
    arrays += [row(gain_one), w_out, w_out_far]
    vectors = sums_two[0] + sums_two[1]
    d_b_in = sums_in[0] + sums_in[1]
    spare = jnp.zeros((1, width), f32)
    vectors = jnp.stack(
        [jnp.concatenate([vectors, d_b_in[side : side + 1], spare], axis=0) for side in range(2)]
    )
    arrays += [proj, w_qkv, blocks, rows, pos_rows, mixed, mixed_far, vectors]
    send, base, keep, give = attend_back(dp_size, jnp.stack([page, low, group]), lengths, arrays)

    half_of = lambda value, index: lax.dynamic_slice_in_dim(value, index * half, half, 0)
    out_mine = half_of(output, low)
    out_far = swap(after(out_mine, other), FAR)

    bits = [1 << k for k in range(dp_size.bit_length() - 1)]
    give = after(give, out_far)
    near_sum = swap(send, NEAR)
    mine = base + near_sum

    group_scalar = jnp.reshape(group, (1,))
    out_turned = swap(out_far, NEAR)
    ffn_rows = ffn.shape[0] // 2
    crossed = swap(jnp.concatenate([mine, ffn[ffn_rows:]], axis=0), FAR)
    ffn = ffn[:ffn_rows] + crossed[half:]
    far_mine = crossed[:half]
    total = keep + group_swap(give, bits[0])
    more = bits[1:]

    def after_all(*values):
        return lax.optimization_barrier(values)

    cut = total.shape[1] // 2
    upper, lower = total[:, :cut], total[:, cut:]
    for step in range(len(more)):
        upper = upper.reshape((-1, 2) + upper.shape[1:])
        lower = lower.reshape((2, -1) + lower.shape[1:])
        give_upper, give_lower = after_all(upper[:, 1], lower[1], *([out_turned] if step else []))[:2]
        got_upper = group_swap(give_upper, more[step])
        got_lower = group_swap(give_lower, more[-1 - step])
        upper = upper[:, 0] + got_upper
        lower = lower[0] + got_lower
    upper, lower = upper[0], lower[0]
    far_sum = swap(after(lower, crossed), FAR)
    ffn = after(ffn, got_upper, got_lower)

    rest = swap(after(jnp.stack([mine, far_mine]), far_sum), NEAR)
    grad_tokens = spread(scalars, (mine, far_mine, rest), f32)
    out_rest = half_of(output, 1 - low)
    layer_out = spread(scalars, (out_mine, out_far, out_rest, after(out_turned, far_sum)), bf16)
    total = upper + far_sum
    cut = total.shape[0] // 16 * 8
    upper, lower = total[None, :cut], total[None, cut:]
    for step in range(len(more)):
        if step:
            upper, lower = after_all(upper, lower, layer_out)[:2]
        got_upper = group_swap(upper, more[step])
        got_lower = group_swap(lower, more[-1 - step])
        upper = jnp.concatenate([upper, got_upper], axis=0)
        lower = jnp.concatenate([lower, got_lower], axis=0)
    grad_w_in, grad_w_back = split_blocks(gather(ffn).reshape(dp_size, ffn_rows, units))
    upper, lower = after_all(upper, lower, rest, grad_w_in)[:2]
    parts = [upper, lower, group_swap(upper, bits[0]), group_swap(lower, bits[0])]
    grad_w_qkv, grad_w_pos, grad_w_out, vectors = place_grads(group_scalar, parts, columns, 8)
    grad_w_qkv, grad_w_pos = turn(grad_w_qkv), turn(grad_w_pos)
    grad_b_out, grad_gain_one, grad_shift_one = vectors[0], vectors[1], vectors[2]
    grad_b_back, grad_gain_two, grad_shift_two = vectors[3], vectors[4], vectors[5]
    grad_b_in = vectors[6]

    return (
        layer_out,
        grad_tokens,
        grad_w_qkv,
        grad_w_pos,
        grad_w_out,
        grad_b_out,
        grad_gain_one,
        grad_shift_one,
        grad_w_in,
        grad_b_in,
        grad_w_back,
        grad_b_back,
        grad_gain_two,
        grad_shift_two,
    )


def solution(mesh):
    mp_size = mesh.shape["mp"]
    dp_size = mesh.devices.size // mp_size
    split = jax.sharding.Mesh(mesh.devices.reshape(dp_size, mp_size // 2, 2), ("dp",) + MP)
    placed = (
        P("dp", None, None),
        P("dp"),
        P("dp", None, None),
        P(None, None, MP),
        P(None, None, MP),
        P(MP, None),
        P(),
        P(),
        P(),
        P(None, MP),
        P(MP),
        P(MP, None),
        P(),
        P(),
        P(),
        P("dp", None, None),
    )
    return jax.shard_map(
        partial(body, dp_size, mp_size),
        mesh=split,
        in_specs=placed,
        out_specs=(
            P("dp", None, None),
            P("dp", None, None),
            P(None, None, MP),
            P(None, None, MP),
            P(MP, None),
            P(),
            P(),
            P(),
            P(None, MP),
            P(MP),
            P(MP, None),
            P(),
            P(),
            P(),
        ),
        check_vma=False,
    )
```

```python
from functools import partial
import math

import jax
import jax.numpy as jnp
import numpy as np
from jax import lax
from jax.experimental import pallas as pl
from jax.experimental.pallas import tpu as pltpu
from jax.sharding import PartitionSpec as P

HEAD_DIM = 64
STEP_BITS = 5
STEP = 1 << STEP_BITS
NEAR = 1
MP = ("far", "near")
FAR = 2
MASKED = -1e30


def mm(left, right):
    return jnp.dot(left, right, preferred_element_type=jnp.float32)


def mm_nt(left, right):
    return lax.dot_general(
        left, right, (((1,), (1,)), ((), ())), preferred_element_type=jnp.float32
    )


def mm_tn(left, right):
    return lax.dot_general(
        left, right, (((0,), (0,)), ((), ())), preferred_element_type=jnp.float32
    )


def angle_tables(model_width):
    quarter = model_width // 4
    rate = np.exp(np.arange(quarter) * (-math.log(10000.0) / quarter))
    fine = np.arange(STEP)[:, None] * rate
    coarse = fine * STEP
    zero = np.zeros((STEP, 2 * quarter))
    table = np.concatenate(
        [
            np.concatenate([np.sin(coarse), np.cos(coarse), zero], axis=1),
            np.concatenate([zero, np.sin(fine), np.cos(fine)], axis=1),
        ],
        axis=0,
    )
    parts = []
    rest = table
    for _ in range(3):
        part = rest.astype(jnp.bfloat16)
        parts.append(part)
        rest = rest - part.astype(np.float64)
    return np.concatenate(parts, axis=0)


def sinusoid(coord, table_ref):
    quarter = table_ref.shape[1] // 4
    slot = lax.broadcasted_iota(jnp.int32, (2 * STEP, coord.shape[1]), 0)
    coarse = coord >> STEP_BITS
    fine = (coord & (STEP - 1)) + STEP
    hit = ((slot == coarse) | (slot == fine)).astype(jnp.float32).astype(jnp.bfloat16)
    looked = mm_tn(jnp.concatenate([hit, hit, hit], axis=0), table_ref[...])
    sin_a, cos_a, sin_b, cos_b = [looked[:, k * quarter : (k + 1) * quarter] for k in range(4)]
    return jnp.concatenate([sin_a * cos_b + cos_a * sin_b, cos_a * cos_b - sin_a * sin_b], axis=1)


def probs_t(q, k, pq, pk, length, factor):
    left = jnp.concatenate([k, pk, k], axis=0)
    right = jnp.concatenate([q, q, pq], axis=0)
    scores = mm_tn(left, right) * factor
    visible = lax.broadcasted_iota(jnp.int32, scores.shape, 0) < length
    scores = jnp.where(visible, scores, MASKED)
    raised = jnp.exp(scores - jnp.max(scores, axis=0, keepdims=True))
    return raised * (1.0 / jnp.sum(raised, axis=0, keepdims=True))


def rows_at(head):
    return pl.ds(pl.multiple_of(head * HEAD_DIM, HEAD_DIM), HEAD_DIM)


def attend_kernel(
    heads, scalars_ref, lengths_ref, x_ref, coords_ref, table_ref, wqkv_ref, wpos_ref,
    send_ref, own_ref, proj_ref, pos_ref,
):
    step = pl.program_id(0)
    length = lengths_ref[scalars_ref[0] ^ (1 - step)]
    factor = 1.0 / math.sqrt(3.0 * HEAD_DIM)
    rows = x_ref[0]
    for part in range(3):
        proj_ref[part] = mm_nt(wqkv_ref[part], rows).astype(jnp.bfloat16)
    sides = [sinusoid(coords_ref[0, axis : axis + 1], table_ref) for axis in range(2)]
    position = jnp.concatenate(sides, axis=1).astype(jnp.bfloat16)
    pos_ref[...] = position
    for part in range(2):
        proj_ref[3 + part] = mm_nt(wpos_ref[part], position).astype(jnp.bfloat16)

    def one_head(head, _):
        at = rows_at(head)
        q, k, v, pq, pk = [proj_ref[part, at] for part in range(5)]
        weights = probs_t(q, k, pq, pk, length, factor).astype(jnp.bfloat16)
        mixed = mm(v, weights).astype(jnp.bfloat16)

        @pl.when(step == 0)
        def _():
            send_ref[at] = mixed.astype(jnp.float32)

        @pl.when(step == 1)
        def _():
            own_ref[at] = mixed

        return 0

    lax.fori_loop(0, heads, one_head, 0)


def attend(scalars, lengths, tokens, coords, table, w_qkv, w_pos):
    pages, length, width = tokens.shape
    columns = w_qkv.shape[1]
    whole = lambda shape: pl.BlockSpec(shape, lambda i, s, n: (0,) * len(shape))
    shapes = (
        jax.ShapeDtypeStruct((columns, length), jnp.float32),
        jax.ShapeDtypeStruct((columns, length), jnp.bfloat16),
        jax.ShapeDtypeStruct((5, columns, length), jnp.bfloat16),
        jax.ShapeDtypeStruct((length, width), jnp.bfloat16),
    )
    page = lambda i, s, n: (s[0] ^ (1 - i), 0, 0)
    return pl.pallas_call(
        partial(attend_kernel, columns // HEAD_DIM),
        out_shape=shapes,
        grid_spec=pltpu.PrefetchScalarGridSpec(
            num_scalar_prefetch=2,
            grid=(pages,),
            in_specs=[
                pl.BlockSpec((1, length, width), page),
                pl.BlockSpec((1,) + coords.shape[1:], page),
                whole(table.shape),
                whole(w_qkv.shape),
                whole(w_pos.shape),
            ],
            out_specs=[whole(shape.shape) for shape in shapes],
        ),
        compiler_params=pltpu.CompilerParams(vmem_limit_bytes=40 << 20),
        cost_estimate=pl.CostEstimate(
            flops=2 * pages * length * columns * (5 * width + 4 * length),
            transcendentals=pages * length * length * columns // HEAD_DIM,
            bytes_accessed=pages * length * (4 * width + 14 * columns),
        ),
        name="attend",
    )(scalars, lengths, tokens, coords, table, w_qkv, w_pos)


def norm_parts(values):
    center = values - jnp.mean(values, axis=-1, keepdims=True)
    spread = jnp.mean(center * center, axis=-1, keepdims=True)
    scale = lax.rsqrt(spread + 1e-05)
    return center * scale, scale


def norm_back(grad, gain, xhat, scale):
    up = grad * gain
    mean = jnp.mean(up, axis=-1, keepdims=True)
    along = jnp.mean(up * xhat, axis=-1, keepdims=True)
    return scale * (up - mean - xhat * along)


def column_sum(values):
    return jnp.sum(values.astype(jnp.float32), axis=0, keepdims=True)


def feed_kernel(
    scalars_ref, x_ref, part_ref, other_ref, b_out_ref, gain_ref, shift_ref, w_in_ref, w_in_far_ref, b_in_ref,
    w_back_ref, w_back_far_ref, xhat_ref, scale_ref, low_ref, hidden_ref, slope_ref, next_ref,
):
    first = x_ref[0].astype(jnp.float32) + (part_ref[...] + other_ref[...] + b_out_ref[...])
    xhat, scale = norm_parts(first)
    low = (xhat * gain_ref[...] + shift_ref[...]).astype(jnp.bfloat16)
    xhat_ref[...] = xhat
    scale_ref[...] = scale
    low_ref[...] = low
    units = w_in_ref.shape[1]
    total = None
    for side, (into, back) in enumerate(((w_in_ref, w_back_ref), (w_in_far_ref, w_back_far_ref))):
        at = slice(side * units, (side + 1) * units)
        pre = mm(low, into[...]) + b_in_ref[side : side + 1]
        cdf = 0.5 * (1.0 + lax.erf(pre * math.sqrt(0.5)))
        hidden = (pre * cdf).astype(jnp.bfloat16)
        hidden_ref[:, at] = hidden
        slope_ref[:, at] = cdf + pre * (jnp.exp(-0.5 * pre * pre) * (1.0 / math.sqrt(2.0 * math.pi)))
        product = mm(hidden, back[...])
        total = product if total is None else total + product
    next_ref[...] = total


def feed_back_kernel(
    scalars_ref, cot_ref, part_ref, other_ref, xhat_ref, slope_ref, gain_one_ref, shift_one_ref, b_back_ref,
    gain_ref, shift_ref, w_in_ref, w_in_far_ref, w_back_ref, w_back_far_ref,
    next_ref, second_ref, feed_ref, pre_ref, out_ref, sums_ref, sums_in_ref,
):
    normed = xhat_ref[...] * gain_one_ref[...] + shift_one_ref[...]
    second = normed + (part_ref[...] + other_ref[...] + b_back_ref[...])
    xhat, scale = norm_parts(second)
    out_ref[...] = xhat * gain_ref[...] + shift_ref[...]
    grad = cot_ref[0].astype(jnp.float32)
    d_second = norm_back(grad, gain_ref[...], xhat, scale)
    second_ref[...] = d_second
    d_feed = d_second.astype(jnp.bfloat16)
    feed_ref[...] = d_feed
    sums_ref[0:1] = column_sum(d_feed)
    sums_ref[1:2] = column_sum(grad * xhat)
    sums_ref[2:3] = column_sum(grad)
    units = w_in_ref.shape[1]
    total = None
    for side, (into, back) in enumerate(((w_in_ref, w_back_ref), (w_in_far_ref, w_back_far_ref))):
        at = slice(side * units, (side + 1) * units)
        d_pre = (mm_nt(d_feed, back[...]) * slope_ref[:, at]).astype(jnp.bfloat16)
        pre_ref[:, at] = d_pre
        sums_in_ref[side : side + 1] = column_sum(d_pre)
        product = mm_nt(d_pre, into[...])
        total = product if total is None else total + product
    next_ref[...] = total


def without(kernel, first, count):
    def call(*refs):
        return kernel(*refs[:first], *refs[first + count :])

    return call


def on_chunk(kernel, name, chunk, scalars, pages_array, rows, arrays, shapes, before=()):
    length, width = pages_array.shape[1:]

    def rows_of(array):
        if array.shape[0] == length and len(array.shape) == 2:
            return pl.BlockSpec((rows, array.shape[1]), lambda i, s: (chunk, 0))
        return pl.BlockSpec(memory_space=pltpu.VMEM)

    def whole(shape):
        if shape.shape[0] == length:
            return rows_of(shape)
        return pl.BlockSpec(shape.shape, lambda i, s: (0,) * len(shape.shape))

    inputs = 2 + len(arrays)
    return pl.pallas_call(
        without(kernel, inputs, len(before)),
        out_shape=shapes,
        grid_spec=pltpu.PrefetchScalarGridSpec(
            num_scalar_prefetch=1,
            grid=(1,),
            in_specs=[pl.BlockSpec((1, rows, width), lambda i, s: (s[0], chunk, 0))]
            + [rows_of(array) for array in arrays]
            + [pl.BlockSpec(memory_space=pl.ANY)] * len(before),
            out_specs=[whole(shape) for shape in shapes],
        ),
        input_output_aliases={inputs + index: index for index in range(len(before))},
        compiler_params=pltpu.CompilerParams(vmem_limit_bytes=48 << 20),
        cost_estimate=pl.CostEstimate(
            flops=16 * rows * width * width, transcendentals=2 * rows * width, bytes_accessed=40 * rows * width
        ),
        name=name,
    )(scalars, pages_array, *arrays, *before)


def feed_grads_kernel(count, low_ref, pre_ref, hidden_ref, feed_ref, out_ref):
    rows = out_ref.shape[2]

    def put(left, right):
        product = mm_tn(left[...], right[...])
        for block in range(count):
            out_ref[block, 0] = product[block * rows : (block + 1) * rows]

    @pl.when(pl.program_id(0) % 2 == 0)
    def _():
        put(low_ref, pre_ref)

    @pl.when(pl.program_id(0) % 2 == 1)
    def _():
        put(hidden_ref, feed_ref)


def feed_grads(count, low, d_pre, hidden, d_feed):
    length, width = low.shape
    units = hidden.shape[1] // 2
    return pl.pallas_call(
        partial(feed_grads_kernel, count),
        out_shape=pltpu.HBM((count, 4, width // count, units), jnp.float32),
        grid_spec=pl.GridSpec(
            grid=(4,),
            in_specs=[
                pl.BlockSpec((length, width), lambda i: (0, 0)),
                pl.BlockSpec((length, units), lambda i: (0, i // 2)),
                pl.BlockSpec((length, units), lambda i: (0, i // 2)),
                pl.BlockSpec((length, width), lambda i: (0, 0)),
            ],
            out_specs=pl.BlockSpec((count, 1, width // count, units), lambda i: (0, i, 0, 0)),
        ),
        compiler_params=pltpu.CompilerParams(vmem_limit_bytes=40 << 20),
        cost_estimate=pl.CostEstimate(
            flops=8 * length * width * units, transcendentals=0, bytes_accessed=16 * width * units
        ),
        name="feed_grads",
    )(low, d_pre, hidden, d_feed)


def weight_grads(count, group, x_ref, pos_ref, d_ref, db_ref, mixed_ref, far_ref, vec_ref, keep_ref, send_ref):
    columns = mixed_ref.shape[0]
    rows = columns // count
    odd = group & 1
    extra = vec_ref.shape[1]
    side_rows = 6 * rows + extra
    mixed = jnp.concatenate([mixed_ref[...], far_ref[...]], axis=0)
    rights = [x_ref] * 3 + [pos_ref] * 2 + [db_ref]

    def put(block, at, value):
        place = (block ^ group) >> 1

        @pl.when(odd == (block & 1))
        def _():
            keep_ref[place, at] = value

        @pl.when(odd != (block & 1))
        def _():
            send_ref[place, at] = value

    for part, right in enumerate(rights):
        product = mm(d_ref[part] if part < 5 else mixed, right[...])
        for block in range(count):
            for side in range(2):
                start = side * columns + block * rows
                at = side * side_rows + part * rows
                put(block, slice(at, at + rows), product[start : start + rows])
    for block in range(count):
        for side in range(2):
            at = slice(side * side_rows + 6 * rows, (side + 1) * side_rows)
            put(block, at, vec_ref[side] if block == 0 else jnp.zeros(vec_ref.shape[1:], jnp.float32))


def attend_back_kernel(
    heads, count, scalars_ref, lengths_ref, part_ref, other_ref, second_ref, xhat_ref, scale_ref, gain_ref, w_out_ref, w_out_far_ref, own_ref, wqkv_ref, blocks_ref, x_ref, pos_ref, mixed_ref, mixed_far_ref, more_ref,
    send_ref, base_ref, keep_ref, give_ref, d_ref, branch_ref, dm_ref, first_ref, proj_ref, wfar_ref, vec_ref,
):
    page, low = scalars_ref[0], scalars_ref[1]
    length = lengths_ref[page]
    factor = 1.0 / math.sqrt(3.0 * HEAD_DIM)
    columns = heads * HEAD_DIM
    half = part_ref.shape[0] // 2
    block_rows = blocks_ref.shape[3]
    for part in range(5):
        for block in range(count):
            at = slice(block * block_rows, (block + 1) * block_rows)
            wfar_ref[part, at] = blocks_ref[0, block, part]
        weight = wfar_ref[part].astype(jnp.bfloat16)
        left = x_ref if part < 3 else pos_ref
        proj_ref[part, columns:] = mm_nt(weight, left[...]).astype(jnp.bfloat16)
        proj_ref[part, :columns] = own_ref[part]
    sums = None
    for index in range(2):
        at = slice(index * half, (index + 1) * half)
        xhat = xhat_ref[at]
        d_normed = second_ref[at] + (part_ref[at] + other_ref[at])
        d_first = norm_back(d_normed, gain_ref[...], xhat, scale_ref[at])
        first_ref[at] = d_first
        d_branch = d_first.astype(jnp.bfloat16)
        branch_ref[at] = d_branch
        some = (column_sum(d_branch), column_sum(d_normed * xhat), column_sum(d_normed))
        sums = some if sums is None else tuple(x + y for x, y in zip(sums, some))
        dm_ref[:columns, at] = mm_nt(w_out_ref[...], d_branch).astype(jnp.bfloat16)
        dm_ref[columns:, at] = mm_nt(w_out_far_ref[...], d_branch).astype(jnp.bfloat16)
    for side in range(2):
        for index, value in enumerate(sums):
            vec_ref[side, index : index + 1] = value
        vec_ref[side, len(sums) :] = more_ref[side]

    def one_head(head, _):
        at = rows_at(head)
        q, k, v, pq, pk = [proj_ref[part, at] for part in range(5)]
        dm = dm_ref[at]
        probs = probs_t(q, k, pq, pk, length, factor)
        weights = probs.astype(jnp.bfloat16)
        d_values = mm(weights, dm.T)
        d_probs = mm_tn(v, dm)
        inner = jnp.sum(d_probs * probs, axis=0, keepdims=True)
        d_scores = (probs * (d_probs - inner)).astype(jnp.bfloat16)
        by_queries = mm(d_scores, jnp.concatenate([q, pq], axis=0).T).T
        by_query, by_pos_query = by_queries[:HEAD_DIM], by_queries[HEAD_DIM:]
        by_keys = mm(jnp.concatenate([k, pk], axis=0), d_scores)
        by_key, by_pos_key = by_keys[:HEAD_DIM], by_keys[HEAD_DIM:]
        grads = (
            (by_key + by_pos_key) * factor,
            (by_query + by_pos_query) * factor,
            d_values.T,
            by_key * factor,
            by_query * factor,
        )
        for part, value in enumerate(grads):
            d_ref[part, at] = value.astype(jnp.bfloat16)
        return 0

    lax.fori_loop(0, 2 * heads, one_head, 0)
    for part in range(3):
        for side in range(2):
            at = slice(side * columns, (side + 1) * columns)
            weight = wqkv_ref[part] if side == 0 else wfar_ref[part].astype(jnp.bfloat16)
            first_ref_part = mm_tn(d_ref[part, at], weight)
            if part == side == 0:
                total = first_ref_part
            else:
                total = total + first_ref_part
    upper, lower = total[:half], total[half:]
    send_ref[...] = jnp.where(low == 0, lower, upper)
    base_ref[...] = jnp.where(low == 0, upper + first_ref[:half], lower + first_ref[half:])
    weight_grads(
        count, scalars_ref[2], x_ref, pos_ref, d_ref, branch_ref, mixed_ref, mixed_far_ref, vec_ref, keep_ref, give_ref
    )


def attend_back(count, scalars, lengths, arrays):
    proj = arrays[8]
    parts, columns, length = proj.shape
    half, width = length // 2, arrays[0].shape[1]
    heads = columns // HEAD_DIM
    whole = lambda shape: pl.BlockSpec(shape, lambda i, s, n: (0,) * len(shape))
    shapes = (
        jax.ShapeDtypeStruct((half, width), jnp.float32),
        jax.ShapeDtypeStruct((half, width), jnp.float32),
    ) + 2 * (jax.ShapeDtypeStruct((count // 2, 2 * (6 * (columns // count) + 8), width), jnp.float32),)
    return pl.pallas_call(
        partial(attend_back_kernel, heads, count),
        out_shape=shapes,
        grid_spec=pltpu.PrefetchScalarGridSpec(
            num_scalar_prefetch=2,
            grid=(1,),
            in_specs=[
                whole(array.shape)
                if len(array.shape) < 5
                else pl.BlockSpec((1,) + array.shape[1:], lambda i, s, n: (0, 0, 0, 0, 0))
                for array in arrays
            ],
            out_specs=[whole(shape.shape) for shape in shapes],
            scratch_shapes=[
                pltpu.VMEM((parts, 2 * columns, length), jnp.bfloat16),
                pltpu.VMEM((length, width), jnp.bfloat16),
                pltpu.VMEM((2 * columns, length), jnp.bfloat16),
                pltpu.VMEM((length, width), jnp.float32),
                pltpu.VMEM((parts, 2 * columns, length), jnp.bfloat16),
                pltpu.VMEM((parts, columns, width), jnp.float32),
                pltpu.VMEM((2, 8, width), jnp.float32),
            ],
        ),
        compiler_params=pltpu.CompilerParams(vmem_limit_bytes=58 << 20),
        cost_estimate=pl.CostEstimate(
            flops=2 * 2 * heads * length * length * HEAD_DIM * 9 + 20 * length * width * columns,
            transcendentals=2 * heads * length * length,
            bytes_accessed=40 * length * width,
        ),
        name="attend_back",
    )(scalars, lengths, *arrays)


def spread_kernel(count, scalars_ref, *refs):
    out_ref = refs[-1]
    pieces = [refs[0].at[0], refs[0].at[1]] if len(refs[0].shape) == 3 else refs[:count]
    for step, ref in enumerate(pieces):

        @pl.when(pl.program_id(0) == step)
        def _():
            out_ref[0] = ref[...].astype(out_ref.dtype)


def spread(scalars, pieces, kind, start, onto=()):
    half, width = pieces[0].shape[-2:]
    count = max(len(pieces), 2)
    return pl.pallas_call(
        partial(spread_kernel, count),
        out_shape=pltpu.HBM((2, 2 * half, width), kind),
        grid_spec=pltpu.PrefetchScalarGridSpec(
            num_scalar_prefetch=1,
            grid=(count,),
            in_specs=[pl.BlockSpec(memory_space=pltpu.VMEM)] * len(pieces)
            + [pl.BlockSpec(memory_space=pltpu.HBM)] * len(onto),
            out_specs=pl.BlockSpec(
                (1, half, width), lambda i, s: (s[0] ^ ((start + i) % 2), s[1] ^ ((start + i) // 2), 0)
            ),
        ),
        input_output_aliases={1 + len(pieces): 0} if onto else {},
        compiler_params=pltpu.CompilerParams(vmem_limit_bytes=16 << 20),
        cost_estimate=pl.CostEstimate(flops=0, transcendentals=0, bytes_accessed=32 * half * width),
        name="spread",
    )(scalars, *pieces, *onto)


def split_blocks_kernel(in_ref, first_ref, second_ref):
    count, both, _ = in_ref.shape
    rows = both // 2
    for block in range(count):
        at = slice(block * rows, (block + 1) * rows)
        first_ref[at] = in_ref[block, :rows]
        second_ref[at] = in_ref[block, rows:]


def split_blocks(blocks):
    count, both, width = blocks.shape
    lanes = width // 3 if width % 384 == 0 else width
    shape = pltpu.HBM((count * both // 2, width), blocks.dtype)
    out_spec = pl.BlockSpec((count * both // 2, lanes), lambda i: (0, i))
    return pl.pallas_call(
        split_blocks_kernel,
        out_shape=(shape, shape),
        grid_spec=pl.GridSpec(
            grid=(width // lanes,),
            in_specs=[pl.BlockSpec((count, both, lanes), lambda i: (0, 0, i))],
            out_specs=[out_spec, out_spec],
        ),
        compiler_params=pltpu.CompilerParams(vmem_limit_bytes=24 << 20),
        cost_estimate=pl.CostEstimate(flops=0, transcendentals=0, bytes_accessed=8 * blocks.size),
        name="split_blocks",
    )(blocks)


def place_grads_kernel(
    order, scalars_ref, low_a_ref, low_b_ref, high_a_ref, high_b_ref, qkv_ref, pos_ref, out_ref, vec_ref
):
    group = scalars_ref[0]
    count = 2 * low_a_ref.shape[0]
    rows = qkv_ref.shape[1] // count
    cut = low_a_ref.shape[1]

    def read(place, start, stop):
        upper = (place & 1) == 1
        index = place >> 1
        pieces = []
        if start < cut:
            at = slice(start, min(stop, cut))
            pieces.append(jnp.where(upper, high_a_ref[index, at], low_a_ref[index, at]))
        if stop > cut:
            at = slice(max(start, cut) - cut, stop - cut)
            turned_index = 0
            for bit in range(len(order)):
                turned_index = turned_index | (((index >> bit) & 1) << order[bit])
            pieces.append(jnp.where(upper, high_b_ref[turned_index, at], low_b_ref[turned_index, at]))
        return jnp.concatenate(pieces, axis=0) if len(pieces) > 1 else pieces[0]

    for block in range(count):
        place = block ^ group
        at = slice(block * rows, (block + 1) * rows)
        for part in range(6):
            value = read(place, part * rows, (part + 1) * rows)
            if part < 3:
                qkv_ref[part, at] = value
            elif part < 5:
                pos_ref[part - 3, at] = value
            else:
                out_ref[at] = value
        if block == 0:
            vec_ref[...] = read(place, 6 * rows, cut + low_b_ref.shape[1])


def place_grads(scalars, parts, columns, vec_rows):
    width = parts[0].shape[2]
    bits = parts[0].shape[0].bit_length() - 1
    whole = lambda shape: pl.BlockSpec(shape, lambda i: (0,) * len(shape))
    shapes = (
        jax.ShapeDtypeStruct((3, columns, width), jnp.float32),
        jax.ShapeDtypeStruct((2, columns, width), jnp.float32),
        jax.ShapeDtypeStruct((columns, width), jnp.float32),
        jax.ShapeDtypeStruct((vec_rows, width), jnp.float32),
    )
    return pl.pallas_call(
        partial(place_grads_kernel, tuple(range(bits))[::-1]),
        out_shape=shapes,
        grid_spec=pl.GridSpec(
            grid=(1,),
            in_specs=[pl.BlockSpec(memory_space=pltpu.SMEM)] + [whole(part.shape) for part in parts],
            out_specs=[whole(shape.shape) for shape in shapes],
        ),
        compiler_params=pltpu.CompilerParams(vmem_limit_bytes=40 << 20),
        cost_estimate=pl.CostEstimate(
            flops=0, transcendentals=0, bytes_accessed=32 * width * columns * 3
        ),
        name="place_grads",
    )(scalars, *parts)


def body(
    dp_size,
    mp_size,
    tokens,
    lengths,
    coords,
    w_qkv,
    w_pos,
    w_out,
    b_out,
    gain_one,
    shift_one,
    w_in,
    b_in,
    w_back,
    b_back,
    gain_two,
    shift_two,
    cotangent,
):
    pages, length, width = tokens.shape
    columns = w_qkv.shape[2]
    units = w_in.shape[1]
    here = lax.axis_index(MP)
    low = here & 1
    page = here >> 1
    group = lax.axis_index("dp")
    f32, bf16 = jnp.float32, jnp.bfloat16
    half = length // 2
    one = jnp.where(lengths[0] > 0, 1.0, 0.0).astype(f32)

    def arrived(value):
        return value * one

    def swap(value, bit):
        pairs = [(i, i ^ bit) for i in range(mp_size)]
        return lax.ppermute(value, MP, pairs)

    def group_swap(value, bit):
        pairs = [(i, i ^ bit) for i in range(dp_size)]
        return lax.ppermute(value, "dp", pairs)

    def my_rows(value):
        rows = value.shape[0] // dp_size
        return lax.dynamic_slice_in_dim(value, group * rows, rows, 0)

    def gather(value):
        return lax.all_gather(value, "dp", axis=0, tiled=True)

    def take(value, index):
        return lax.dynamic_index_in_dim(value, index, 0, keepdims=False)

    def after(value, *others):
        return lax.optimization_barrier((value,) + others)[0]

    def row(value):
        return value.reshape(1, -1)

    chunk_rows = lambda value: [value[:half], value[half:]]

    turn = lambda value: jnp.swapaxes(value, 1, 2)
    w_qkv, w_pos = turn(w_qkv), turn(w_pos)
    out_rows = swap(my_rows(w_out).astype(f32), FAR)
    out_rows = jnp.pad(out_rows, ((0, max(0, 48 - out_rows.shape[0])), (0, 0)))
    unit_rows = jnp.concatenate([my_rows(w_in), my_rows(w_back)], axis=0).astype(f32)
    tail = jnp.concatenate([row(b_in), jnp.zeros((7, units), f32)], axis=0)
    far_rows = swap(jnp.concatenate([unit_rows, tail], axis=0), FAR)
    count = columns // dp_size

    table = jnp.asarray(angle_tables(width))
    scalars = jnp.stack([page, low])
    mixed_send, mixed, proj, pos_rows = attend(scalars, lengths, tokens, coords, table, w_qkv, w_pos)
    w_out_far = gather(out_rows).reshape(dp_size, -1, width)[:, : columns // dp_size]
    w_out_far = arrived(w_out_far.reshape(columns, width)).astype(bf16)
    mixed_far = swap(mixed_send, FAR)
    far_rows = after(far_rows, mixed_send)
    count = unit_rows.shape[0]
    b_in_two = jnp.stack([b_in, far_rows[count]])
    blocks = arrived(gather(far_rows)).reshape(dp_size, count + 8, -1)
    in_rows = width // dp_size
    w_in_far = blocks[:, :in_rows].reshape(width, units).astype(bf16)
    w_back_far = blocks[:, in_rows:count].reshape(units, width).astype(bf16)

    mixed_far = arrived(mixed_far).astype(bf16)
    part = mm_tn(jnp.concatenate([mixed, mixed_far], axis=0), jnp.concatenate([w_out, w_out_far], axis=0))
    other = swap(part, NEAR)
    head_rows = jnp.concatenate([w_qkv, w_pos], axis=0)
    count = columns // dp_size
    head_rows = lax.dynamic_slice_in_dim(head_rows, group * count, count, 1).astype(f32)
    blocks = gather(swap(after(head_rows, part), FAR).reshape(-1, width))
    blocks = blocks.reshape(1, dp_size, 5, count, width)

    rows_f32 = jax.ShapeDtypeStruct((length, width), f32)
    rows_low = jax.ShapeDtypeStruct((length, width), bf16)
    units_f32 = jax.ShapeDtypeStruct((length, 2 * units), f32)
    units_low = jax.ShapeDtypeStruct((length, 2 * units), bf16)
    chunk_f32 = jax.ShapeDtypeStruct((half, width), f32)
    scale_of = jax.ShapeDtypeStruct((length, 1), f32)
    shapes = (rows_f32, scale_of, rows_low, units_low, units_f32, chunk_f32)
    arrays = [part, other, row(b_out), row(gain_one), row(shift_one)]
    arrays += [w_in, w_in_far, b_in_two, w_back, w_back_far]
    part, other = [], []
    fed = ()
    for index in range(2):
        *fed, product = on_chunk(
            feed_kernel, "feed", index, scalars, tokens, half, arrays, shapes, tuple(fed)
        )
        part.append(product)
        other.append(swap(product, NEAR))
    xhat_one, scale_one, normed_low, hidden, slope = fed
    shapes = (rows_f32, rows_f32, rows_low, units_low, rows_f32)
    shapes += (jax.ShapeDtypeStruct((3, width), f32), jax.ShapeDtypeStruct((2, units), f32))
    back, sums_two, sums_in = (), [], []
    for index in range(2):
        arrays = [part[index], other[index], xhat_one, slope, row(gain_one), row(shift_one)]
        arrays += [row(b_back), row(gain_two), row(shift_two), w_in, w_in_far, w_back, w_back_far]
        *back, some, some_in = on_chunk(
            feed_back_kernel, "feed_back", index, scalars, cotangent, half, arrays, shapes, tuple(back)
        )
        sums_two.append(some)
        sums_in.append(some_in)
    part, d_second, d_feed, d_pre, output = back
    other = swap(part, NEAR)

    ffn = feed_grads(dp_size, normed_low, d_pre, hidden, d_feed)
    ffn = lax.psum_scatter(ffn.reshape(-1, units), "dp", scatter_dimension=0, tiled=True)

    rows = take(tokens, page)
    arrays = [part, other, d_second, xhat_one, scale_one]
    arrays += [row(gain_one), w_out, w_out_far]
    vectors = sums_two[0] + sums_two[1]
    d_b_in = sums_in[0] + sums_in[1]
    spare = jnp.zeros((1, width), f32)
    vectors = jnp.stack(
        [jnp.concatenate([vectors, d_b_in[side : side + 1], spare], axis=0) for side in range(2)]
    )
    arrays += [proj, w_qkv, blocks, rows, pos_rows, mixed, mixed_far, vectors]
    send, base, keep, give = attend_back(dp_size, jnp.stack([page, low, group]), lengths, arrays)

    half_of = lambda value, index: lax.dynamic_slice_in_dim(value, index * half, half, 0)
    out_mine = half_of(output, low)
    out_far = swap(after(out_mine, other), FAR)

    bits = [1 << k for k in range(dp_size.bit_length() - 1)]
    give = after(give, out_far)
    near_sum = swap(send, NEAR)
    mine = base + near_sum

    group_scalar = jnp.reshape(group, (1,))
    out_turned = swap(out_far, NEAR)
    ffn_rows = ffn.shape[0] // 2
    crossed = swap(jnp.concatenate([mine, ffn[ffn_rows:]], axis=0), FAR)
    ffn = ffn[:ffn_rows] + crossed[half:]
    far_mine = crossed[:half]
    total = keep + group_swap(give, bits[0])
    more = bits[1:]

    def after_all(*values):
        return lax.optimization_barrier(values)

    cut = total.shape[1] // 2
    upper, lower = total[:, :cut], total[:, cut:]
    for step in range(len(more)):
        upper = upper.reshape((-1, 2) + upper.shape[1:])
        lower = lower.reshape((2, -1) + lower.shape[1:])
        give_upper, give_lower = after_all(upper[:, 1], lower[1], *([out_turned] if step else []))[:2]
        got_upper = group_swap(give_upper, more[step])
        got_lower = group_swap(give_lower, more[-1 - step])
        upper = upper[:, 0] + got_upper
        lower = lower[0] + got_lower
    upper, lower = upper[0], lower[0]
    far_sum = swap(after(lower, crossed), FAR)
    ffn = after(ffn, got_upper, got_lower)

    rest = swap(after(jnp.stack([mine, far_mine]), far_sum), NEAR)
    grad_half = spread(scalars, (mine, far_mine), f32, 0)
    grad_tokens = spread(scalars, (rest,), f32, 2, (grad_half,))
    out_rest = half_of(output, 1 - low)
    layer_out = spread(scalars, (out_mine, out_far, out_rest, after(out_turned, far_sum)), bf16, 0)
    total = upper + far_sum
    cut = total.shape[0] // 16 * 8
    upper, lower = total[None, :cut], total[None, cut:]
    for step in range(len(more)):
        if step:
            upper, lower = after_all(upper, lower, layer_out, grad_half)[:2]
        got_upper = group_swap(upper, more[step])
        got_lower = group_swap(lower, more[-1 - step])
        upper = jnp.concatenate([upper, got_upper], axis=0)
        lower = jnp.concatenate([lower, got_lower], axis=0)
    grad_w_in, grad_w_back = split_blocks(gather(ffn).reshape(dp_size, ffn_rows, units))
    upper, lower = after_all(upper, lower, rest, grad_w_in)[:2]
    parts = [upper, lower, group_swap(upper, bits[0]), group_swap(lower, bits[0])]
    grad_w_qkv, grad_w_pos, grad_w_out, vectors = place_grads(group_scalar, parts, columns, 8)
    grad_w_qkv, grad_w_pos = turn(grad_w_qkv), turn(grad_w_pos)
    grad_b_out, grad_gain_one, grad_shift_one = vectors[0], vectors[1], vectors[2]
    grad_b_back, grad_gain_two, grad_shift_two = vectors[3], vectors[4], vectors[5]
    grad_b_in = vectors[6]

    return (
        layer_out,
        grad_tokens,
        grad_w_qkv,
        grad_w_pos,
        grad_w_out,
        grad_b_out,
        grad_gain_one,
        grad_shift_one,
        grad_w_in,
        grad_b_in,
        grad_w_back,
        grad_b_back,
        grad_gain_two,
        grad_shift_two,
    )


def solution(mesh):
    mp_size = mesh.shape["mp"]
    dp_size = mesh.devices.size // mp_size
    split = jax.sharding.Mesh(mesh.devices.reshape(dp_size, mp_size // 2, 2), ("dp",) + MP)
    placed = (
        P("dp", None, None),
        P("dp"),
        P("dp", None, None),
        P(None, None, MP),
        P(None, None, MP),
        P(MP, None),
        P(),
        P(),
        P(),
        P(None, MP),
        P(MP),
        P(MP, None),
        P(),
        P(),
        P(),
        P("dp", None, None),
    )
    return jax.shard_map(
        partial(body, dp_size, mp_size),
        mesh=split,
        in_specs=placed,
        out_specs=(
            P("dp", None, None),
            P("dp", None, None),
            P(None, None, MP),
            P(None, None, MP),
            P(MP, None),
            P(),
            P(),
            P(),
            P(None, MP),
            P(MP),
            P(MP, None),
            P(),
            P(),
            P(),
        ),
        check_vma=False,
    )
```

```python
from functools import partial
import math

import jax
import jax.numpy as jnp
import numpy as np
from jax import lax
from jax.experimental import pallas as pl
from jax.experimental.pallas import tpu as pltpu
from jax.sharding import PartitionSpec as P

HEAD_DIM = 64
STEP_BITS = 5
STEP = 1 << STEP_BITS
NEAR = 1
MP = ("far", "near")
FAR = 2
MASKED = -1e30


def mm(left, right):
    return jnp.dot(left, right, preferred_element_type=jnp.float32)


def mm_nt(left, right):
    return lax.dot_general(
        left, right, (((1,), (1,)), ((), ())), preferred_element_type=jnp.float32
    )


def mm_tn(left, right):
    return lax.dot_general(
        left, right, (((0,), (0,)), ((), ())), preferred_element_type=jnp.float32
    )


def angle_tables(model_width):
    quarter = model_width // 4
    rate = np.exp(np.arange(quarter) * (-math.log(10000.0) / quarter))
    fine = np.arange(STEP)[:, None] * rate
    coarse = fine * STEP
    zero = np.zeros((STEP, 2 * quarter))
    table = np.concatenate(
        [
            np.concatenate([np.sin(coarse), np.cos(coarse), zero], axis=1),
            np.concatenate([zero, np.sin(fine), np.cos(fine)], axis=1),
        ],
        axis=0,
    )
    parts = []
    rest = table
    for _ in range(3):
        part = rest.astype(jnp.bfloat16)
        parts.append(part)
        rest = rest - part.astype(np.float64)
    return np.concatenate(parts, axis=0)


def sinusoid(coord, table_ref):
    quarter = table_ref.shape[1] // 4
    slot = lax.broadcasted_iota(jnp.int32, (2 * STEP, coord.shape[1]), 0)
    coarse = coord >> STEP_BITS
    fine = (coord & (STEP - 1)) + STEP
    hit = ((slot == coarse) | (slot == fine)).astype(jnp.float32).astype(jnp.bfloat16)
    looked = mm_tn(jnp.concatenate([hit, hit, hit], axis=0), table_ref[...])
    sin_a, cos_a, sin_b, cos_b = [looked[:, k * quarter : (k + 1) * quarter] for k in range(4)]
    return jnp.concatenate([sin_a * cos_b + cos_a * sin_b, cos_a * cos_b - sin_a * sin_b], axis=1)


def probs_t(q, k, pq, pk, length, factor):
    left = jnp.concatenate([k, pk, k], axis=0)
    right = jnp.concatenate([q, q, pq], axis=0)
    scores = mm_tn(left, right) * factor
    visible = lax.broadcasted_iota(jnp.int32, scores.shape, 0) < length
    scores = jnp.where(visible, scores, MASKED)
    raised = jnp.exp(scores - jnp.max(scores, axis=0, keepdims=True))
    return raised * (1.0 / jnp.sum(raised, axis=0, keepdims=True))


def rows_at(head):
    return pl.ds(pl.multiple_of(head * HEAD_DIM, HEAD_DIM), HEAD_DIM)


def attend_kernel(
    heads, scalars_ref, lengths_ref, x_ref, coords_ref, table_ref, wqkv_ref, wpos_ref,
    send_ref, own_ref, proj_ref, pos_ref,
):
    step = pl.program_id(0)
    length = lengths_ref[scalars_ref[0] ^ (1 - step)]
    factor = 1.0 / math.sqrt(3.0 * HEAD_DIM)
    rows = x_ref[0]
    for part in range(3):
        proj_ref[part] = mm_nt(wqkv_ref[part], rows).astype(jnp.bfloat16)
    sides = [sinusoid(coords_ref[0, axis : axis + 1], table_ref) for axis in range(2)]
    position = jnp.concatenate(sides, axis=1).astype(jnp.bfloat16)
    pos_ref[...] = position
    for part in range(2):
        proj_ref[3 + part] = mm_nt(wpos_ref[part], position).astype(jnp.bfloat16)

    def one_head(head, _):
        at = rows_at(head)
        q, k, v, pq, pk = [proj_ref[part, at] for part in range(5)]
        weights = probs_t(q, k, pq, pk, length, factor).astype(jnp.bfloat16)
        mixed = mm(v, weights).astype(jnp.bfloat16)

        @pl.when(step == 0)
        def _():
            send_ref[at] = mixed.astype(jnp.float32)

        @pl.when(step == 1)
        def _():
            own_ref[at] = mixed

        return 0

    lax.fori_loop(0, heads, one_head, 0)


def attend(scalars, lengths, tokens, coords, table, w_qkv, w_pos):
    pages, length, width = tokens.shape
    columns = w_qkv.shape[1]
    whole = lambda shape: pl.BlockSpec(shape, lambda i, s, n: (0,) * len(shape))
    shapes = (
        jax.ShapeDtypeStruct((columns, length), jnp.float32),
        jax.ShapeDtypeStruct((columns, length), jnp.bfloat16),
        jax.ShapeDtypeStruct((5, columns, length), jnp.bfloat16),
        jax.ShapeDtypeStruct((length, width), jnp.bfloat16),
    )
    page = lambda i, s, n: (s[0] ^ (1 - i), 0, 0)
    return pl.pallas_call(
        partial(attend_kernel, columns // HEAD_DIM),
        out_shape=shapes,
        grid_spec=pltpu.PrefetchScalarGridSpec(
            num_scalar_prefetch=2,
            grid=(pages,),
            in_specs=[
                pl.BlockSpec((1, length, width), page),
                pl.BlockSpec((1,) + coords.shape[1:], page),
                whole(table.shape),
                whole(w_qkv.shape),
                whole(w_pos.shape),
            ],
            out_specs=[whole(shape.shape) for shape in shapes],
        ),
        compiler_params=pltpu.CompilerParams(vmem_limit_bytes=40 << 20),
        cost_estimate=pl.CostEstimate(
            flops=2 * pages * length * columns * (5 * width + 4 * length),
            transcendentals=pages * length * length * columns // HEAD_DIM,
            bytes_accessed=pages * length * (4 * width + 14 * columns),
        ),
        name="attend",
    )(scalars, lengths, tokens, coords, table, w_qkv, w_pos)


def norm_parts(values):
    center = values - jnp.mean(values, axis=-1, keepdims=True)
    spread = jnp.mean(center * center, axis=-1, keepdims=True)
    scale = lax.rsqrt(spread + 1e-05)
    return center * scale, scale


def norm_back(grad, gain, xhat, scale):
    up = grad * gain
    mean = jnp.mean(up, axis=-1, keepdims=True)
    along = jnp.mean(up * xhat, axis=-1, keepdims=True)
    return scale * (up - mean - xhat * along)


def column_sum(values):
    return jnp.sum(values.astype(jnp.float32), axis=0, keepdims=True)


def feed_kernel(
    scalars_ref, x_ref, part_ref, other_ref, b_out_ref, gain_ref, shift_ref, w_in_ref, w_in_far_ref, b_in_ref,
    w_back_ref, w_back_far_ref, xhat_ref, scale_ref, low_ref, hidden_ref, slope_ref, next_ref,
):
    first = x_ref[0].astype(jnp.float32) + (part_ref[...] + other_ref[...] + b_out_ref[...])
    xhat, scale = norm_parts(first)
    low = (xhat * gain_ref[...] + shift_ref[...]).astype(jnp.bfloat16)
    xhat_ref[...] = xhat
    scale_ref[...] = scale
    low_ref[...] = low
    units = w_in_ref.shape[1]
    total = None
    for side, (into, back) in enumerate(((w_in_ref, w_back_ref), (w_in_far_ref, w_back_far_ref))):
        at = slice(side * units, (side + 1) * units)
        pre = mm(low, into[...]) + b_in_ref[side : side + 1]
        cdf = 0.5 * (1.0 + lax.erf(pre * math.sqrt(0.5)))
        hidden = (pre * cdf).astype(jnp.bfloat16)
        hidden_ref[:, at] = hidden
        slope_ref[:, at] = cdf + pre * (jnp.exp(-0.5 * pre * pre) * (1.0 / math.sqrt(2.0 * math.pi)))
        product = mm(hidden, back[...])
        total = product if total is None else total + product
    next_ref[...] = total


def feed_back_kernel(
    scalars_ref, cot_ref, part_ref, other_ref, xhat_ref, slope_ref, gain_one_ref, shift_one_ref, b_back_ref,
    gain_ref, shift_ref, w_in_ref, w_in_far_ref, w_back_ref, w_back_far_ref,
    next_ref, second_ref, feed_ref, pre_ref, out_ref, sums_ref, sums_in_ref,
):
    normed = xhat_ref[...] * gain_one_ref[...] + shift_one_ref[...]
    second = normed + (part_ref[...] + other_ref[...] + b_back_ref[...])
    xhat, scale = norm_parts(second)
    out_ref[...] = xhat * gain_ref[...] + shift_ref[...]
    grad = cot_ref[0].astype(jnp.float32)
    d_second = norm_back(grad, gain_ref[...], xhat, scale)
    second_ref[...] = d_second
    d_feed = d_second.astype(jnp.bfloat16)
    feed_ref[...] = d_feed
    sums_ref[0:1] = column_sum(d_feed)
    sums_ref[1:2] = column_sum(grad * xhat)
    sums_ref[2:3] = column_sum(grad)
    units = w_in_ref.shape[1]
    total = None
    for side, (into, back) in enumerate(((w_in_ref, w_back_ref), (w_in_far_ref, w_back_far_ref))):
        at = slice(side * units, (side + 1) * units)
        d_pre = (mm_nt(d_feed, back[...]) * slope_ref[:, at]).astype(jnp.bfloat16)
        pre_ref[:, at] = d_pre
        sums_in_ref[side : side + 1] = column_sum(d_pre)
        product = mm_nt(d_pre, into[...])
        total = product if total is None else total + product
    next_ref[...] = total


def without(kernel, first, count):
    def call(*refs):
        return kernel(*refs[:first], *refs[first + count :])

    return call


def on_chunk(kernel, name, chunk, scalars, pages_array, rows, arrays, shapes, before=()):
    length, width = pages_array.shape[1:]

    def rows_of(array):
        if array.shape[0] == length and len(array.shape) == 2:
            return pl.BlockSpec((rows, array.shape[1]), lambda i, s: (chunk, 0))
        return pl.BlockSpec(memory_space=pltpu.VMEM)

    def whole(shape):
        if shape.shape[0] == length:
            return rows_of(shape)
        return pl.BlockSpec(shape.shape, lambda i, s: (0,) * len(shape.shape))

    inputs = 2 + len(arrays)
    return pl.pallas_call(
        without(kernel, inputs, len(before)),
        out_shape=shapes,
        grid_spec=pltpu.PrefetchScalarGridSpec(
            num_scalar_prefetch=1,
            grid=(1,),
            in_specs=[pl.BlockSpec((1, rows, width), lambda i, s: (s[0], chunk, 0))]
            + [rows_of(array) for array in arrays]
            + [pl.BlockSpec(memory_space=pl.ANY)] * len(before),
            out_specs=[whole(shape) for shape in shapes],
        ),
        input_output_aliases={inputs + index: index for index in range(len(before))},
        compiler_params=pltpu.CompilerParams(vmem_limit_bytes=48 << 20),
        cost_estimate=pl.CostEstimate(
            flops=16 * rows * width * width, transcendentals=2 * rows * width, bytes_accessed=40 * rows * width
        ),
        name=name,
    )(scalars, pages_array, *arrays, *before)


def feed_grads_kernel(count, low_ref, pre_ref, hidden_ref, feed_ref, out_ref):
    rows = out_ref.shape[2]

    def put(left, right):
        product = mm_tn(left[...], right[...])
        for block in range(count):
            out_ref[block, 0] = product[block * rows : (block + 1) * rows]

    @pl.when(pl.program_id(0) % 2 == 0)
    def _():
        put(low_ref, pre_ref)

    @pl.when(pl.program_id(0) % 2 == 1)
    def _():
        put(hidden_ref, feed_ref)


def feed_grads(count, low, d_pre, hidden, d_feed):
    length, width = low.shape
    units = hidden.shape[1] // 2
    return pl.pallas_call(
        partial(feed_grads_kernel, count),
        out_shape=pltpu.HBM((count, 4, width // count, units), jnp.float32),
        grid_spec=pl.GridSpec(
            grid=(4,),
            in_specs=[
                pl.BlockSpec((length, width), lambda i: (0, 0)),
                pl.BlockSpec((length, units), lambda i: (0, i // 2)),
                pl.BlockSpec((length, units), lambda i: (0, i // 2)),
                pl.BlockSpec((length, width), lambda i: (0, 0)),
            ],
            out_specs=pl.BlockSpec((count, 1, width // count, units), lambda i: (0, i, 0, 0)),
        ),
        compiler_params=pltpu.CompilerParams(vmem_limit_bytes=40 << 20),
        cost_estimate=pl.CostEstimate(
            flops=8 * length * width * units, transcendentals=0, bytes_accessed=16 * width * units
        ),
        name="feed_grads",
    )(low, d_pre, hidden, d_feed)


def weight_grads(count, group, x_ref, pos_ref, d_ref, db_ref, mixed_ref, far_ref, vec_ref, keep_ref, send_ref):
    columns = mixed_ref.shape[0]
    rows = columns // count
    odd = group & 1
    extra = vec_ref.shape[1]
    side_rows = 6 * rows + extra
    mixed = jnp.concatenate([mixed_ref[...], far_ref[...]], axis=0)
    rights = [x_ref] * 3 + [pos_ref] * 2 + [db_ref]

    def put(block, at, value):
        place = (block ^ group) >> 1

        @pl.when(odd == (block & 1))
        def _():
            keep_ref[place, at] = value

        @pl.when(odd != (block & 1))
        def _():
            send_ref[place, at] = value

    for part, right in enumerate(rights):
        product = mm(d_ref[part] if part < 5 else mixed, right[...])
        for block in range(count):
            for side in range(2):
                start = side * columns + block * rows
                at = side * side_rows + part * rows
                put(block, slice(at, at + rows), product[start : start + rows])
    for block in range(count):
        for side in range(2):
            at = slice(side * side_rows + 6 * rows, (side + 1) * side_rows)
            put(block, at, vec_ref[side] if block == 0 else jnp.zeros(vec_ref.shape[1:], jnp.float32))


def attend_back_kernel(
    heads, count, scalars_ref, lengths_ref, part_ref, other_ref, second_ref, xhat_ref, scale_ref, gain_ref, w_out_ref, w_out_far_ref, own_ref, wqkv_ref, blocks_ref, x_ref, pos_ref, mixed_ref, mixed_far_ref, more_ref,
    send_ref, base_ref, keep_ref, give_ref, d_ref, branch_ref, dm_ref, first_ref, proj_ref, wfar_ref, vec_ref,
):
    page, low = scalars_ref[0], scalars_ref[1]
    length = lengths_ref[page]
    factor = 1.0 / math.sqrt(3.0 * HEAD_DIM)
    columns = heads * HEAD_DIM
    half = part_ref.shape[0] // 2
    block_rows = blocks_ref.shape[3]
    for part in range(5):
        for block in range(count):
            at = slice(block * block_rows, (block + 1) * block_rows)
            wfar_ref[part, at] = blocks_ref[0, block, part]
        weight = wfar_ref[part].astype(jnp.bfloat16)
        left = x_ref if part < 3 else pos_ref
        proj_ref[part, columns:] = mm_nt(weight, left[...]).astype(jnp.bfloat16)
        proj_ref[part, :columns] = own_ref[part]
    sums = None
    for index in range(2):
        at = slice(index * half, (index + 1) * half)
        xhat = xhat_ref[at]
        d_normed = second_ref[at] + (part_ref[at] + other_ref[at])
        d_first = norm_back(d_normed, gain_ref[...], xhat, scale_ref[at])
        first_ref[at] = d_first
        d_branch = d_first.astype(jnp.bfloat16)
        branch_ref[at] = d_branch
        some = (column_sum(d_branch), column_sum(d_normed * xhat), column_sum(d_normed))
        sums = some if sums is None else tuple(x + y for x, y in zip(sums, some))
        dm_ref[:columns, at] = mm_nt(w_out_ref[...], d_branch).astype(jnp.bfloat16)
        dm_ref[columns:, at] = mm_nt(w_out_far_ref[...], d_branch).astype(jnp.bfloat16)
    for side in range(2):
        for index, value in enumerate(sums):
            vec_ref[side, index : index + 1] = value
        vec_ref[side, len(sums) :] = more_ref[side]

    def one_head(head, _):
        at = rows_at(head)
        q, k, v, pq, pk = [proj_ref[part, at] for part in range(5)]
        dm = dm_ref[at]
        probs = probs_t(q, k, pq, pk, length, factor)
        weights = probs.astype(jnp.bfloat16)
        d_values = mm(weights, dm.T)
        d_probs = mm_tn(v, dm)
        inner = jnp.sum(d_probs * probs, axis=0, keepdims=True)
        d_scores = (probs * (d_probs - inner)).astype(jnp.bfloat16)
        by_queries = mm(d_scores, jnp.concatenate([q, pq], axis=0).T).T
        by_query, by_pos_query = by_queries[:HEAD_DIM], by_queries[HEAD_DIM:]
        by_keys = mm(jnp.concatenate([k, pk], axis=0), d_scores)
        by_key, by_pos_key = by_keys[:HEAD_DIM], by_keys[HEAD_DIM:]
        grads = (
            (by_key + by_pos_key) * factor,
            (by_query + by_pos_query) * factor,
            d_values.T,
            by_key * factor,
            by_query * factor,
        )
        for part, value in enumerate(grads):
            d_ref[part, at] = value.astype(jnp.bfloat16)
        return 0

    lax.fori_loop(0, 2 * heads, one_head, 0)
    for part in range(3):
        for side in range(2):
            at = slice(side * columns, (side + 1) * columns)
            weight = wqkv_ref[part] if side == 0 else wfar_ref[part].astype(jnp.bfloat16)
            first_ref_part = mm_tn(d_ref[part, at], weight)
            if part == side == 0:
                total = first_ref_part
            else:
                total = total + first_ref_part
    upper, lower = total[:half], total[half:]
    send_ref[...] = jnp.where(low == 0, lower, upper)
    base_ref[...] = jnp.where(low == 0, upper + first_ref[:half], lower + first_ref[half:])
    weight_grads(
        count, scalars_ref[2], x_ref, pos_ref, d_ref, branch_ref, mixed_ref, mixed_far_ref, vec_ref, keep_ref, give_ref
    )


def attend_back(count, scalars, lengths, arrays):
    proj = arrays[8]
    parts, columns, length = proj.shape
    half, width = length // 2, arrays[0].shape[1]
    heads = columns // HEAD_DIM
    whole = lambda shape: pl.BlockSpec(shape, lambda i, s, n: (0,) * len(shape))
    shapes = (
        jax.ShapeDtypeStruct((half, width), jnp.float32),
        jax.ShapeDtypeStruct((half, width), jnp.float32),
    ) + 2 * (jax.ShapeDtypeStruct((count // 2, 2 * (6 * (columns // count) + 8), width), jnp.float32),)
    return pl.pallas_call(
        partial(attend_back_kernel, heads, count),
        out_shape=shapes,
        grid_spec=pltpu.PrefetchScalarGridSpec(
            num_scalar_prefetch=2,
            grid=(1,),
            in_specs=[
                whole(array.shape)
                if len(array.shape) < 5
                else pl.BlockSpec((1,) + array.shape[1:], lambda i, s, n: (0, 0, 0, 0, 0))
                for array in arrays
            ],
            out_specs=[whole(shape.shape) for shape in shapes],
            scratch_shapes=[
                pltpu.VMEM((parts, 2 * columns, length), jnp.bfloat16),
                pltpu.VMEM((length, width), jnp.bfloat16),
                pltpu.VMEM((2 * columns, length), jnp.bfloat16),
                pltpu.VMEM((length, width), jnp.float32),
                pltpu.VMEM((parts, 2 * columns, length), jnp.bfloat16),
                pltpu.VMEM((parts, columns, width), jnp.float32),
                pltpu.VMEM((2, 8, width), jnp.float32),
            ],
        ),
        compiler_params=pltpu.CompilerParams(vmem_limit_bytes=58 << 20),
        cost_estimate=pl.CostEstimate(
            flops=2 * 2 * heads * length * length * HEAD_DIM * 9 + 20 * length * width * columns,
            transcendentals=2 * heads * length * length,
            bytes_accessed=40 * length * width,
        ),
        name="attend_back",
    )(scalars, lengths, *arrays)


def spread_kernel(count, scalars_ref, *refs):
    out_ref = refs[-1]
    pieces = [refs[0].at[0], refs[0].at[1]] if len(refs[0].shape) == 3 else refs[:count]
    for step, ref in enumerate(pieces):

        @pl.when(pl.program_id(0) == step)
        def _():
            rows = out_ref.shape[1]
            at = pl.ds(pl.multiple_of(pl.program_id(1) * rows, rows), rows)
            out_ref[0] = ref[at].astype(out_ref.dtype)


def spread(scalars, pieces, kind, start, onto=()):
    half, width = pieces[0].shape[-2:]
    count = max(len(pieces), 2)
    return pl.pallas_call(
        partial(spread_kernel, count),
        out_shape=pltpu.HBM((2, 2 * half, width), kind),
        grid_spec=pltpu.PrefetchScalarGridSpec(
            num_scalar_prefetch=1,
            grid=(count, 2),
            in_specs=[pl.BlockSpec(memory_space=pltpu.VMEM)] * len(pieces)
            + [pl.BlockSpec(memory_space=pltpu.HBM)] * len(onto),
            out_specs=pl.BlockSpec(
                (1, half // 2, width),
                lambda i, j, s: (s[0] ^ ((start + i) % 2), 2 * (s[1] ^ ((start + i) // 2)) + j, 0),
            ),
        ),
        input_output_aliases={1 + len(pieces): 0} if onto else {},
        compiler_params=pltpu.CompilerParams(vmem_limit_bytes=16 << 20),
        cost_estimate=pl.CostEstimate(flops=0, transcendentals=0, bytes_accessed=32 * half * width),
        name="spread",
    )(scalars, *pieces, *onto)


def split_blocks_kernel(in_ref, first_ref, second_ref):
    count, both, _ = in_ref.shape
    rows = both // 2
    for block in range(count):
        at = slice(block * rows, (block + 1) * rows)
        first_ref[at] = in_ref[block, :rows]
        second_ref[at] = in_ref[block, rows:]


def split_blocks(blocks):
    count, both, width = blocks.shape
    lanes = width // 3 if width % 384 == 0 else width
    shape = pltpu.HBM((count * both // 2, width), blocks.dtype)
    out_spec = pl.BlockSpec((count * both // 2, lanes), lambda i: (0, i))
    return pl.pallas_call(
        split_blocks_kernel,
        out_shape=(shape, shape),
        grid_spec=pl.GridSpec(
            grid=(width // lanes,),
            in_specs=[pl.BlockSpec((count, both, lanes), lambda i: (0, 0, i))],
            out_specs=[out_spec, out_spec],
        ),
        compiler_params=pltpu.CompilerParams(vmem_limit_bytes=24 << 20),
        cost_estimate=pl.CostEstimate(flops=0, transcendentals=0, bytes_accessed=8 * blocks.size),
        name="split_blocks",
    )(blocks)


def place_grads_kernel(
    order, scalars_ref, low_a_ref, low_b_ref, high_a_ref, high_b_ref, qkv_ref, pos_ref, out_ref, vec_ref
):
    group = scalars_ref[0]
    count = 2 * low_a_ref.shape[0]
    rows = qkv_ref.shape[1] // count
    cut = low_a_ref.shape[1]

    def read(place, start, stop):
        upper = (place & 1) == 1
        index = place >> 1
        pieces = []
        if start < cut:
            at = slice(start, min(stop, cut))
            pieces.append(jnp.where(upper, high_a_ref[index, at], low_a_ref[index, at]))
        if stop > cut:
            at = slice(max(start, cut) - cut, stop - cut)
            turned_index = 0
            for bit in range(len(order)):
                turned_index = turned_index | (((index >> bit) & 1) << order[bit])
            pieces.append(jnp.where(upper, high_b_ref[turned_index, at], low_b_ref[turned_index, at]))
        return jnp.concatenate(pieces, axis=0) if len(pieces) > 1 else pieces[0]

    for block in range(count):
        place = block ^ group
        at = slice(block * rows, (block + 1) * rows)
        for part in range(6):
            value = read(place, part * rows, (part + 1) * rows)
            if part < 3:
                qkv_ref[part, at] = value
            elif part < 5:
                pos_ref[part - 3, at] = value
            else:
                out_ref[at] = value
        if block == 0:
            vec_ref[...] = read(place, 6 * rows, cut + low_b_ref.shape[1])


def place_grads(scalars, parts, columns, vec_rows):
    width = parts[0].shape[2]
    bits = parts[0].shape[0].bit_length() - 1
    whole = lambda shape: pl.BlockSpec(shape, lambda i: (0,) * len(shape))
    shapes = (
        jax.ShapeDtypeStruct((3, columns, width), jnp.float32),
        jax.ShapeDtypeStruct((2, columns, width), jnp.float32),
        jax.ShapeDtypeStruct((columns, width), jnp.float32),
        jax.ShapeDtypeStruct((vec_rows, width), jnp.float32),
    )
    return pl.pallas_call(
        partial(place_grads_kernel, tuple(range(bits))[::-1]),
        out_shape=shapes,
        grid_spec=pl.GridSpec(
            grid=(1,),
            in_specs=[pl.BlockSpec(memory_space=pltpu.SMEM)] + [whole(part.shape) for part in parts],
            out_specs=[whole(shape.shape) for shape in shapes],
        ),
        compiler_params=pltpu.CompilerParams(vmem_limit_bytes=40 << 20),
        cost_estimate=pl.CostEstimate(
            flops=0, transcendentals=0, bytes_accessed=32 * width * columns * 3
        ),
        name="place_grads",
    )(scalars, *parts)


def body(
    dp_size,
    mp_size,
    tokens,
    lengths,
    coords,
    w_qkv,
    w_pos,
    w_out,
    b_out,
    gain_one,
    shift_one,
    w_in,
    b_in,
    w_back,
    b_back,
    gain_two,
    shift_two,
    cotangent,
):
    pages, length, width = tokens.shape
    columns = w_qkv.shape[2]
    units = w_in.shape[1]
    here = lax.axis_index(MP)
    low = here & 1
    page = here >> 1
    group = lax.axis_index("dp")
    f32, bf16 = jnp.float32, jnp.bfloat16
    half = length // 2
    one = jnp.where(lengths[0] > 0, 1.0, 0.0).astype(f32)

    def arrived(value):
        return value * one

    def swap(value, bit):
        pairs = [(i, i ^ bit) for i in range(mp_size)]
        return lax.ppermute(value, MP, pairs)

    def group_swap(value, bit):
        pairs = [(i, i ^ bit) for i in range(dp_size)]
        return lax.ppermute(value, "dp", pairs)

    def my_rows(value):
        rows = value.shape[0] // dp_size
        return lax.dynamic_slice_in_dim(value, group * rows, rows, 0)

    def gather(value):
        return lax.all_gather(value, "dp", axis=0, tiled=True)

    def take(value, index):
        return lax.dynamic_index_in_dim(value, index, 0, keepdims=False)

    def after(value, *others):
        return lax.optimization_barrier((value,) + others)[0]

    def row(value):
        return value.reshape(1, -1)

    chunk_rows = lambda value: [value[:half], value[half:]]

    turn = lambda value: jnp.swapaxes(value, 1, 2)
    w_qkv, w_pos = turn(w_qkv), turn(w_pos)
    out_rows = swap(my_rows(w_out).astype(f32), FAR)
    out_rows = jnp.pad(out_rows, ((0, max(0, 48 - out_rows.shape[0])), (0, 0)))
    unit_rows = jnp.concatenate([my_rows(w_in), my_rows(w_back)], axis=0).astype(f32)
    tail = jnp.concatenate([row(b_in), jnp.zeros((7, units), f32)], axis=0)
    far_rows = swap(jnp.concatenate([unit_rows, tail], axis=0), FAR)
    count = columns // dp_size

    table = jnp.asarray(angle_tables(width))
    scalars = jnp.stack([page, low])
    mixed_send, mixed, proj, pos_rows = attend(scalars, lengths, tokens, coords, table, w_qkv, w_pos)
    w_out_far = gather(out_rows).reshape(dp_size, -1, width)[:, : columns // dp_size]
    w_out_far = arrived(w_out_far.reshape(columns, width)).astype(bf16)
    mixed_far = swap(mixed_send, FAR)
    far_rows = after(far_rows, mixed_send)
    count = unit_rows.shape[0]
    b_in_two = jnp.stack([b_in, far_rows[count]])
    blocks = arrived(gather(far_rows)).reshape(dp_size, count + 8, -1)
    in_rows = width // dp_size
    w_in_far = blocks[:, :in_rows].reshape(width, units).astype(bf16)
    w_back_far = blocks[:, in_rows:count].reshape(units, width).astype(bf16)

    mixed_far = arrived(mixed_far).astype(bf16)
    part = mm_tn(jnp.concatenate([mixed, mixed_far], axis=0), jnp.concatenate([w_out, w_out_far], axis=0))
    other = swap(part, NEAR)
    head_rows = jnp.concatenate([w_qkv, w_pos], axis=0)
    count = columns // dp_size
    head_rows = lax.dynamic_slice_in_dim(head_rows, group * count, count, 1).astype(f32)
    blocks = gather(swap(after(head_rows, part), FAR).reshape(-1, width))
    blocks = blocks.reshape(1, dp_size, 5, count, width)

    rows_f32 = jax.ShapeDtypeStruct((length, width), f32)
    rows_low = jax.ShapeDtypeStruct((length, width), bf16)
    units_f32 = jax.ShapeDtypeStruct((length, 2 * units), f32)
    units_low = jax.ShapeDtypeStruct((length, 2 * units), bf16)
    chunk_f32 = jax.ShapeDtypeStruct((half, width), f32)
    scale_of = jax.ShapeDtypeStruct((length, 1), f32)
    shapes = (rows_f32, scale_of, rows_low, units_low, units_f32, chunk_f32)
    arrays = [part, other, row(b_out), row(gain_one), row(shift_one)]
    arrays += [w_in, w_in_far, b_in_two, w_back, w_back_far]
    part, other = [], []
    fed = ()
    for index in range(2):
        *fed, product = on_chunk(
            feed_kernel, "feed", index, scalars, tokens, half, arrays, shapes, tuple(fed)
        )
        part.append(product)
        other.append(swap(product, NEAR))
    xhat_one, scale_one, normed_low, hidden, slope = fed
    shapes = (rows_f32, rows_f32, rows_low, units_low, rows_f32)
    shapes += (jax.ShapeDtypeStruct((3, width), f32), jax.ShapeDtypeStruct((2, units), f32))
    back, sums_two, sums_in = (), [], []
    for index in range(2):
        arrays = [part[index], other[index], xhat_one, slope, row(gain_one), row(shift_one)]
        arrays += [row(b_back), row(gain_two), row(shift_two), w_in, w_in_far, w_back, w_back_far]
        *back, some, some_in = on_chunk(
            feed_back_kernel, "feed_back", index, scalars, cotangent, half, arrays, shapes, tuple(back)
        )
        sums_two.append(some)
        sums_in.append(some_in)
    part, d_second, d_feed, d_pre, output = back
    other = swap(part, NEAR)

    ffn = feed_grads(dp_size, normed_low, d_pre, hidden, d_feed)
    ffn = lax.psum_scatter(ffn.reshape(-1, units), "dp", scatter_dimension=0, tiled=True)

    rows = take(tokens, page)
    arrays = [part, other, d_second, xhat_one, scale_one]
    arrays += [row(gain_one), w_out, w_out_far]
    vectors = sums_two[0] + sums_two[1]
    d_b_in = sums_in[0] + sums_in[1]
    spare = jnp.zeros((1, width), f32)
    vectors = jnp.stack(
        [jnp.concatenate([vectors, d_b_in[side : side + 1], spare], axis=0) for side in range(2)]
    )
    arrays += [proj, w_qkv, blocks, rows, pos_rows, mixed, mixed_far, vectors]
    send, base, keep, give = attend_back(dp_size, jnp.stack([page, low, group]), lengths, arrays)

    half_of = lambda value, index: lax.dynamic_slice_in_dim(value, index * half, half, 0)
    out_mine = half_of(output, low)
    out_far = swap(after(out_mine, other), FAR)

    bits = [1 << k for k in range(dp_size.bit_length() - 1)]
    give = after(give, out_far)
    near_sum = swap(send, NEAR)
    mine = base + near_sum

    group_scalar = jnp.reshape(group, (1,))
    out_turned = swap(out_far, NEAR)
    ffn_rows = ffn.shape[0] // 2
    crossed = swap(jnp.concatenate([mine, ffn[ffn_rows:]], axis=0), FAR)
    ffn = ffn[:ffn_rows] + crossed[half:]
    far_mine = crossed[:half]
    total = keep + group_swap(give, bits[0])
    more = bits[1:]

    def after_all(*values):
        return lax.optimization_barrier(values)

    cut = total.shape[1] // 2
    upper, lower = total[:, :cut], total[:, cut:]
    for step in range(len(more)):
        upper = upper.reshape((-1, 2) + upper.shape[1:])
        lower = lower.reshape((2, -1) + lower.shape[1:])
        give_upper, give_lower = after_all(upper[:, 1], lower[1], *([out_turned] if step else []))[:2]
        got_upper = group_swap(give_upper, more[step])
        got_lower = group_swap(give_lower, more[-1 - step])
        upper = upper[:, 0] + got_upper
        lower = lower[0] + got_lower
    upper, lower = upper[0], lower[0]
    far_sum = swap(after(lower, crossed), FAR)
    ffn = after(ffn, got_upper, got_lower)

    rest = swap(after(jnp.stack([mine, far_mine]), far_sum), NEAR)
    grad_half = spread(scalars, (mine, far_mine), f32, 0)
    grad_tokens = spread(scalars, (rest,), f32, 2, (grad_half,))
    out_rest = half_of(output, 1 - low)
    layer_out = spread(scalars, (out_mine, out_far, out_rest, after(out_turned, far_sum)), bf16, 0)
    total = upper + far_sum
    cut = total.shape[0] // 16 * 8
    upper, lower = total[None, :cut], total[None, cut:]
    for step in range(len(more)):
        if step:
            upper, lower = after_all(upper, lower, layer_out, grad_half)[:2]
        got_upper = group_swap(upper, more[step])
        got_lower = group_swap(lower, more[-1 - step])
        upper = jnp.concatenate([upper, got_upper], axis=0)
        lower = jnp.concatenate([lower, got_lower], axis=0)
    grad_w_in, grad_w_back = split_blocks(gather(ffn).reshape(dp_size, ffn_rows, units))
    upper, lower = after_all(upper, lower, rest, grad_w_in)[:2]
    parts = [upper, lower, group_swap(upper, bits[0]), group_swap(lower, bits[0])]
    grad_w_qkv, grad_w_pos, grad_w_out, vectors = place_grads(group_scalar, parts, columns, 8)
    grad_w_qkv, grad_w_pos = turn(grad_w_qkv), turn(grad_w_pos)
    grad_b_out, grad_gain_one, grad_shift_one = vectors[0], vectors[1], vectors[2]
    grad_b_back, grad_gain_two, grad_shift_two = vectors[3], vectors[4], vectors[5]
    grad_b_in = vectors[6]

    return (
        layer_out,
        grad_tokens,
        grad_w_qkv,
        grad_w_pos,
        grad_w_out,
        grad_b_out,
        grad_gain_one,
        grad_shift_one,
        grad_w_in,
        grad_b_in,
        grad_w_back,
        grad_b_back,
        grad_gain_two,
        grad_shift_two,
    )


def solution(mesh):
    mp_size = mesh.shape["mp"]
    dp_size = mesh.devices.size // mp_size
    split = jax.sharding.Mesh(mesh.devices.reshape(dp_size, mp_size // 2, 2), ("dp",) + MP)
    placed = (
        P("dp", None, None),
        P("dp"),
        P("dp", None, None),
        P(None, None, MP),
        P(None, None, MP),
        P(MP, None),
        P(),
        P(),
        P(),
        P(None, MP),
        P(MP),
        P(MP, None),
        P(),
        P(),
        P(),
        P("dp", None, None),
    )
    return jax.shard_map(
        partial(body, dp_size, mp_size),
        mesh=split,
        in_specs=placed,
        out_specs=(
            P("dp", None, None),
            P("dp", None, None),
            P(None, None, MP),
            P(None, None, MP),
            P(MP, None),
            P(),
            P(),
            P(),
            P(None, MP),
            P(MP),
            P(MP, None),
            P(),
            P(),
            P(),
        ),
        check_vma=False,
    )
```
